128 devices in a mesh: token: 8 (over y, core), tensor: 16 (over z, x).
Axes of the slice: x: 4, y: 4, z: 4, core: 2. Of those that a mesh axis runs over, the one named last changes fastest.
Arguments:
- tokens: bfloat16 [8192, 4096], P(('token', 'tensor')), may hold values from -6 to 6
- doc_lengths: int32 [4], replicated, may hold values from 1 to 4096, 8192 in all
- attn_gain: float32 [4096], replicated, may hold values from 0.1 to 1.9
- mlp_gain: float32 [4096], replicated, may hold values from 0.1 to 1.9
- w_query: bfloat16 [4096, 4096], P(None, 'tensor'), may hold values from -0.067528728 to 0.067528728
- w_keyval: bfloat16 [4096, 2048], P(None, 'tensor'), may hold values from -0.067528728 to 0.067528728
- w_out: bfloat16 [4096, 4096], P('tensor'), may hold values from -0.09375 to 0.09375
- w_gate: bfloat16 [4096, 7168], P(None, 'tensor'), may hold values from -0.09375 to 0.09375
- w_up: bfloat16 [4096, 7168], P(None, 'tensor'), may hold values from -0.09375 to 0.09375
- w_down: bfloat16 [7168, 4096], P('tensor'), may hold values from -0.0625 to 0.0625
Outputs:
- layer_out: bfloat16 [8192, 4096], P(('token', 'tensor'))
The draws below stay inside these ranges and needn't reach their ends.
Inputs may be any that keep to these rules, and one draw needn't show every extreme that they name: `doc_lengths`: the lengths sum to 8192; exactly one document has length 4096, the largest allowed.
All inputs are finite; a program needn't handle non-finite values.
Results may differ from the reference program's by a relative error of at most 0.017.
Values may be sent and summed in bfloat16 or wider, within the bound.
A program may use at most 128 MiB of HBM per device.

```python
import math
import jax
import jax.numpy as jnp
import numpy as np
from jax import lax

D = 4096
HEADS = 32
KV_HEADS = 8
HEAD_DIM = 128
FF_WIN = 7168
KBLK = 512
DOCS = 4
TOKENS = 8192
QBLK = 256
N_TENSOR = 16


def shared_direction(key):
    picks = jax.random.bernoulli(jax.random.fold_in(key, 7001), 0.5, (D,))
    return jnp.where(picks, 1.0, -1.0).astype(jnp.float32)


def drawn_columns():
    dims = jnp.arange(HEAD_DIM, dtype=jnp.int32)
    half = HEAD_DIM // 2
    return (dims % half >= half - HEAD_DIM // 8).astype(jnp.float32)


def spike_amplitude():
    strength = 180.0
    return 2.0 * math.sqrt(4.0 * strength / math.sqrt(HEAD_DIM)) / D


def base_weight(key, shape):
    spread = D ** (-0.5)
    return spread * jax.random.truncated_normal(key, -4.0, 4.0, shape, jnp.float32)


def draw_tokens(key, part):
    noise = jax.random.truncated_normal(jax.random.fold_in(key, 31), -3.0, 3.0, (TOKENS, D), jnp.float32)
    chance = max(1.0 / 32.0, 8.0 / TOKENS)
    marked = jax.random.bernoulli(jax.random.fold_in(key, 32), chance, (TOKENS,)).astype(jnp.float32)
    rows_out = noise + marked[:, None] * shared_direction(key)[None, :]
    return jnp.clip(rows_out, -6.0, 6.0).astype(jnp.bfloat16)


def draw_w_query(key, part):
    base = base_weight(jax.random.fold_in(key, 11), (D, HEADS * HEAD_DIM))
    strength = jax.random.uniform(jax.random.fold_in(key, 12), (HEADS,), jnp.float32, 0.5, 1.0)
    column = (strength[:, None] * drawn_columns()[None, :]).reshape(HEADS * HEAD_DIM)
    extra = spike_amplitude() * shared_direction(key)[:, None] * column[None, :]
    return (base + extra).astype(jnp.bfloat16)


def draw_w_keyval(key, part):
    base = base_weight(jax.random.fold_in(key, 21), (D, 2 * KV_HEADS * HEAD_DIM))
    strength = jax.random.uniform(jax.random.fold_in(key, 22), (KV_HEADS,), jnp.float32, 0.5, 1.0)
    kind = jnp.array([1.0, 0.0], jnp.float32)
    column = (strength[:, None, None] * kind[None, :, None] * drawn_columns()[None, None, :]).reshape(2 * KV_HEADS * HEAD_DIM)
    extra = spike_amplitude() * shared_direction(key)[:, None] * column[None, :]
    return (base + extra).astype(jnp.bfloat16)


def levels(own_key, shape, cuts, least, high):
    def one(axis_at, shards_of):
        heights = jax.random.uniform(jax.random.fold_in(jax.random.fold_in(own_key, 6), axis_at), (shards_of,), jnp.float32, least / len(cuts), high / len(cuts))
        return jnp.repeat(jnp.exp(heights), shape[axis_at] // shards_of).reshape((-1,) + (1,) * (len(shape) - axis_at - 1))

    loudness = one(*cuts[0])
    for cut in cuts[1:]:
        loudness = loudness * one(*cut)
    return loudness


def length_profile(number_of, total, most, lean):
    loads = [(1 << 20) // math.isqrt(rank ** lean) + 1 for rank in range(2, number_of + 1)]
    spare, given = total - most - (number_of - 1), [1] * (number_of - 1)
    while spare > 0:
        free = [i for i in range(number_of - 1) if given[i] < most]
        mass, remaining = sum([loads[i] for i in free]), spare
        for i in free:
            addition = min(most - given[i], max(1, remaining * loads[i] // mass), spare)
            given[i] = given[i] + addition
            spare = spare - addition
    return np.array([most] + given)


def uneven_parts(stream_key, count, total, bound, slope):
    if count == 2:
        one = jax.random.randint(stream_key, (), max(1, total - bound), min(bound, total - 1) + 1)
        return jnp.stack([one, total - one])
    sizes = jnp.asarray(length_profile(count, total, bound, slope), jnp.int32)
    pairs = (count - 1) // 2
    giver, receiver = sizes[1:1 + 2 * pairs:2], sizes[2:2 + 2 * pairs:2]
    margin = jnp.minimum(giver - 1, bound - receiver)
    moved = jax.random.randint(jax.random.fold_in(stream_key, 1), (pairs,), 0, 1 << 20) % (margin + 1)
    sizes = sizes.at[1:1 + 2 * pairs:2].set(giver - moved).at[2:2 + 2 * pairs:2].set(receiver + moved)
    return sizes[jax.random.permutation(jax.random.fold_in(stream_key, 2), count)]


def gaussian(stream_key, shape, scale, limit, shards=(), held_as=jnp.bfloat16):
    values = jax.random.normal(stream_key, shape, jnp.float32) * scale
    if len(shards) > 0:
        values = levels(stream_key, shape, shards, -0.22, 0.18) * values
    return jnp.clip(values, min=-limit, max=limit).astype(held_as)


def setup_inputs(seed: int = 0) -> dict:
    key_of = jax.random.split(jax.random.key(seed), 11)
    tokens = draw_tokens(jax.random.fold_in(key_of[10], 71), 0)
    doc_lengths = uneven_parts(key_of[1], DOCS, TOKENS, TOKENS // 2, 2).astype(jnp.int32)
    attn_gain = jnp.clip(1.0 + 0.18 * jax.random.normal(key_of[2], (D,), jnp.float32), 0.1, 1.9)
    mlp_gain = jnp.clip(1.0 + 0.18 * jax.random.normal(key_of[3], (D,), jnp.float32), 0.1, 1.9)
    w_query = draw_w_query(jax.random.fold_in(key_of[10], 71), 0)
    w_keyval = draw_w_keyval(jax.random.fold_in(key_of[10], 71), 0)
    w_out = gaussian(key_of[6], (HEADS * HEAD_DIM, D), (HEADS * HEAD_DIM) ** -0.5, 0.09375, ((0, 16),))
    w_gate = gaussian(key_of[7], (D, FF_WIN), D ** -0.5, 0.09375, ((1, 16),))
    w_up = gaussian(key_of[8], (D, FF_WIN), D ** -0.5, 0.09375, ((1, 16),))
    w_down = gaussian(key_of[9], (FF_WIN, D), FF_WIN ** -0.5, 0.0625, ((0, 16),))
    return {"tokens": tokens, "doc_lengths": doc_lengths, "attn_gain": attn_gain, "mlp_gain": mlp_gain, "w_query": w_query, "w_keyval": w_keyval, "w_out": w_out, "w_gate": w_gate, "w_up": w_up, "w_down": w_down}


EPSILON = 1e-05
ROPE_BASE = 500000.0
NEGATIVE = -1e+30

def rms_scale(row_data, gain):
    floats = row_data.astype(jnp.float32)
    mean_square = lax.optimization_barrier(jnp.mean(floats * floats, axis=-1, keepdims=True))
    return (floats * lax.rsqrt(mean_square + EPSILON) * gain.astype(jnp.float32)).astype(jnp.bfloat16)

def doc_layout(doc_lengths, total):
    ends = jnp.cumsum(doc_lengths).astype(jnp.int32)
    starts = (ends - doc_lengths).astype(jnp.int32)
    counter = jnp.arange(total, dtype=jnp.int32)
    segment = lax.optimization_barrier(jnp.sum((counter[:, None] >= ends[None, :-1]).astype(jnp.int32), axis=1)).astype(jnp.int32)
    labels = jnp.arange(doc_lengths.shape[0], dtype=jnp.int32)
    first = lax.optimization_barrier(jnp.sum(jnp.where(segment[:, None] == labels[None, :], starts[None, :], 0), axis=1)).astype(jnp.int32)
    return (segment, (counter - first).astype(jnp.int32), starts)

def rotate(floats, position):
    half = floats.shape[-1] // 2
    freq = jnp.exp(-math.log(ROPE_BASE) * jnp.arange(half, dtype=jnp.float32) * (2.0 / floats.shape[-1]))
    angle = position.astype(jnp.float32)[:, None] * freq[None, :]
    cosine = jnp.cos(angle)[:, None, :]
    sine = jnp.sin(angle)[:, None, :]
    lower = floats[..., :half]
    upper = floats[..., half:]
    return jnp.concatenate([lower * cosine - upper * sine, upper * cosine + lower * sine], axis=-1)

def attend(block_query, block_number, key_rows, value_rows, segment, starts, qblk, kblk):
    heads = block_query.shape[1]
    width = block_query.shape[2]
    count = qblk * heads
    flat_query = block_query.reshape(count, width)
    first_row = (block_number * qblk).astype(jnp.int32)
    query_pos = first_row + jnp.arange(qblk, dtype=jnp.int32)
    query_seg = lax.dynamic_slice_in_dim(segment, first_row, qblk)
    pos_rows = jnp.repeat(query_pos, heads)
    seg_rows = jnp.repeat(query_seg, heads)
    labels = jnp.arange(starts.shape[0], dtype=jnp.int32)
    doc_first = jnp.sum(jnp.where(labels == query_seg[0], starts, 0)).astype(jnp.int32)
    lowest = (doc_first // kblk).astype(jnp.int32)
    highest = ((first_row + qblk - 1) // kblk + 1).astype(jnp.int32)
    factor = 1.0 / math.sqrt(width)

    def advance(key_block, carry):
        peak, totals, summed = carry
        key_start = (key_block * kblk).astype(jnp.int32)
        key_tile = lax.dynamic_slice_in_dim(key_rows, key_start, kblk)
        value_tile = lax.dynamic_slice_in_dim(value_rows, key_start, kblk)
        key_seg = lax.dynamic_slice_in_dim(segment, key_start, kblk)
        key_pos = key_start + jnp.arange(kblk, dtype=jnp.int32)
        scores = lax.dot_general(flat_query, key_tile, (((1,), (1,)), ((), ())), preferred_element_type=jnp.float32) * factor
        allowed = (key_seg[None, :] == seg_rows[:, None]) & (key_pos[None, :] <= pos_rows[:, None])
        scores = jnp.where(allowed, scores, NEGATIVE)
        new_peak = jnp.maximum(peak, lax.optimization_barrier(jnp.max(scores, axis=1)))
        decay = jnp.exp(peak - new_peak)
        weights = jnp.exp(scores - new_peak[:, None])
        totals = totals * decay + lax.optimization_barrier(jnp.sum(weights, axis=1))
        summed = summed * decay[:, None] + jnp.dot(weights.astype(jnp.bfloat16), value_tile, preferred_element_type=jnp.float32)
        return (new_peak, totals, summed)
    start_carry = (jnp.full((count,), NEGATIVE, jnp.float32), jnp.zeros((count,), jnp.float32), jnp.zeros((count, width), jnp.float32))
    peak, totals, summed = lax.fori_loop(lowest, highest, advance, start_carry)
    return (summed / totals[:, None]).astype(jnp.bfloat16).reshape(qblk, heads, width)

def grouped_product(left, right, groups):
    inner = left.shape[1] // groups

    def add_group(accum, group_index):
        left_part = lax.dynamic_slice_in_dim(left, group_index * inner, inner, axis=1)
        right_part = lax.dynamic_slice_in_dim(right, group_index * inner, inner, axis=0)
        rounded = lax.optimization_barrier(jnp.dot(left_part, right_part, preferred_element_type=jnp.float32).astype(jnp.bfloat16))
        return (accum + rounded.astype(jnp.float32), None)
    start_sum = jnp.zeros((left.shape[0], right.shape[1]), jnp.float32)
    result, unused = lax.scan(add_group, start_sum, jnp.arange(groups, dtype=jnp.int32))
    return result

def reference(tokens, doc_lengths, attn_gain, mlp_gain, w_query, w_keyval, w_out, w_gate, w_up, w_down):
    total = tokens.shape[0]
    segment, position, starts = doc_layout(doc_lengths, total)
    normed = rms_scale(tokens, attn_gain)
    queries = rotate(jnp.dot(normed, w_query, preferred_element_type=jnp.float32).reshape(total, HEADS, HEAD_DIM), position).astype(jnp.bfloat16)
    keyval = jnp.dot(normed, w_keyval, preferred_element_type=jnp.float32).reshape(total, KV_HEADS, 2, HEAD_DIM)
    key_rows = rotate(keyval[:, :, 0], position).astype(jnp.bfloat16)
    value_rows = keyval[:, :, 1].astype(jnp.bfloat16)
    group = HEADS // KV_HEADS
    blocks = total // QBLK
    grouped = queries.reshape(total, KV_HEADS, group, HEAD_DIM).transpose(1, 0, 2, 3)

    def per_head(inputs):
        head_query, head_keys, head_values = inputs

        def per_block(block_number):
            piece_query = lax.dynamic_slice_in_dim(head_query, block_number * QBLK, QBLK)
            return attend(piece_query, block_number, head_keys, head_values, segment, starts, QBLK, KBLK)
        return lax.map(per_block, jnp.arange(blocks, dtype=jnp.int32))
    heads_out = lax.map(per_head, (grouped, key_rows.transpose(1, 0, 2), value_rows.transpose(1, 0, 2)))
    attn = heads_out.transpose(1, 2, 0, 3, 4).reshape(total, HEADS * HEAD_DIM)
    proj = grouped_product(attn, w_out, N_TENSOR)
    state = (tokens.astype(jnp.float32) + proj).astype(jnp.bfloat16)
    normed_two = rms_scale(state, mlp_gain)
    gate = jnp.dot(normed_two, w_gate, preferred_element_type=jnp.float32)
    upward = jnp.dot(normed_two, w_up, preferred_element_type=jnp.float32)
    hidden = (jax.nn.silu(gate) * upward).astype(jnp.bfloat16)
    down = grouped_product(hidden, w_down, N_TENSOR)
    return (state.astype(jnp.float32) + down).astype(jnp.bfloat16)
```

```python
import functools
import math

import jax
import jax.numpy as jnp
from jax import lax
from jax.experimental import pallas as pl
from jax.experimental.pallas import tpu as pltpu
from jax.sharding import PartitionSpec as P

HEAD_DIM = 128
KBLK = 512
SIDE = 4

EPSILON = 1e-05
ROPE_BASE = 500000.0
NEGATIVE = -1e30
MESH = pl.DeviceIdType.MESH

RANK = {0: 0, 3: 1, 1: 2, 2: 3}
ARRIVE = (0, 3, 1, 2)
DEPART = (2, 1, 3, 0)


def neighbour(half, first, step):
    me = lax.axis_index("tensor")
    z, x = me // SIDE, me % SIDE
    if (half == 0) == first:
        x = (x + step + SIDE) % SIDE
    else:
        z = (z + step + SIDE) % SIDE
    return {"tensor": z * SIDE + x}


def block_number(dz, dx):
    me = lax.axis_index("tensor")
    z, x = me // SIDE, me % SIDE
    return ((z + dz) % SIDE) * SIDE + (x + dx) % SIDE


def offsets(half, s, f):
    return (s, f) if half == 0 else (f, s)


def greet():
    barrier = pltpu.get_barrier_semaphore()
    for first in (True, False):
        for step in (1, -1):
            pl.semaphore_signal(barrier, inc=1, device_id=neighbour(0, first, step), device_id_type=MESH)
    pl.semaphore_wait(barrier, 4)


class Wires:
    def __init__(self, send_sems, recv_sems):
        self.send_sems, self.recv_sems, self.slots, self.started = send_sems, recv_sems, {}, []

    def copy(self, key, src, dst, device):
        slot = self.slots.setdefault(key, len(self.slots))
        return pltpu.make_async_remote_copy(
            src_ref=src,
            dst_ref=dst,
            send_sem=self.send_sems.at[slot],
            recv_sem=self.recv_sems.at[slot],
            device_id=device,
            device_id_type=MESH,
        )

    def start(self, key, src, dst, device):
        made = self.copy(key, src, dst, device)
        made.start()
        self.started.append(made)

    def arrive(self, key, dst, device):
        self.copy(key, dst, dst, device).wait_recv()

    def drain(self):
        for made in self.started:
            made.wait_send()
        self.started = []


def gather(wires, blocks, halves, consume):
    rows = blocks.shape[3]
    low, high = pl.ds(0, rows // 2), pl.ds(rows // 2, rows // 2)

    def at(h, s, f, part=None):
        return blocks.at[h, s, f] if part is None else blocks.at[h, s, f, part]

    def spread(h, f):
        wires.start((h, "s", 3, f), at(h, 0, f), at(h, 3, f), neighbour(h, False, 1))
        wires.start((h, "s", 1, f), at(h, 0, f), at(h, 1, f), neighbour(h, False, -1))

    def relay_second(h, f):
        wires.arrive((h, "s", 3, f), at(h, 3, f), neighbour(h, False, -1))
        wires.start((h, "t", 0, f), at(h, 3, f, low), at(h, 2, f, low), neighbour(h, False, 1))
        wires.arrive((h, "s", 1, f), at(h, 1, f), neighbour(h, False, 1))
        wires.start((h, "t", 1, f), at(h, 1, f, high), at(h, 2, f, high), neighbour(h, False, -1))

    for h in halves:
        wires.start((h, "f", 3), at(h, 0, 0), at(h, 0, 3), neighbour(h, True, 1))
        wires.start((h, "f", 1), at(h, 0, 0), at(h, 0, 1), neighbour(h, True, -1))
    for h in halves:
        spread(h, 0)
    for h in halves:
        wires.arrive((h, "f", 3), at(h, 0, 3), neighbour(h, True, -1))
        wires.start((h, "g", 0), at(h, 0, 3, low), at(h, 0, 2, low), neighbour(h, True, 1))
        wires.arrive((h, "f", 1), at(h, 0, 1), neighbour(h, True, 1))
        wires.start((h, "g", 1), at(h, 0, 1, high), at(h, 0, 2, high), neighbour(h, True, -1))
    for h in halves:
        spread(h, 3)
        spread(h, 1)
    for h in halves:
        relay_second(h, 0)
    for h in halves:
        wires.arrive((h, "g", 0), at(h, 0, 2, low), neighbour(h, True, -1))
        wires.arrive((h, "g", 1), at(h, 0, 2, high), neighbour(h, True, 1))
        spread(h, 2)
    for h in halves:
        consume(h, 0)
    for f in (3, 1, 2):
        for h in halves:
            relay_second(h, f)
    for s in (3, 1):
        for h in halves:
            consume(h, s)
    for h in halves:
        for f in (0, 3, 1, 2):
            wires.arrive((h, "t", 0, f), at(h, 2, f, low), neighbour(h, False, -1))
            wires.arrive((h, "t", 1, f), at(h, 2, f, high), neighbour(h, False, 1))
        consume(h, 2)
    wires.drain()


def scatter(wires, out, half_in, full_in, edge_half, edge_full, halves, produce):
    rows = out.shape[3]
    low, high = pl.ds(0, rows // 2), pl.ds(rows // 2, rows // 2)
    f32 = jnp.float32

    def wide(ref):
        return ref[...].astype(f32)

    for h in halves:
        produce(h, 2)
        for f in DEPART:
            wires.start((h, "a", 0, f), out.at[h, 2, f, low], half_in.at[h, 0, f], neighbour(h, False, 1))
            wires.start((h, "a", 1, f), out.at[h, 2, f, high], half_in.at[h, 1, f], neighbour(h, False, -1))
    for h in halves:
        produce(h, 1)
        produce(h, 3)
    for f in DEPART:
        for h in halves:
            wires.arrive((h, "a", 0, f), half_in.at[h, 0, f], neighbour(h, False, -1))
            mine = out.at[h, 1, f, low]
            mine[...] = (wide(mine) + wide(half_in.at[h, 0, f])).astype(mine.dtype)
            wires.start((h, "b", 0, f), out.at[h, 1, f], full_in.at[h, 0, f], neighbour(h, False, 1))
            wires.arrive((h, "a", 1, f), half_in.at[h, 1, f], neighbour(h, False, 1))
            mine = out.at[h, 3, f, high]
            mine[...] = (wide(mine) + wide(half_in.at[h, 1, f])).astype(mine.dtype)
            wires.start((h, "b", 1, f), out.at[h, 3, f], full_in.at[h, 1, f], neighbour(h, False, -1))
    for h in halves:
        produce(h, 0)

    def settle(h, f):
        wires.arrive((h, "b", 0, f), full_in.at[h, 0, f], neighbour(h, False, -1))
        wires.arrive((h, "b", 1, f), full_in.at[h, 1, f], neighbour(h, False, 1))
        return wide(out.at[h, 0, f]) + wide(full_in.at[h, 0, f]) + wide(full_in.at[h, 1, f])

    for h in halves:
        mine = out.at[h, 0, 2]
        mine[...] = settle(h, 2).astype(mine.dtype)
        wires.start((h, "c", 0), out.at[h, 0, 2, low], edge_half.at[h, 0], neighbour(h, True, 1))
        wires.start((h, "c", 1), out.at[h, 0, 2, high], edge_half.at[h, 1], neighbour(h, True, -1))
    for h in halves:
        for way, f, part, step in ((0, 1, low, 1), (1, 3, high, -1)):
            mine = out.at[h, 0, f]
            mine[...] = settle(h, f).astype(mine.dtype)
            wires.arrive((h, "c", way), edge_half.at[h, way], neighbour(h, True, -step))
            mine = out.at[h, 0, f, part]
            mine[...] = (wide(mine) + wide(edge_half.at[h, way])).astype(mine.dtype)
            wires.start((h, "d", way), out.at[h, 0, f], edge_full.at[h, way], neighbour(h, True, step))
    total = {}
    for h in halves:
        own = settle(h, 0)
        wires.arrive((h, "d", 0), edge_full.at[h, 0], neighbour(h, True, -1))
        wires.arrive((h, "d", 1), edge_full.at[h, 1], neighbour(h, True, 1))
        total[h] = own + wide(edge_full.at[h, 0]) + wide(edge_full.at[h, 1])
    wires.drain()
    return total


def norm_halves(rows, gain, width):
    mean_square = jnp.mean(rows * rows, axis=-1, keepdims=True)
    normed = (rows * lax.rsqrt(mean_square + EPSILON) * gain).astype(jnp.bfloat16)
    return normed[:, :width], normed[:, width:]


def project_kernel(
    tokens_ref, gain_ref, cos_ref, sin_ref, wq_hbm, wkv_hbm, q_ref, kv_ref,
    weights, blocks, acc, load_sems, send_sems, recv_sems,
):
    half_width = blocks.shape[4]
    qcols = wq_hbm.shape[1]
    cols = qcols + wkv_hbm.shape[1]
    loads = [
        pltpu.make_async_copy(wq_hbm, weights.at[:, pl.ds(0, qcols)], load_sems.at[0]),
        pltpu.make_async_copy(wkv_hbm, weights.at[:, pl.ds(qcols, cols - qcols)], load_sems.at[1]),
    ]
    for load in loads:
        load.start()
    greet()
    first, second = norm_halves(tokens_ref[...].astype(jnp.float32), gain_ref[...], half_width)
    blocks[0, 0, 0] = first
    blocks[1, 0, 0] = second
    holds_keys = lax.axis_index("tensor") % 2 == 0
    loaded = []

    def consume(h, s):
        if not loaded:
            for load in loads:
                load.wait()
            loaded.append(True)
        rows = blocks.shape[3]
        left = blocks[h, s].reshape(SIDE * rows, half_width)
        part = jnp.dot(
            left, weights[h * half_width : (h + 1) * half_width, :], preferred_element_type=jnp.float32
        ).reshape(SIDE, rows, cols)
        for f in range(SIDE):
            dz, dx = offsets(h, s, f)
            earlier = RANK[f] < RANK[s] or (RANK[f] == RANK[s] and h == 1)
            if not earlier:
                acc[dz, dx] = part[f]
                continue
            whole = acc[dz, dx] + part[f]
            number = block_number(dz, dx)
            cosine, sine = cos_ref[number], sin_ref[number]
            for head in range(qcols // HEAD_DIM):
                piece = whole[:, head * HEAD_DIM : (head + 1) * HEAD_DIM]
                turned = piece * cosine + pltpu.roll(piece, HEAD_DIM // 2, 1) * sine
                q_ref[number, :, head * HEAD_DIM : (head + 1) * HEAD_DIM] = turned.astype(jnp.bfloat16)
            piece = whole[:, qcols:]
            turned = piece * cosine + pltpu.roll(piece, HEAD_DIM // 2, 1) * sine
            kv_ref[number] = jnp.where(holds_keys, turned, piece).astype(jnp.bfloat16)

    gather(Wires(send_sems, recv_sems), blocks, (0, 1), consume)


def project(tokens, gain, cosine, sine, w_query, w_keyval):
    rows, width = tokens.shape
    devices = SIDE * SIDE
    cols = w_query.shape[1] + w_keyval.shape[1]
    vmem = pl.BlockSpec(memory_space=pltpu.VMEM)
    hbm = pl.BlockSpec(memory_space=pl.ANY)
    return pl.pallas_call(
        project_kernel,
        out_shape=(
            jax.ShapeDtypeStruct((devices, rows, w_query.shape[1]), jnp.bfloat16),
            jax.ShapeDtypeStruct((devices, rows, w_keyval.shape[1]), jnp.bfloat16),
        ),
        in_specs=[vmem] * 4 + [hbm] * 2,
        out_specs=(vmem, vmem),
        scratch_shapes=[
            pltpu.VMEM((width, cols), jnp.bfloat16),
            pltpu.VMEM((2, SIDE, SIDE, rows, width // 2), jnp.bfloat16),
            pltpu.VMEM((SIDE, SIDE, rows, cols), jnp.float32),
            pltpu.SemaphoreType.DMA((2,)),
            pltpu.SemaphoreType.DMA((40,)),
            pltpu.SemaphoreType.DMA((40,)),
        ],
        compiler_params=pltpu.CompilerParams(
            collective_id=0, has_side_effects=True, vmem_limit_bytes=40 << 20
        ),
        name="project",
    )(tokens, gain, cosine, sine, w_query, w_keyval)


def finish_kernel(
    tokens_ref, attn_ref, gain_ref, wo_hbm, wg_hbm, wu_hbm, wd_hbm, out_ref,
    wo, wg, wu, wd, blocks, acc_gate, acc_up, hidden, sending, half_in, full_in, edge_half, edge_full, state,
    load_sems, send_sems, recv_sems,
):
    rows, half_width = blocks.shape[3], blocks.shape[4]
    loads = [
        pltpu.make_async_copy(src, dst, load_sems.at[i])
        for i, (src, dst) in enumerate(((wo_hbm, wo), (wg_hbm, wg), (wu_hbm, wu), (wd_hbm, wd)))
    ]
    for load in loads:
        load.start()
    greet()
    halves = (0, 1)
    loads[0].wait()

    def columns(h):
        return pl.ds(h * half_width, half_width)

    def project_out(h, s):
        left = jnp.concatenate([attn_ref[block_number(*offsets(h, s, f))] for f in range(SIDE)], axis=0)
        part = jnp.dot(left, wo[:, columns(h)], preferred_element_type=jnp.float32)
        sending[h, s] = part.astype(jnp.bfloat16).reshape(SIDE, rows, half_width)

    proj = scatter(
        Wires(send_sems.at[0], recv_sems.at[0]),
        sending, half_in, full_in, edge_half, edge_full, halves, project_out,
    )
    for h in halves:
        state[:, columns(h)] = (tokens_ref[:, columns(h)].astype(jnp.float32) + proj[h]).astype(jnp.bfloat16)
    first, second = norm_halves(state[...].astype(jnp.float32), gain_ref[...], half_width)
    blocks[0, 0, 0] = first
    blocks[1, 0, 0] = second
    loads[1].wait()
    loads[2].wait()

    def gated(h, s):
        left = blocks[h, s].reshape(SIDE * rows, half_width)
        gate = jnp.dot(left, wg[columns(h), :], preferred_element_type=jnp.float32)
        upward = jnp.dot(left, wu[columns(h), :], preferred_element_type=jnp.float32)
        for f in range(SIDE):
            dz, dx = offsets(h, s, f)
            earlier = RANK[f] < RANK[s] or (RANK[f] == RANK[s] and h == 1)
            g, u = gate[f * rows : (f + 1) * rows], upward[f * rows : (f + 1) * rows]
            if not earlier:
                acc_gate[dz, dx], acc_up[dz, dx] = g, u
                continue
            g, u = g + acc_gate[dz, dx], u + acc_up[dz, dx]
            hidden[dz, dx] = (g / (1.0 + jnp.exp(-g)) * u).astype(jnp.bfloat16)

    gather(Wires(send_sems.at[1], recv_sems.at[1]), blocks, halves, gated)
    loads[3].wait()

    def project_down(h, s):
        left = jnp.concatenate([hidden[offsets(h, s, f)] for f in range(SIDE)], axis=0)
        part = jnp.dot(left, wd[:, columns(h)], preferred_element_type=jnp.float32)
        sending[h, s] = part.astype(jnp.bfloat16).reshape(SIDE, rows, half_width)

    down = scatter(
        Wires(send_sems.at[2], recv_sems.at[2]),
        sending, half_in, full_in, edge_half, edge_full, halves, project_down,
    )
    for h in halves:
        out_ref[:, columns(h)] = (state[:, columns(h)].astype(jnp.float32) + down[h]).astype(jnp.bfloat16)


def finish(tokens, attn, gain, w_out, w_gate, w_up, w_down):
    rows, width = tokens.shape
    hidden = w_gate.shape[1]
    vmem = pl.BlockSpec(memory_space=pltpu.VMEM)
    hbm = pl.BlockSpec(memory_space=pl.ANY)
    half = width // 2
    bf16 = jnp.bfloat16
    return pl.pallas_call(
        finish_kernel,
        out_shape=jax.ShapeDtypeStruct((rows, width), bf16),
        in_specs=[vmem] * 3 + [hbm] * 4,
        out_specs=vmem,
        scratch_shapes=[
            pltpu.VMEM(w_out.shape, bf16),
            pltpu.VMEM(w_gate.shape, bf16),
            pltpu.VMEM(w_up.shape, bf16),
            pltpu.VMEM(w_down.shape, bf16),
            pltpu.VMEM((2, SIDE, SIDE, rows, half), bf16),
            pltpu.VMEM((SIDE, SIDE, rows, hidden), jnp.float32),
            pltpu.VMEM((SIDE, SIDE, rows, hidden), jnp.float32),
            pltpu.VMEM((SIDE, SIDE, rows, hidden), bf16),
            pltpu.VMEM((2, SIDE, SIDE, rows, half), bf16),
            pltpu.VMEM((2, 2, SIDE, rows // 2, half), bf16),
            pltpu.VMEM((2, 2, SIDE, rows, half), bf16),
            pltpu.VMEM((2, 2, rows // 2, half), bf16),
            pltpu.VMEM((2, 2, rows, half), bf16),
            pltpu.VMEM((rows, width), bf16),
            pltpu.SemaphoreType.DMA((4,)),
            pltpu.SemaphoreType.DMA((3, 40)),
            pltpu.SemaphoreType.DMA((3, 40)),
        ],
        compiler_params=pltpu.CompilerParams(
            collective_id=1, has_side_effects=True, vmem_limit_bytes=60 << 20
        ),
        name="finish",
    )(tokens, attn, gain, w_out, w_gate, w_up, w_down)


def attend_kernel(bounds, q_ref, k_ref, v_ref, first_ref, o_ref, *, qblk):
    block = pl.program_id(0)
    low, high, clear_low, clear_high, row0 = (bounds[i, block] for i in range(5))
    heads = q_ref.shape[1] // HEAD_DIM
    rows = heads * qblk
    factor = math.log2(math.e) / math.sqrt(HEAD_DIM)
    query = jnp.concatenate([q_ref[:, h * HEAD_DIM : (h + 1) * HEAD_DIM] for h in range(heads)], axis=0)
    first = jnp.concatenate([first_ref[...]] * heads, axis=0)
    spot = lax.broadcasted_iota(jnp.int32, (qblk, 1), 0) + row0
    last = jnp.concatenate([spot] * heads, axis=0)

    def advance(masked, number, carry):
        peak, totals, summed = carry
        start = pl.multiple_of(number * KBLK, KBLK)
        keys = k_ref[pl.ds(start, KBLK), :]
        values = v_ref[pl.ds(start, KBLK), :]
        scores = lax.dot_general(query, keys, (((1,), (1,)), ((), ())), preferred_element_type=jnp.float32) * factor
        if masked:
            spots = lax.broadcasted_iota(jnp.int32, (rows, KBLK), 1) + start
            scores = jnp.where((spots >= first) & (spots <= last), scores, NEGATIVE)
        new_peak = jnp.maximum(peak, jnp.max(scores, axis=1, keepdims=True))
        decay = jnp.exp2(peak - new_peak)
        weights = jnp.exp2(scores - new_peak)
        totals = totals * decay + jnp.sum(weights, axis=1, keepdims=True)
        summed = summed * decay + jnp.dot(weights.astype(jnp.bfloat16), values, preferred_element_type=jnp.float32)
        return new_peak, totals, summed

    carry = (
        jnp.full((rows, 1), NEGATIVE, jnp.float32),
        jnp.zeros((rows, 1), jnp.float32),
        jnp.zeros((rows, HEAD_DIM), jnp.float32),
    )
    carry = lax.fori_loop(low, clear_low, functools.partial(advance, True), carry)
    carry = lax.fori_loop(clear_low, clear_high, functools.partial(advance, False), carry)
    peak, totals, summed = lax.fori_loop(clear_high, high, functools.partial(advance, True), carry)
    answer = (summed / totals).astype(jnp.bfloat16)
    for h in range(heads):
        o_ref[:, h * HEAD_DIM : (h + 1) * HEAD_DIM] = answer[h * qblk : (h + 1) * qblk]


def attend(queries, keys, values, first, bounds, qblk):
    total, cols = queries.shape
    whole = pl.BlockSpec(memory_space=pltpu.VMEM)
    return pl.pallas_call(
        functools.partial(attend_kernel, qblk=qblk),
        out_shape=jax.ShapeDtypeStruct((total, cols), jnp.bfloat16),
        grid_spec=pltpu.PrefetchScalarGridSpec(
            num_scalar_prefetch=1,
            grid=(total // qblk,),
            in_specs=[
                pl.BlockSpec((qblk, cols), lambda i, b: (i, 0)),
                whole,
                whole,
                pl.BlockSpec((qblk, 1), lambda i, b: (i, 0)),
            ],
            out_specs=pl.BlockSpec((qblk, cols), lambda i, b: (i, 0)),
        ),
        compiler_params=pltpu.CompilerParams(vmem_limit_bytes=40 << 20),
        name="attend",
    )(bounds, queries, keys, values, first)


def swapped(block, axis):
    count = lax.axis_size(axis)
    return lax.ppermute(block, axis, [(i, i ^ 1) for i in range(count)])


def body(tokens, doc_lengths, attn_gain, mlp_gain, w_query, w_keyval, w_out, w_gate, w_up, w_down):
    devices = lax.axis_size("tensor")
    token_index = lax.axis_index("token")
    tensor_index = lax.axis_index("tensor")
    rows = tokens.shape[0]
    block_rows = rows * devices
    ends = jnp.cumsum(doc_lengths)
    spots = token_index * block_rows + jnp.arange(block_rows, dtype=jnp.int32)
    passed = spots[:, None] >= ends[None, :-1]
    first = jnp.max(jnp.where(passed, ends[None, :-1], 0), axis=1)
    position = (spots - first).astype(jnp.float32)
    half = HEAD_DIM // 2
    freq = jnp.exp(-math.log(ROPE_BASE) * jnp.arange(half, dtype=jnp.float32) * (2.0 / HEAD_DIM))
    angle = position[:, None] * freq[None, :]
    cosine, sine = jnp.cos(angle), jnp.sin(angle)
    cosine = jnp.concatenate([cosine, cosine], axis=1).reshape(devices, rows, HEAD_DIM)
    sine = jnp.concatenate([-sine, sine], axis=1).reshape(devices, rows, HEAD_DIM)
    queries, own_half = project(tokens, attn_gain[None, :], cosine, sine, w_query, w_keyval)
    queries = queries.reshape(block_rows, w_query.shape[1])
    own_half = own_half.reshape(block_rows, HEAD_DIM)
    is_even = tensor_index % 2 == 0
    other_half = swapped(own_half, "tensor")
    keys = jnp.where(is_even, own_half, other_half)
    values = jnp.where(is_even, other_half, own_half)
    both = lax.all_gather(jnp.concatenate([keys, values], axis=1), "token", axis=0, tiled=True)
    qblk = 256
    heads_of = first[::qblk]
    tails_of = first[qblk - 1 :: qblk]
    row0 = spots[::qblk]
    low = heads_of // KBLK
    high = (row0 + qblk - 1) // KBLK + 1
    clear_low = jnp.minimum((tails_of + KBLK - 1) // KBLK, high)
    clear_high = jnp.maximum(row0 // KBLK, clear_low)
    bounds = jnp.stack([low, high, clear_low, clear_high, row0]).astype(jnp.int32)
    attn = attend(queries, both[:, :HEAD_DIM], both[:, HEAD_DIM:], first[:, None].astype(jnp.int32), bounds, qblk)
    attn = attn.reshape(devices, rows, attn.shape[1])
    return finish(tokens, attn, mlp_gain[None, :], w_out, w_gate, w_up, w_down)


def solution(mesh):
    return jax.shard_map(
        body,
        mesh=mesh,
        in_specs=(
            P(("token", "tensor"), None),
            P(),
            P(),
            P(),
            P(None, "tensor"),
            P(None, "tensor"),
            P("tensor", None),
            P(None, "tensor"),
            P(None, "tensor"),
            P("tensor", None),
        ),
        out_specs=P(("token", "tensor"), None),
        check_vma=False,
    )
```

```python
import functools
import math

import jax
import jax.numpy as jnp
from jax import lax
from jax.experimental import pallas as pl
from jax.experimental.pallas import tpu as pltpu
from jax.sharding import PartitionSpec as P

HEAD_DIM = 128
KBLK = 512
SIDE = 4
CORES = 2
YS = 4

EPSILON = 1e-05
ROPE_BASE = 500000.0
NEGATIVE = -1e30
MESH = pl.DeviceIdType.MESH


def place():
    me, token = lax.axis_index("tensor"), lax.axis_index("token")
    return me // SIDE, me % SIDE, token // CORES, token % CORES


def along_z(step):
    z, x, _, _ = place()
    return {"tensor": ((z + step + SIDE) % SIDE) * SIDE + x}


def mate():
    z, x, _, _ = place()
    return {"tensor": z * SIDE + SIDE - 1 - x}


def holder():
    z, x, _, _ = place()
    return {"tensor": z * SIDE + x + 1 - 2 * (x % 2)}


def along_y(step):
    _, _, y, core = place()
    return {"token": ((y + step + YS) % YS) * CORES + core}


def twin():
    _, _, y, core = place()
    return {"token": y * CORES + 1 - core}


def greet():
    barrier = pltpu.get_barrier_semaphore()
    others = [along_z(1), along_z(-1), mate(), holder(), along_y(1), along_y(-1), twin()]
    for other in others:
        pl.semaphore_signal(barrier, inc=1, device_id=other, device_id_type=MESH)
    pl.semaphore_wait(barrier, len(others))


class Wires:
    def __init__(self, send_sems, recv_sems):
        self.send_sems, self.recv_sems, self.slots, self.started = send_sems, recv_sems, {}, []

    def copy(self, key, src, dst, device):
        slot = self.slots.setdefault(key, len(self.slots))
        return pltpu.make_async_remote_copy(
            src_ref=src,
            dst_ref=dst,
            send_sem=self.send_sems.at[slot],
            recv_sem=self.recv_sems.at[slot],
            device_id=device,
            device_id_type=MESH,
        )

    def start(self, key, src, dst, device):
        made = self.copy(key, src, dst, device)
        made.start()
        self.started.append(made)

    def arrive(self, key, dst, device):
        self.copy(key, dst, dst, device).wait_recv()

    def drain(self):
        for made in self.started:
            made.wait_send()
        self.started = []


class Fetch:
    def __init__(self, wires, name, src, dst, lanes, first_lane=0):
        self.wires, self.name, self.src, self.dst, self.lanes, self.first_lane = wires, name, src, dst, lanes, first_lane
        self.size = src.shape[1 if lanes else 0] // (YS * CORES)

    def cut(self, ref, number, part, offset):
        size = self.size if part is None else self.size // 2
        start = pl.multiple_of(number * self.size, self.size) + (0 if part in (None, 0) else size)
        start = pl.multiple_of(start, size)
        if self.lanes:
            return ref.at[:, pl.ds(start, size)]
        return ref.at[pl.ds(start, size), pl.ds(offset, self.src.shape[1])]

    def slot(self, dy, dc, part=None):
        _, _, y, core = place()
        number = ((y + dy + YS) % YS) * CORES + (core if dc == 0 else 1 - core)
        return self.cut(self.dst, number, part, self.first_lane)

    def start(self, key, ref, device):
        self.wires.start((self.name, key), ref, ref, device)

    def arrive(self, key, ref):
        self.wires.arrive((self.name, key), ref, holder())

    def ask(self):
        _, _, y, core = place()
        self.wires.start((self.name, "x"), self.cut(self.src, y * CORES + core, None, 0), self.slot(0, 0), holder())

    def relay(self):
        self.arrive("x", self.slot(0, 0))
        self.start("y3", self.slot(0, 0), along_y(1))
        self.start("y1", self.slot(0, 0), along_y(-1))
        self.start("c0", self.slot(0, 0), twin())

    def pass_on(self):
        self.arrive("y3", self.slot(3, 0))
        self.start("h0", self.slot(3, 0, 0), along_y(1))
        self.start("c3", self.slot(3, 0), twin())
        self.arrive("y1", self.slot(1, 0))
        self.start("h1", self.slot(1, 0, 1), along_y(-1))
        self.start("c1", self.slot(1, 0), twin())

    def settle(self):
        self.arrive("h0", self.slot(2, 0, 0))
        self.arrive("h1", self.slot(2, 0, 1))
        self.start("c2", self.slot(2, 0), twin())

    def finish(self):
        for dy in (0, 3, 1, 2):
            self.arrive("c%d" % dy, self.slot(dy, 1))


def gather(wires, blocks, hook):
    rows = blocks.shape[3]
    low, high = pl.ds(0, rows // 2), pl.ds(rows // 2, rows // 2)
    up, down = 1, -1

    def full(h, dz, m):
        return blocks.at[h, dz, m]

    def spread(h, m):
        wires.start(("s", h, 3, m), full(h, 0, m), full(h, 3, m), along_z(up))
        wires.start(("s", h, 1, m), full(h, 0, m), full(h, 1, m), along_z(down))

    def to_mate(h, dz):
        wires.start(("m", h, dz), full(h, dz, 0), full(h, dz, 1), mate())

    def relay(h, m, onward):
        wires.arrive(("s", h, 3, m), full(h, 3, m), along_z(down))
        wires.start(("t", h, 0, m), blocks.at[h, 3, m, low], blocks.at[h, 2, m, low], along_z(up))
        if onward:
            to_mate(h, 3)
        wires.arrive(("s", h, 1, m), full(h, 1, m), along_z(up))
        wires.start(("t", h, 1, m), blocks.at[h, 1, m, high], blocks.at[h, 2, m, high], along_z(down))
        if onward:
            to_mate(h, 1)

    def last(h, m):
        wires.arrive(("t", h, 0, m), blocks.at[h, 2, m, low], along_z(down))
        wires.arrive(("t", h, 1, m), blocks.at[h, 2, m, high], along_z(up))

    to_mate(0, 0)
    spread(1, 0)
    spread(0, 0)
    to_mate(1, 0)
    hook("sent")
    wires.arrive(("m", 0, 0), full(0, 0, 1), mate())
    spread(0, 1)
    relay(1, 0, True)
    relay(0, 0, False)
    hook("early")
    wires.arrive(("m", 1, 0), full(1, 0, 1), mate())
    hook("own pair")
    last(1, 0)
    to_mate(1, 2)
    relay(0, 1, False)
    hook("middle")
    wires.arrive(("m", 1, 3), full(1, 3, 1), mate())
    wires.arrive(("m", 1, 1), full(1, 1, 1), mate())
    hook("sides")
    last(0, 0)
    last(0, 1)
    wires.arrive(("m", 1, 2), full(1, 2, 1), mate())
    hook("far")


def scatter(wires, out, bufs, produce, hook):
    z_half, z_full, mate0, mate1, e_half, e_full = bufs
    rows = out.shape[3]
    low, high = pl.ds(0, rows // 2), pl.ds(rows // 2, rows // 2)
    ways = ((0, 1, low, 1), (1, 3, high, -1))
    f32 = jnp.float32

    def wide(ref):
        return ref[...].astype(f32)

    def add_to(ref, *others):
        total = wide(ref)
        for other in others:
            total = total + wide(other)
        ref[...] = total.astype(ref.dtype)

    def mate_send(dz):
        wires.start(("m1", dz), out.at[1, dz, 1], mate1.at[dz], mate())

    def mate_join(dz):
        wires.arrive(("m1", dz), mate1.at[dz], mate())
        add_to(out.at[1, dz, 0], mate1.at[dz])

    produce(1, (2,))
    mate_send(2)
    produce(0, (2,))
    for m in (1, 0):
        for way, dz, part, step in ways:
            wires.start(("a", way, m), out.at[0, 2, m, part], z_half.at[way, m], along_z(step))
    produce(0, (1, 3))
    produce(1, (1, 3))
    mate_send(1)
    mate_send(3)
    mate_join(2)
    for way, dz, part, step in ways:
        wires.start(("e", way), out.at[1, 2, 0, part], e_half.at[way], along_z(step))
    for m in (1, 0):
        for way, dz, part, step in ways:
            wires.arrive(("a", way, m), z_half.at[way, m], along_z(-step))
            add_to(out.at[0, dz, m, part], z_half.at[way, m])
            wires.start(("b", way, m), out.at[0, dz, m], z_full.at[way, m], along_z(step))
    produce(1, (0,))
    mate_send(0)
    produce(0, (0,))
    hook("early")
    for way, dz, part, step in ways:
        mate_join(dz)
        wires.arrive(("e", way), e_half.at[way], along_z(-step))
        add_to(out.at[1, dz, 0, part], e_half.at[way])
        wires.start(("f", way), out.at[1, dz, 0], e_full.at[way], along_z(step))
    hook("middle")
    for way, dz, part, step in ways:
        wires.arrive(("b", way, 1), z_full.at[way, 1], along_z(-step))
    add_to(out.at[0, 0, 1], z_full.at[0, 1], z_full.at[1, 1])
    wires.start(("m0",), out.at[0, 0, 1], mate0, mate())
    hook("late")
    for way, dz, part, step in ways:
        wires.arrive(("b", way, 0), z_full.at[way, 0], along_z(-step))
    first = wide(out.at[0, 0, 0]) + wide(z_full.at[0, 0]) + wide(z_full.at[1, 0])
    wires.arrive(("m1", 0), mate1.at[0], mate())
    second = wide(out.at[1, 0, 0]) + wide(mate1.at[0])
    for way, dz, part, step in ways:
        wires.arrive(("f", way), e_full.at[way], along_z(-step))
        second = second + wide(e_full.at[way])
    wires.arrive(("m0",), mate0, mate())
    first = first + wide(mate0)
    return first, second


def norm_halves(rows, gain, width):
    mean_square = jnp.mean(rows * rows, axis=-1, keepdims=True)
    normed = (rows * lax.rsqrt(mean_square + EPSILON) * gain).astype(jnp.bfloat16)
    return normed[:, :width], normed[:, width:]


def stacked(blocks, h, dzs):
    rows, width = blocks.shape[3], blocks.shape[4]
    parts = [blocks[h, dz].reshape(2 * rows, width) for dz in dzs]
    return parts[0] if len(parts) == 1 else jnp.concatenate(parts, axis=0)


def project_kernel(
    tokens_ref, gain_ref, cos_ref, sin_ref, wq_hbm, wkv_hbm, wo_hbm, q_ref, kv_ref, wo_other,
    weights, others, blocks, load_sems, send_sems, recv_sems,
):
    rows, half_width = blocks.shape[3], blocks.shape[4]
    qcols = wq_hbm.shape[1]
    cols = qcols + wkv_hbm.shape[1]
    z, x, _, _ = place()
    loads = [
        pltpu.make_async_copy(wq_hbm, weights.at[:, pl.ds(0, qcols)], load_sems.at[0]),
        pltpu.make_async_copy(wkv_hbm, weights.at[:, pl.ds(qcols, cols - qcols)], load_sems.at[1]),
    ]
    for load in loads:
        load.start()
    first, second = norm_halves(tokens_ref[...].astype(jnp.float32), gain_ref[...], half_width)
    blocks[0, 0, 0] = first
    blocks[1, 0, 0] = second
    greet()
    wires = Wires(send_sems, recv_sems)
    fetch_q = Fetch(wires, "q", wq_hbm, others, False, 0)
    fetch_kv = Fetch(wires, "kv", wkv_hbm, others, False, qcols)
    fetch_o = Fetch(wires, "o", wo_hbm, wo_other, True)

    def emit(dzs, mine):
        shard = weights if mine else others
        part = sum(
            jnp.dot(
                stacked(blocks, h, dzs),
                shard[h * half_width : (h + 1) * half_width, :],
                preferred_element_type=jnp.float32,
            )
            for h in range(2)
        )
        is_key = (x % 2 == 0) if mine else (x % 2 == 1)
        which = x % 2 if mine else 1 - x % 2
        first_col = 0 if mine else qcols
        for i, dz in enumerate(dzs):
            for m in range(2):
                whole = part[(2 * i + m) * rows : (2 * i + m + 1) * rows]
                zz = (z + dz) % SIDE
                mm = x // 2 if m == 0 else 1 - x // 2
                cosine, sine = cos_ref[zz, mm], sin_ref[zz, mm]
                for head in range(qcols // HEAD_DIM):
                    piece = whole[:, head * HEAD_DIM : (head + 1) * HEAD_DIM]
                    turned = piece * cosine + pltpu.roll(piece, HEAD_DIM // 2, 1) * sine
                    at = first_col + head * HEAD_DIM
                    q_ref[zz, mm, :, at : at + HEAD_DIM] = turned.astype(jnp.bfloat16)
                piece = whole[:, qcols:]
                turned = piece * cosine + pltpu.roll(piece, HEAD_DIM // 2, 1) * sine
                kv_ref[which, zz, mm] = jnp.where(is_key, turned, piece).astype(jnp.bfloat16)

    def hook(name):
        if name == "sent":
            for fetch in (fetch_q, fetch_kv, fetch_o):
                fetch.ask()
        elif name == "early":
            fetch_q.relay()
            fetch_kv.relay()
            for load in loads:
                load.wait()
        elif name == "own pair":
            emit((0,), True)
        elif name == "middle":
            fetch_q.pass_on()
            fetch_kv.pass_on()
            fetch_o.relay()
        elif name == "sides":
            emit((3, 1), True)
            fetch_q.settle()
            fetch_kv.settle()
            fetch_q.finish()
            fetch_kv.finish()
            emit((0,), False)
            emit((3, 1), False)
            fetch_o.pass_on()
        else:
            emit((2,), True)
            emit((2,), False)
            fetch_o.settle()
            fetch_o.finish()

    gather(wires, blocks, hook)
    wires.drain()


def project(tokens, gain, cosine, sine, w_query, w_keyval, w_out):
    rows, width = tokens.shape
    cols = w_query.shape[1] + w_keyval.shape[1]
    vmem = pl.BlockSpec(memory_space=pltpu.VMEM)
    hbm = pl.BlockSpec(memory_space=pl.ANY)
    bf16 = jnp.bfloat16
    return pl.pallas_call(
        project_kernel,
        out_shape=(
            jax.ShapeDtypeStruct((SIDE, 2, rows, 2 * w_query.shape[1]), bf16),
            jax.ShapeDtypeStruct((2, SIDE, 2, rows, w_keyval.shape[1]), bf16),
            jax.ShapeDtypeStruct(w_out.shape, bf16),
        ),
        in_specs=[vmem] * 4 + [hbm] * 3,
        out_specs=(vmem, vmem, hbm),
        scratch_shapes=[
            pltpu.VMEM((width, cols), bf16),
            pltpu.VMEM((width, cols), bf16),
            pltpu.VMEM((2, SIDE, 2, rows, width // 2), bf16),
            pltpu.SemaphoreType.DMA((2,)),
            pltpu.SemaphoreType.DMA((64,)),
            pltpu.SemaphoreType.DMA((64,)),
        ],
        compiler_params=pltpu.CompilerParams(
            collective_id=0, has_side_effects=True, vmem_limit_bytes=48 << 20
        ),
        name="project",
    )(tokens, gain, cosine, sine, w_query, w_keyval, w_out)


def finish_kernel(
    tokens_ref, attn_ref, gain_ref, wo_hbm, wo2_hbm, wg_hbm, wu_hbm, wd_hbm, out_ref,
    wo, wg, wu, wd, wg2, wu2, wd2, blocks, hidden, hidden2, sending,
    z_half, z_full, mate0, mate1, e_half, e_full, state, load_sems, send_sems, recv_sems,
):
    rows, half_width = blocks.shape[3], blocks.shape[4]
    own = wo_hbm.shape[0]
    z, x, _, _ = place()
    loads = [
        pltpu.make_async_copy(src, dst, load_sems.at[i])
        for i, (src, dst) in enumerate(
            ((wo_hbm, wo.at[pl.ds(0, own)]), (wo2_hbm, wo.at[pl.ds(own, own)]), (wg_hbm, wg), (wu_hbm, wu), (wd_hbm, wd))
        )
    ]
    for load in loads:
        load.start()
    greet()
    bufs = (z_half, z_full, mate0, mate1, e_half, e_full)
    weight_wires = Wires(send_sems.at[3], recv_sems.at[3])
    fetch_g = Fetch(weight_wires, "g", wg_hbm, wg2, True)
    fetch_u = Fetch(weight_wires, "u", wu_hbm, wu2, True)
    fetch_d = Fetch(weight_wires, "d", wd_hbm, wd2, True)
    fetch_g.ask()
    fetch_u.ask()
    loads[0].wait()
    loads[1].wait()

    def columns(h):
        return pl.ds(h * half_width, half_width)

    def keep(h, dzs, part):
        for i, dz in enumerate(dzs):
            piece = part[2 * i * rows : 2 * (i + 1) * rows].astype(jnp.bfloat16)
            sending[h, dz] = piece.reshape(2, rows, half_width)

    def project_out(h, dzs):
        mine, other = x // 2, 1 - x // 2
        left = [attn_ref[(z + dz) % SIDE, m] for dz in dzs for m in (mine, other)]
        left = jnp.concatenate(left, axis=0)
        keep(h, dzs, jnp.dot(left, wo[:, columns(h)], preferred_element_type=jnp.float32))

    def hook_out(name):
        if name == "early":
            fetch_g.relay()
        elif name == "middle":
            fetch_g.pass_on()
        else:
            fetch_u.relay()

    out_wires = Wires(send_sems.at[0], recv_sems.at[0])
    first, second = scatter(out_wires, sending, bufs, project_out, hook_out)
    for h, proj in enumerate((first, second)):
        state[:, columns(h)] = (tokens_ref[:, columns(h)].astype(jnp.float32) + proj).astype(jnp.bfloat16)
    first, second = norm_halves(state[...].astype(jnp.float32), gain_ref[...], half_width)
    blocks[0, 0, 0] = first
    blocks[1, 0, 0] = second

    def gated(dzs, mine):
        gates, ups, result = (wg, wu, hidden) if mine else (wg2, wu2, hidden2)
        gate = upward = 0.0
        for h in range(2):
            left = stacked(blocks, h, dzs)
            across = (((1,), (1,)), ((), ()))
            gate = gate + lax.dot_general(left, gates[:, columns(h)], across, preferred_element_type=jnp.float32)
            upward = upward + lax.dot_general(left, ups[:, columns(h)], across, preferred_element_type=jnp.float32)
        value = (gate / (1.0 + jnp.exp(-gate)) * upward).astype(jnp.bfloat16)
        for i, dz in enumerate(dzs):
            result[dz] = value[2 * i * rows : 2 * (i + 1) * rows].reshape(2, rows, value.shape[1])

    def hook_gated(name):
        if name == "sent":
            fetch_d.ask()
            fetch_g.settle()
            loads[2].wait()
            loads[3].wait()
        elif name == "early":
            fetch_u.pass_on()
            fetch_g.finish()
        elif name == "own pair":
            gated((0,), True)
            fetch_d.relay()
        elif name == "middle":
            fetch_u.settle()
        elif name == "sides":
            gated((3, 1), True)
            fetch_u.finish()
            gated((0,), False)
            gated((3, 1), False)
            fetch_d.pass_on()
        else:
            gated((2,), True)
            gated((2,), False)
            fetch_d.settle()
            fetch_d.finish()
            loads[4].wait()

    gather_wires = Wires(send_sems.at[1], recv_sems.at[1])
    gather(gather_wires, blocks, hook_gated)
    out_wires.drain()

    def project_down(h, dzs):
        part = 0.0
        for values, weights in ((hidden, wd), (hidden2, wd2)):
            left = [values[dz].reshape(2 * rows, values.shape[3]) for dz in dzs]
            left = left[0] if len(left) == 1 else jnp.concatenate(left, axis=0)
            part = part + jnp.dot(left, weights[:, columns(h)], preferred_element_type=jnp.float32)
        keep(h, dzs, part)

    down_wires = Wires(send_sems.at[2], recv_sems.at[2])
    down = scatter(down_wires, sending, bufs, project_down, lambda name: None)
    for h in range(2):
        out_ref[:, columns(h)] = (state[:, columns(h)].astype(jnp.float32) + down[h]).astype(jnp.bfloat16)
    for wires in (gather_wires, down_wires, weight_wires):
        wires.drain()


def finish(tokens, attn, gain, w_out, w_out_other, w_gate, w_up, w_down):
    rows, width = tokens.shape
    hidden = w_gate.shape[0]
    vmem = pl.BlockSpec(memory_space=pltpu.VMEM)
    hbm = pl.BlockSpec(memory_space=pl.ANY)
    half = width // 2
    bf16 = jnp.bfloat16
    return pl.pallas_call(
        finish_kernel,
        out_shape=jax.ShapeDtypeStruct((rows, width), bf16),
        in_specs=[vmem] * 3 + [hbm] * 5,
        out_specs=vmem,
        scratch_shapes=[
            pltpu.VMEM((2 * w_out.shape[0], width), bf16),
            *[pltpu.VMEM((hidden, width), bf16)] * 6,
            pltpu.VMEM((2, SIDE, 2, rows, half), bf16),
            pltpu.VMEM((SIDE, 2, rows, hidden), bf16),
            pltpu.VMEM((SIDE, 2, rows, hidden), bf16),
            pltpu.VMEM((2, SIDE, 2, rows, half), bf16),
            pltpu.VMEM((2, 2, rows // 2, half), bf16),
            pltpu.VMEM((2, 2, rows, half), bf16),
            pltpu.VMEM((rows, half), bf16),
            pltpu.VMEM((SIDE, rows, half), bf16),
            pltpu.VMEM((2, rows // 2, half), bf16),
            pltpu.VMEM((2, rows, half), bf16),
            pltpu.VMEM((rows, width), bf16),
            pltpu.SemaphoreType.DMA((5,)),
            pltpu.SemaphoreType.DMA((4, 48)),
            pltpu.SemaphoreType.DMA((4, 48)),
        ],
        compiler_params=pltpu.CompilerParams(
            collective_id=1, has_side_effects=True, vmem_limit_bytes=60 << 20
        ),
        name="finish",
    )(tokens, attn, gain, w_out, w_out_other, w_gate, w_up, w_down)


def attend_kernel(bounds, q_ref, k_ref, v_ref, first_ref, last_ref, o_ref, *, qblk):
    block = pl.program_id(0)
    low, high, clear_low, clear_high = (bounds[i, block] for i in range(4))
    heads = q_ref.shape[1] // HEAD_DIM
    rows = heads * qblk
    factor = math.log2(math.e) / math.sqrt(HEAD_DIM)
    query = jnp.concatenate([q_ref[:, h * HEAD_DIM : (h + 1) * HEAD_DIM] for h in range(heads)], axis=0)
    first = jnp.concatenate([first_ref[...]] * heads, axis=0)
    last = jnp.concatenate([last_ref[...]] * heads, axis=0)

    def advance(masked, number, carry):
        peak, totals, summed = carry
        start = pl.multiple_of(number * KBLK, KBLK)
        keys = k_ref[pl.ds(start, KBLK), :]
        values = v_ref[pl.ds(start, KBLK), :]
        scores = lax.dot_general(query, keys, (((1,), (1,)), ((), ())), preferred_element_type=jnp.float32) * factor
        if masked:
            spots = lax.broadcasted_iota(jnp.int32, (rows, KBLK), 1) + start
            scores = jnp.where((spots >= first) & (spots <= last), scores, NEGATIVE)
        new_peak = jnp.maximum(peak, jnp.max(scores, axis=1, keepdims=True))
        decay = jnp.exp2(peak - new_peak)
        weights = jnp.exp2(scores - new_peak)
        totals = totals * decay + jnp.sum(weights, axis=1, keepdims=True)
        summed = summed * decay + jnp.dot(weights.astype(jnp.bfloat16), values, preferred_element_type=jnp.float32)
        return new_peak, totals, summed

    carry = (
        jnp.full((rows, 1), NEGATIVE, jnp.float32),
        jnp.zeros((rows, 1), jnp.float32),
        jnp.zeros((rows, HEAD_DIM), jnp.float32),
    )
    carry = lax.fori_loop(low, clear_low, functools.partial(advance, True), carry)
    carry = lax.fori_loop(clear_low, clear_high, functools.partial(advance, False), carry)
    peak, totals, summed = lax.fori_loop(clear_high, high, functools.partial(advance, True), carry)
    answer = (summed / totals).astype(jnp.bfloat16)
    for h in range(heads):
        o_ref[:, h * HEAD_DIM : (h + 1) * HEAD_DIM] = answer[h * qblk : (h + 1) * qblk]


def attend(queries, keys, values, first, last, bounds, qblk):
    total, cols = queries.shape
    whole = pl.BlockSpec(memory_space=pltpu.VMEM)
    return pl.pallas_call(
        functools.partial(attend_kernel, qblk=qblk),
        out_shape=jax.ShapeDtypeStruct((total, cols), jnp.bfloat16),
        grid_spec=pltpu.PrefetchScalarGridSpec(
            num_scalar_prefetch=1,
            grid=(total // qblk,),
            in_specs=[
                pl.BlockSpec((qblk, cols), lambda i, b: (i, 0)),
                whole,
                whole,
                pl.BlockSpec((qblk, 1), lambda i, b: (i, 0)),
                pl.BlockSpec((qblk, 1), lambda i, b: (i, 0)),
            ],
            out_specs=pl.BlockSpec((qblk, cols), lambda i, b: (i, 0)),
        ),
        compiler_params=pltpu.CompilerParams(vmem_limit_bytes=40 << 20),
        name="attend",
    )(bounds, queries, keys, values, first, last)


def body(tokens, doc_lengths, attn_gain, mlp_gain, w_query, w_keyval, w_out, w_gate, w_up, w_down):
    token_index = lax.axis_index("token")
    x = lax.axis_index("tensor") % SIDE
    rows = tokens.shape[0]
    qblk = 2 * rows
    block_rows = rows * SIDE * SIDE
    outer = (x == 0) | (x == SIDE - 1)
    lows, highs = jnp.where(outer, 0, 1), jnp.where(outer, SIDE - 1, SIDE - 2)
    runs = token_index * block_rows + jnp.arange(SIDE, dtype=jnp.int32) * (SIDE * rows)
    blocks = runs[:, None] + jnp.stack([lows, highs])[None, :] * rows
    spots = (blocks[:, :, None] + jnp.arange(rows, dtype=jnp.int32)).reshape(-1).astype(jnp.int32)
    ends = jnp.cumsum(doc_lengths)
    passed = spots[:, None] >= ends[None, :-1]
    first = jnp.max(jnp.where(passed, ends[None, :-1], 0), axis=1).astype(jnp.int32)
    position = (spots - first).astype(jnp.float32)
    half = HEAD_DIM // 2
    freq = jnp.exp(-math.log(ROPE_BASE) * jnp.arange(half, dtype=jnp.float32) * (2.0 / HEAD_DIM))
    angle = position[:, None] * freq[None, :]
    cosine, sine = jnp.cos(angle), jnp.sin(angle)
    cosine = jnp.concatenate([cosine, cosine], axis=1).reshape(SIDE, 2, rows, HEAD_DIM)
    sine = jnp.concatenate([-sine, sine], axis=1).reshape(SIDE, 2, rows, HEAD_DIM)
    queries, own, w_out_other = project(tokens, attn_gain[None, :], cosine, sine, w_query, w_keyval, w_out)
    queries = queries.reshape(SIDE * qblk, -1)
    count = SIDE * SIDE
    other = lax.ppermute(own, "tensor", [(i, i ^ 1) for i in range(count)])
    wide, narrow = jnp.where(outer, own, other), jnp.where(outer, other, own)
    both = jnp.stack([wide[:, :, 0], narrow[:, :, 0], narrow[:, :, 1], wide[:, :, 1]], axis=2)
    both = both.reshape(2, block_rows, HEAD_DIM)
    both = lax.all_gather(both, "token", axis=1, tiled=True)
    low = first[::qblk] // KBLK
    high = spots[qblk - 1 :: qblk] // KBLK + 1
    clear_low = jnp.minimum((first[qblk - 1 :: qblk] + KBLK - 1) // KBLK, high)
    clear_high = jnp.maximum(spots[::qblk] // KBLK, clear_low)
    bounds = jnp.stack([low, high, clear_low, clear_high]).astype(jnp.int32)
    attn = attend(queries, both[0], both[1], first[:, None], spots[:, None], bounds, qblk)
    attn = attn.reshape(SIDE, 2, rows, attn.shape[1])
    return finish(tokens, attn, mlp_gain[None, :], w_out, w_out_other, w_gate.T, w_up.T, w_down)


def solution(mesh):
    return jax.shard_map(
        body,
        mesh=mesh,
        in_specs=(
            P(("token", "tensor"), None),
            P(),
            P(),
            P(),
            P(None, "tensor"),
            P(None, "tensor"),
            P("tensor", None),
            P(None, "tensor"),
            P(None, "tensor"),
            P("tensor", None),
        ),
        out_specs=P(("token", "tensor"), None),
        check_vma=False,
    )
```

```python
import functools
import math

import jax
import jax.numpy as jnp
from jax import lax
from jax.experimental import pallas as pl
from jax.experimental.pallas import tpu as pltpu
from jax.sharding import PartitionSpec as P

HEAD_DIM = 128
SIDE = 4
CORES = 2
YS = 4

EPSILON = 1e-05
ROPE_BASE = 500000.0
NEGATIVE = -1e30
MESH = pl.DeviceIdType.MESH


def place():
    me, token = lax.axis_index("tensor"), lax.axis_index("token")
    return me // SIDE, me % SIDE, token // CORES, token % CORES


def along_z(step):
    z, x, _, _ = place()
    return {"tensor": ((z + step + SIDE) % SIDE) * SIDE + x}


def mate():
    z, x, _, _ = place()
    return {"tensor": z * SIDE + SIDE - 1 - x}


def holder():
    z, x, _, _ = place()
    return {"tensor": z * SIDE + x + 1 - 2 * (x % 2)}


def along_y(step):
    _, _, y, core = place()
    return {"token": ((y + step + YS) % YS) * CORES + core}


def twin():
    _, _, y, core = place()
    return {"token": y * CORES + 1 - core}


def greet():
    barrier = pltpu.get_barrier_semaphore()
    others = [along_z(1), along_z(-1), mate(), holder(), along_y(1), along_y(-1), twin()]
    for other in others:
        pl.semaphore_signal(barrier, inc=1, device_id=other, device_id_type=MESH)
    pl.semaphore_wait(barrier, len(others))


class Wires:
    def __init__(self, send_sems, recv_sems):
        self.send_sems, self.recv_sems, self.slots, self.started = send_sems, recv_sems, {}, []

    def copy(self, key, src, dst, device):
        slot = self.slots.setdefault(key, len(self.slots))
        return pltpu.make_async_remote_copy(
            src_ref=src,
            dst_ref=dst,
            send_sem=self.send_sems.at[slot],
            recv_sem=self.recv_sems.at[slot],
            device_id=device,
            device_id_type=MESH,
        )

    def start(self, key, src, dst, device):
        made = self.copy(key, src, dst, device)
        made.start()
        self.started.append(made)

    def arrive(self, key, dst, device):
        self.copy(key, dst, dst, device).wait_recv()

    def drain(self):
        for made in self.started:
            made.wait_send()
        self.started = []


class Fetch:
    def __init__(self, wires, name, src, dst, lanes, first_lane=0):
        self.wires, self.name, self.src, self.dst, self.lanes, self.first_lane = wires, name, src, dst, lanes, first_lane
        self.size = src.shape[1 if lanes else 0] // (YS * CORES)

    def cut(self, ref, number, part, offset):
        size = self.size if part is None else self.size // 2
        start = pl.multiple_of(number * self.size, self.size) + (0 if part in (None, 0) else size)
        start = pl.multiple_of(start, size)
        if self.lanes:
            return ref.at[:, pl.ds(start, size)]
        return ref.at[pl.ds(start, size), pl.ds(offset, self.src.shape[1])]

    def slot(self, dy, dc, part=None):
        _, _, y, core = place()
        number = ((y + dy + YS) % YS) * CORES + (core if dc == 0 else 1 - core)
        return self.cut(self.dst, number, part, self.first_lane)

    def start(self, key, ref, device):
        self.wires.start((self.name, key), ref, ref, device)

    def arrive(self, key, ref):
        self.wires.arrive((self.name, key), ref, holder())

    def ask(self):
        _, _, y, core = place()
        self.wires.start((self.name, "x"), self.cut(self.src, y * CORES + core, None, 0), self.slot(0, 0), holder())

    def relay(self):
        self.arrive("x", self.slot(0, 0))
        self.start("y3", self.slot(0, 0), along_y(1))
        self.start("y1", self.slot(0, 0), along_y(-1))
        self.start("c0", self.slot(0, 0), twin())

    def pass_on(self):
        self.arrive("y3", self.slot(3, 0))
        self.start("h0", self.slot(3, 0, 0), along_y(1))
        self.start("c3", self.slot(3, 0), twin())
        self.arrive("y1", self.slot(1, 0))
        self.start("h1", self.slot(1, 0, 1), along_y(-1))
        self.start("c1", self.slot(1, 0), twin())

    def settle(self):
        self.arrive("h0", self.slot(2, 0, 0))
        self.arrive("h1", self.slot(2, 0, 1))
        self.start("c2", self.slot(2, 0), twin())

    def finish(self):
        for dy in (0, 3, 1, 2):
            self.arrive("c%d" % dy, self.slot(dy, 1))


def gather(wires, blocks, hook):
    rows = blocks.shape[3]
    low, high = pl.ds(0, rows // 2), pl.ds(rows // 2, rows // 2)
    up, down = 1, -1

    def full(h, dz, m):
        return blocks.at[h, dz, m]

    def spread(h, m):
        wires.start(("s", h, 3, m), full(h, 0, m), full(h, 3, m), along_z(up))
        wires.start(("s", h, 1, m), full(h, 0, m), full(h, 1, m), along_z(down))

    def to_mate(h, dz):
        wires.start(("m", h, dz), full(h, dz, 0), full(h, dz, 1), mate())

    def relay(h, m, onward):
        wires.arrive(("s", h, 3, m), full(h, 3, m), along_z(down))
        wires.start(("t", h, 0, m), blocks.at[h, 3, m, low], blocks.at[h, 2, m, low], along_z(up))
        if onward:
            to_mate(h, 3)
        wires.arrive(("s", h, 1, m), full(h, 1, m), along_z(up))
        wires.start(("t", h, 1, m), blocks.at[h, 1, m, high], blocks.at[h, 2, m, high], along_z(down))
        if onward:
            to_mate(h, 1)

    def last(h, m):
        wires.arrive(("t", h, 0, m), blocks.at[h, 2, m, low], along_z(down))
        wires.arrive(("t", h, 1, m), blocks.at[h, 2, m, high], along_z(up))

    to_mate(0, 0)
    spread(1, 0)
    spread(0, 0)
    to_mate(1, 0)
    hook("sent")
    wires.arrive(("m", 0, 0), full(0, 0, 1), mate())
    spread(0, 1)
    relay(1, 0, True)
    relay(0, 0, False)
    hook("early")
    wires.arrive(("m", 1, 0), full(1, 0, 1), mate())
    hook("own pair")
    last(1, 0)
    to_mate(1, 2)
    relay(0, 1, False)
    hook("middle")
    wires.arrive(("m", 1, 3), full(1, 3, 1), mate())
    wires.arrive(("m", 1, 1), full(1, 1, 1), mate())
    hook("sides")
    last(0, 0)
    last(0, 1)
    wires.arrive(("m", 1, 2), full(1, 2, 1), mate())
    hook("far")


def scatter(wires, out, bufs, produce, hook):
    z_half, z_full, mate0, mate1, e_half, e_full = bufs
    rows = out.shape[3]
    low, high = pl.ds(0, rows // 2), pl.ds(rows // 2, rows // 2)
    ways = ((0, 1, low, 1), (1, 3, high, -1))
    f32 = jnp.float32

    def wide(ref):
        return ref[...].astype(f32)

    def add_to(ref, *others):
        total = wide(ref)
        for other in others:
            total = total + wide(other)
        ref[...] = total.astype(ref.dtype)

    def mate_send(dz):
        wires.start(("m1", dz), out.at[1, dz, 1], mate1.at[dz], mate())

    def mate_join(dz):
        wires.arrive(("m1", dz), mate1.at[dz], mate())
        add_to(out.at[1, dz, 0], mate1.at[dz])

    produce(1, (2,))
    mate_send(2)
    produce(0, (2,))
    for m in (1, 0):
        for way, dz, part, step in ways:
            wires.start(("a", way, m), out.at[0, 2, m, part], z_half.at[way, m], along_z(step))
    produce(0, (1, 3))
    produce(1, (1, 3))
    mate_send(1)
    mate_send(3)
    mate_join(2)
    for way, dz, part, step in ways:
        wires.start(("e", way), out.at[1, 2, 0, part], e_half.at[way], along_z(step))
    for m in (1, 0):
        for way, dz, part, step in ways:
            wires.arrive(("a", way, m), z_half.at[way, m], along_z(-step))
            add_to(out.at[0, dz, m, part], z_half.at[way, m])
            wires.start(("b", way, m), out.at[0, dz, m], z_full.at[way, m], along_z(step))
    produce(1, (0,))
    mate_send(0)
    produce(0, (0,))
    hook("early")
    for way, dz, part, step in ways:
        mate_join(dz)
        wires.arrive(("e", way), e_half.at[way], along_z(-step))
        add_to(out.at[1, dz, 0, part], e_half.at[way])
        wires.start(("f", way), out.at[1, dz, 0], e_full.at[way], along_z(step))
    hook("middle")
    for way, dz, part, step in ways:
        wires.arrive(("b", way, 1), z_full.at[way, 1], along_z(-step))
    add_to(out.at[0, 0, 1], z_full.at[0, 1], z_full.at[1, 1])
    wires.start(("m0",), out.at[0, 0, 1], mate0, mate())
    hook("late")
    for way, dz, part, step in ways:
        wires.arrive(("b", way, 0), z_full.at[way, 0], along_z(-step))
    first = wide(out.at[0, 0, 0]) + wide(z_full.at[0, 0]) + wide(z_full.at[1, 0])
    wires.arrive(("m1", 0), mate1.at[0], mate())
    second = wide(out.at[1, 0, 0]) + wide(mate1.at[0])
    for way, dz, part, step in ways:
        wires.arrive(("f", way), e_full.at[way], along_z(-step))
        second = second + wide(e_full.at[way])
    wires.arrive(("m0",), mate0, mate())
    first = first + wide(mate0)
    return first, second


def norm_halves(rows, gain, width):
    mean_square = jnp.mean(rows * rows, axis=-1, keepdims=True)
    normed = (rows * lax.rsqrt(mean_square + EPSILON) * gain).astype(jnp.bfloat16)
    return normed[:, :width], normed[:, width:]


def stacked(blocks, h, dzs):
    rows, width = blocks.shape[3], blocks.shape[4]
    parts = [blocks[h, dz].reshape(2 * rows, width) for dz in dzs]
    return parts[0] if len(parts) == 1 else jnp.concatenate(parts, axis=0)


def project_kernel(
    tokens_ref, gain_ref, cos_ref, sin_ref, wq_hbm, wkv_hbm, wo_hbm, q_ref, kv_ref, wo_other,
    weights, others, blocks, load_sems, send_sems, recv_sems,
):
    rows, half_width = blocks.shape[3], blocks.shape[4]
    qcols = wq_hbm.shape[1]
    cols = qcols + wkv_hbm.shape[1]
    z, x, _, _ = place()
    loads = [
        pltpu.make_async_copy(wq_hbm, weights.at[:, pl.ds(0, qcols)], load_sems.at[0]),
        pltpu.make_async_copy(wkv_hbm, weights.at[:, pl.ds(qcols, cols - qcols)], load_sems.at[1]),
    ]
    for load in loads:
        load.start()
    first, second = norm_halves(tokens_ref[...].astype(jnp.float32), gain_ref[...], half_width)
    blocks[0, 0, 0] = first
    blocks[1, 0, 0] = second
    greet()
    wires = Wires(send_sems, recv_sems)
    fetch_q = Fetch(wires, "q", wq_hbm, others, False, 0)
    fetch_kv = Fetch(wires, "kv", wkv_hbm, others, False, qcols)
    fetch_o = Fetch(wires, "o", wo_hbm, wo_other, True)

    def emit(dzs, mine):
        shard = weights if mine else others
        part = sum(
            jnp.dot(
                stacked(blocks, h, dzs),
                shard[h * half_width : (h + 1) * half_width, :],
                preferred_element_type=jnp.float32,
            )
            for h in range(2)
        )
        is_key = (x % 2 == 0) if mine else (x % 2 == 1)
        which = x % 2 if mine else 1 - x % 2
        first_col = 0 if mine else qcols
        for i, dz in enumerate(dzs):
            for m in range(2):
                whole = part[(2 * i + m) * rows : (2 * i + m + 1) * rows]
                zz = (z + dz) % SIDE
                mm = x // 2 if m == 0 else 1 - x // 2
                cosine, sine = cos_ref[zz, mm], sin_ref[zz, mm]
                for head in range(qcols // HEAD_DIM):
                    piece = whole[:, head * HEAD_DIM : (head + 1) * HEAD_DIM]
                    turned = piece * cosine + pltpu.roll(piece, HEAD_DIM // 2, 1) * sine
                    at = first_col + head * HEAD_DIM
                    q_ref[zz, mm, :, at : at + HEAD_DIM] = turned.astype(jnp.bfloat16)
                piece = whole[:, qcols:]
                turned = piece * cosine + pltpu.roll(piece, HEAD_DIM // 2, 1) * sine
                kv_ref[which, zz, mm] = jnp.where(is_key, turned, piece).astype(jnp.bfloat16)

    def hook(name):
        if name == "sent":
            for fetch in (fetch_q, fetch_kv, fetch_o):
                fetch.ask()
        elif name == "early":
            fetch_q.relay()
            fetch_kv.relay()
            for load in loads:
                load.wait()
        elif name == "own pair":
            emit((0,), True)
        elif name == "middle":
            fetch_q.pass_on()
            fetch_kv.pass_on()
            fetch_o.relay()
        elif name == "sides":
            emit((3, 1), True)
            fetch_q.settle()
            fetch_kv.settle()
            fetch_q.finish()
            fetch_kv.finish()
            emit((0,), False)
            emit((3, 1), False)
            fetch_o.pass_on()
        else:
            emit((2,), True)
            emit((2,), False)
            fetch_o.settle()
            fetch_o.finish()

    gather(wires, blocks, hook)
    wires.drain()


def project(tokens, gain, cosine, sine, w_query, w_keyval, w_out):
    rows, width = tokens.shape
    cols = w_query.shape[1] + w_keyval.shape[1]
    vmem = pl.BlockSpec(memory_space=pltpu.VMEM)
    hbm = pl.BlockSpec(memory_space=pl.ANY)
    bf16 = jnp.bfloat16
    return pl.pallas_call(
        project_kernel,
        out_shape=(
            jax.ShapeDtypeStruct((SIDE, 2, rows, 2 * w_query.shape[1]), bf16),
            jax.ShapeDtypeStruct((2, SIDE, 2, rows, w_keyval.shape[1]), bf16),
            jax.ShapeDtypeStruct(w_out.shape, bf16),
        ),
        in_specs=[vmem] * 4 + [hbm] * 3,
        out_specs=(vmem, vmem, hbm),
        scratch_shapes=[
            pltpu.VMEM((width, cols), bf16),
            pltpu.VMEM((width, cols), bf16),
            pltpu.VMEM((2, SIDE, 2, rows, width // 2), bf16),
            pltpu.SemaphoreType.DMA((2,)),
            pltpu.SemaphoreType.DMA((64,)),
            pltpu.SemaphoreType.DMA((64,)),
        ],
        compiler_params=pltpu.CompilerParams(
            collective_id=0, has_side_effects=True, vmem_limit_bytes=48 << 20
        ),
        name="project",
    )(tokens, gain, cosine, sine, w_query, w_keyval, w_out)


def finish_kernel(
    tokens_ref, attn_ref, gain_ref, wo_hbm, wo2_hbm, wg_hbm, wu_hbm, wd_hbm, out_ref,
    wo, wg, wu, wd, wg2, wu2, wd2, blocks, hidden, hidden2, sending,
    z_half, z_full, mate0, mate1, e_half, e_full, state, load_sems, send_sems, recv_sems,
):
    rows, half_width = blocks.shape[3], blocks.shape[4]
    own = wo_hbm.shape[0]
    z, x, _, _ = place()
    loads = [
        pltpu.make_async_copy(src, dst, load_sems.at[i])
        for i, (src, dst) in enumerate(
            ((wo_hbm, wo.at[pl.ds(0, own)]), (wo2_hbm, wo.at[pl.ds(own, own)]), (wg_hbm, wg), (wu_hbm, wu), (wd_hbm, wd))
        )
    ]
    for load in loads:
        load.start()
    greet()
    bufs = (z_half, z_full, mate0, mate1, e_half, e_full)
    weight_wires = Wires(send_sems.at[3], recv_sems.at[3])
    fetch_g = Fetch(weight_wires, "g", wg_hbm, wg2, True)
    fetch_u = Fetch(weight_wires, "u", wu_hbm, wu2, True)
    fetch_d = Fetch(weight_wires, "d", wd_hbm, wd2, True)
    fetch_g.ask()
    fetch_u.ask()
    loads[0].wait()
    loads[1].wait()

    def columns(h):
        return pl.ds(h * half_width, half_width)

    def keep(h, dzs, part):
        for i, dz in enumerate(dzs):
            piece = part[2 * i * rows : 2 * (i + 1) * rows].astype(jnp.bfloat16)
            sending[h, dz] = piece.reshape(2, rows, half_width)

    def project_out(h, dzs):
        mine, other = x // 2, 1 - x // 2
        left = [attn_ref[(z + dz) % SIDE, m] for dz in dzs for m in (mine, other)]
        left = jnp.concatenate(left, axis=0)
        keep(h, dzs, jnp.dot(left, wo[:, columns(h)], preferred_element_type=jnp.float32))

    def hook_out(name):
        if name == "early":
            fetch_g.relay()
        elif name == "middle":
            fetch_g.pass_on()
        else:
            fetch_u.relay()

    out_wires = Wires(send_sems.at[0], recv_sems.at[0])
    first, second = scatter(out_wires, sending, bufs, project_out, hook_out)
    for h, proj in enumerate((first, second)):
        state[:, columns(h)] = (tokens_ref[:, columns(h)].astype(jnp.float32) + proj).astype(jnp.bfloat16)
    first, second = norm_halves(state[...].astype(jnp.float32), gain_ref[...], half_width)
    blocks[0, 0, 0] = first
    blocks[1, 0, 0] = second

    def gated(dzs, mine):
        gates, ups, result = (wg, wu, hidden) if mine else (wg2, wu2, hidden2)
        gate = upward = 0.0
        for h in range(2):
            left = stacked(blocks, h, dzs)
            across = (((1,), (1,)), ((), ()))
            gate = gate + lax.dot_general(left, gates[:, columns(h)], across, preferred_element_type=jnp.float32)
            upward = upward + lax.dot_general(left, ups[:, columns(h)], across, preferred_element_type=jnp.float32)
        value = (gate / (1.0 + jnp.exp(-gate)) * upward).astype(jnp.bfloat16)
        for i, dz in enumerate(dzs):
            result[dz] = value[2 * i * rows : 2 * (i + 1) * rows].reshape(2, rows, value.shape[1])

    def hook_gated(name):
        if name == "sent":
            fetch_d.ask()
            fetch_g.settle()
            loads[2].wait()
            loads[3].wait()
        elif name == "early":
            fetch_u.pass_on()
            fetch_g.finish()
        elif name == "own pair":
            gated((0,), True)
            fetch_d.relay()
        elif name == "middle":
            fetch_u.settle()
        elif name == "sides":
            gated((3, 1), True)
            fetch_u.finish()
            gated((0,), False)
            gated((3, 1), False)
            fetch_d.pass_on()
        else:
            gated((2,), True)
            gated((2,), False)
            fetch_d.settle()
            fetch_d.finish()
            loads[4].wait()

    gather_wires = Wires(send_sems.at[1], recv_sems.at[1])
    gather(gather_wires, blocks, hook_gated)
    out_wires.drain()

    def project_down(h, dzs):
        part = 0.0
        for values, weights in ((hidden, wd), (hidden2, wd2)):
            left = [values[dz].reshape(2 * rows, values.shape[3]) for dz in dzs]
            left = left[0] if len(left) == 1 else jnp.concatenate(left, axis=0)
            part = part + jnp.dot(left, weights[:, columns(h)], preferred_element_type=jnp.float32)
        keep(h, dzs, part)

    down_wires = Wires(send_sems.at[2], recv_sems.at[2])
    down = scatter(down_wires, sending, bufs, project_down, lambda name: None)
    for h in range(2):
        out_ref[:, columns(h)] = (state[:, columns(h)].astype(jnp.float32) + down[h]).astype(jnp.bfloat16)
    for wires in (gather_wires, down_wires, weight_wires):
        wires.drain()


def finish(tokens, attn, gain, w_out, w_out_other, w_gate, w_up, w_down):
    rows, width = tokens.shape
    hidden = w_gate.shape[0]
    vmem = pl.BlockSpec(memory_space=pltpu.VMEM)
    hbm = pl.BlockSpec(memory_space=pl.ANY)
    half = width // 2
    bf16 = jnp.bfloat16
    return pl.pallas_call(
        finish_kernel,
        out_shape=jax.ShapeDtypeStruct((rows, width), bf16),
        in_specs=[vmem] * 3 + [hbm] * 5,
        out_specs=vmem,
        scratch_shapes=[
            pltpu.VMEM((2 * w_out.shape[0], width), bf16),
            *[pltpu.VMEM((hidden, width), bf16)] * 6,
            pltpu.VMEM((2, SIDE, 2, rows, half), bf16),
            pltpu.VMEM((SIDE, 2, rows, hidden), bf16),
            pltpu.VMEM((SIDE, 2, rows, hidden), bf16),
            pltpu.VMEM((2, SIDE, 2, rows, half), bf16),
            pltpu.VMEM((2, 2, rows // 2, half), bf16),
            pltpu.VMEM((2, 2, rows, half), bf16),
            pltpu.VMEM((rows, half), bf16),
            pltpu.VMEM((SIDE, rows, half), bf16),
            pltpu.VMEM((2, rows // 2, half), bf16),
            pltpu.VMEM((2, rows, half), bf16),
            pltpu.VMEM((rows, width), bf16),
            pltpu.SemaphoreType.DMA((5,)),
            pltpu.SemaphoreType.DMA((4, 48)),
            pltpu.SemaphoreType.DMA((4, 48)),
        ],
        compiler_params=pltpu.CompilerParams(
            collective_id=1, has_side_effects=True, vmem_limit_bytes=60 << 20
        ),
        name="finish",
    )(tokens, attn, gain, w_out, w_out_other, w_gate, w_up, w_down)


def serve_kernel(q_ref, own_ref, first_ref, spot_ref, o_ref, held, peak, total, summed, send_sems, recv_sems):
    z, x, y, core = place()
    mine = lax.rem(lax.div(x + 1, 2), 2)
    theirs = 1 - mine
    base = 1 - core
    rows = q_ref.shape[2]
    width = own_ref.shape[4]
    heads = q_ref.shape[3] // width
    count = heads * 2 * rows
    keys_here = SIDE * 2 * rows
    factor = math.log2(math.e) / math.sqrt(width)
    across, ahead, other_core = holder(), along_y(1), twin()
    greet()
    started = []

    def send(g, c, target, device):
        made = pltpu.make_async_remote_copy(
            src_ref=held.at[g, c],
            dst_ref=held.at[target, c],
            send_sem=send_sems.at[len(started)],
            recv_sem=recv_sems.at[target, c],
            device_id=device,
            device_id_type=MESH,
        )
        made.start()
        started.append(True)

    def arrive(g, c):
        pltpu.make_async_remote_copy(
            src_ref=held.at[g, c],
            dst_ref=held.at[g, c],
            send_sem=send_sems.at[0],
            recv_sem=recv_sems.at[g, c],
            device_id=across,
            device_id_type=MESH,
        ).wait_recv()

    held[base, mine] = own_ref[...]
    send(base, mine, base, across)
    send(base, mine, base + 2, ahead)
    send(base, mine, base, other_core)
    peak[...] = jnp.full(peak.shape, NEGATIVE, jnp.float32)
    total[...] = jnp.zeros(total.shape, jnp.float32)
    summed[...] = jnp.zeros(summed.shape, jnp.float32)

    def column(ref, zz):
        return jnp.concatenate([ref[zz]] * heads, axis=0)

    def step(zz, g, c, back, begin, size, causal):
        run = 2 * rows
        tile = [q_ref[zz, :, :, h * width : (h + 1) * width].reshape(run, width) for h in range(heads)]
        query = jnp.concatenate(tile, axis=0)
        keys = held[g, c, 0, begin : begin + size].reshape(size * run, width)
        values = held[g, c, 1, begin : begin + size].reshape(size * run, width)
        scores = lax.dot_general(query, keys, (((1,), (1,)), ((), ())), preferred_element_type=jnp.float32) * factor
        number = lax.broadcasted_iota(jnp.int32, (1, size * run), 1)
        in_run = lax.rem(number, jnp.full_like(number, run))
        later = (in_run >= rows).astype(jnp.int32)
        at_x = c + later * (SIDE - 1 - 2 * c)
        spots = (number - in_run) * 2 + begin * (SIDE * rows) + (at_x - later) * rows + in_run
        spots = spots + ((2 * y + core) - back) * (SIDE * SIDE * rows)
        seen = spots >= column(first_ref, zz)
        if causal:
            seen = seen & (spots <= column(spot_ref, zz))
        scores = jnp.where(seen, scores, NEGATIVE)
        old = peak[zz]
        new = jnp.maximum(old, jnp.max(scores, axis=1, keepdims=True))
        decay = jnp.exp2(old - new)
        weights = jnp.exp2(scores - new)
        peak[zz] = new
        total[zz] = total[zz] * decay + jnp.sum(weights, axis=1, keepdims=True)
        summed[zz] = summed[zz] * decay + jnp.dot(
            weights.astype(jnp.bfloat16), values, preferred_element_type=jnp.float32
        )

    def own_block(c):
        for zz in range(SIDE):
            step(zz, base, c, 0, 0, zz + 1, True)

    def far_block(c):
        for zz in range(SIDE):
            step(zz, base + 4, c, 4, zz, SIDE - zz, False)

    def per_class(work):
        def one(i, carry):
            work(mine + i * (theirs - mine))
            return carry

        return one

    def first_class(i, carry):
        @pl.when(i == 1)
        def _():
            arrive(base, theirs)
            send(base, theirs, base, other_core)
            arrive(base + 2, mine)
            send(base + 2, mine, base + 4, ahead)
            send(base + 2, mine, base + 2, across)
            send(base + 2, mine, base + 2, other_core)

        own_block(mine + i * (theirs - mine))
        return carry

    lax.fori_loop(0, 2, first_class, 0)

    def middle(stage, carry):
        back = lax.div(stage, 2) + 1

        @pl.when(stage == 1)
        def _():
            arrive(base + 2, theirs)
            send(base + 2, theirs, base + 2, other_core)

        @pl.when(stage == 3)
        def _():
            arrive(base + 4, mine)
            send(base + 4, mine, base + 4, across)
            send(base + 4, mine, base + 4, other_core)

        @pl.when(stage == 5)
        def _():
            arrive(base + 4, theirs)
            send(base + 4, theirs, base + 4, other_core)

        c = mine + lax.rem(stage, 2) * (theirs - mine)

        @pl.when(back != 2)
        def _():
            arrive(base + back, c)

        def over_runs(zz, inner):
            step(zz, base + back, c, back, 0, SIDE, False)
            return inner

        return lax.fori_loop(0, SIDE, over_runs, carry)

    lax.fori_loop(0, 6, middle, 0)
    lax.fori_loop(0, 2, per_class(far_block), 0)
    spare = core * 5
    arrive(spare, 0)
    arrive(spare, 1)
    for zz in range(SIDE):
        answer = (summed[zz] / total[zz]).astype(jnp.bfloat16)
        for h in range(heads):
            piece = answer[h * 2 * rows : (h + 1) * 2 * rows]
            o_ref[zz, :, :, h * width : (h + 1) * width] = piece.reshape(2, rows, width)
    for number in range(len(started)):
        pltpu.make_async_remote_copy(
            src_ref=held.at[0, 0],
            dst_ref=held.at[0, 0],
            send_sem=send_sems.at[number],
            recv_sem=recv_sems.at[0, 0],
            device_id=across,
            device_id_type=MESH,
        ).wait_send()


def serve(queries, own, first, spots):
    rows = queries.shape[2]
    width = own.shape[4]
    heads = queries.shape[3] // width
    tall = heads * 2 * rows
    vmem = pl.BlockSpec(memory_space=pltpu.VMEM)
    return pl.pallas_call(
        serve_kernel,
        out_shape=jax.ShapeDtypeStruct(queries.shape, jnp.bfloat16),
        in_specs=[vmem] * 4,
        out_specs=vmem,
        scratch_shapes=[
            pltpu.VMEM((6, 2, *own.shape), jnp.bfloat16),
            pltpu.VMEM((SIDE, tall, 1), jnp.float32),
            pltpu.VMEM((SIDE, tall, 1), jnp.float32),
            pltpu.VMEM((SIDE, tall, width), jnp.float32),
            pltpu.SemaphoreType.DMA((11,)),
            pltpu.SemaphoreType.DMA((6, 2)),
        ],
        compiler_params=pltpu.CompilerParams(
            collective_id=2, has_side_effects=True, vmem_limit_bytes=40 << 20
        ),
        name="serve",
    )(queries, own, first, spots)


def body(tokens, doc_lengths, attn_gain, mlp_gain, w_query, w_keyval, w_out, w_gate, w_up, w_down):
    token_index = lax.axis_index("token")
    x = lax.axis_index("tensor") % SIDE
    rows = tokens.shape[0]
    qblk = 2 * rows
    block_rows = rows * SIDE * SIDE
    outer = (x == 0) | (x == SIDE - 1)
    lows, highs = jnp.where(outer, 0, 1), jnp.where(outer, SIDE - 1, SIDE - 2)
    runs = token_index * block_rows + jnp.arange(SIDE, dtype=jnp.int32) * (SIDE * rows)
    blocks = runs[:, None] + jnp.stack([lows, highs])[None, :] * rows
    spots = (blocks[:, :, None] + jnp.arange(rows, dtype=jnp.int32)).reshape(-1).astype(jnp.int32)
    ends = jnp.cumsum(doc_lengths)
    passed = spots[:, None] >= ends[None, :-1]
    first = jnp.max(jnp.where(passed, ends[None, :-1], 0), axis=1).astype(jnp.int32)
    position = (spots - first).astype(jnp.float32)
    half = HEAD_DIM // 2
    freq = jnp.exp(-math.log(ROPE_BASE) * jnp.arange(half, dtype=jnp.float32) * (2.0 / HEAD_DIM))
    angle = position[:, None] * freq[None, :]
    cosine, sine = jnp.cos(angle), jnp.sin(angle)
    cosine = jnp.concatenate([cosine, cosine], axis=1).reshape(SIDE, 2, rows, HEAD_DIM)
    sine = jnp.concatenate([-sine, sine], axis=1).reshape(SIDE, 2, rows, HEAD_DIM)
    queries, own, w_out_other = project(tokens, attn_gain[None, :], cosine, sine, w_query, w_keyval, w_out)
    attn = serve(queries, own, first.reshape(SIDE, qblk, 1), spots.reshape(SIDE, qblk, 1))
    return finish(tokens, attn, mlp_gain[None, :], w_out, w_out_other, w_gate.T, w_up.T, w_down)


def solution(mesh):
    return jax.shard_map(
        body,
        mesh=mesh,
        in_specs=(
            P(("token", "tensor"), None),
            P(),
            P(),
            P(),
            P(None, "tensor"),
            P(None, "tensor"),
            P("tensor", None),
            P(None, "tensor"),
            P(None, "tensor"),
            P("tensor", None),
        ),
        out_specs=P(("token", "tensor"), None),
        check_vma=False,
    )
```

```python
import functools
import math

import jax
import jax.numpy as jnp
from jax import lax
from jax.experimental import pallas as pl
from jax.experimental.pallas import tpu as pltpu
from jax.sharding import PartitionSpec as P

HEAD_DIM = 128
SIDE = 4
CORES = 2
YS = 4

EPSILON = 1e-05
ROPE_BASE = 500000.0
NEGATIVE = -1e30
MESH = pl.DeviceIdType.MESH


def place():
    me, token = lax.axis_index("tensor"), lax.axis_index("token")
    return me // SIDE, me % SIDE, token // CORES, token % CORES


def along_z(step):
    z, x, _, _ = place()
    return {"tensor": ((z + step + SIDE) % SIDE) * SIDE + x}


def mate():
    z, x, _, _ = place()
    return {"tensor": z * SIDE + SIDE - 1 - x}


def holder():
    z, x, _, _ = place()
    return {"tensor": z * SIDE + x + 1 - 2 * (x % 2)}


def along_y(step):
    _, _, y, core = place()
    return {"token": ((y + step + YS) % YS) * CORES + core}


def twin():
    _, _, y, core = place()
    return {"token": y * CORES + 1 - core}


def greet():
    others = [along_z(1), along_z(-1), mate(), holder(), along_y(1), along_y(-1), twin()]
    for other in others:
        pl.semaphore_signal(pltpu.get_barrier_semaphore(), inc=1, device_id=other, device_id_type=MESH)
    return len(others)


def meet(others):
    pl.semaphore_wait(pltpu.get_barrier_semaphore(), others)


def column_halves(width):
    first = width * 9 // 16
    return first, width - first


class Wires:
    def __init__(self, send_sems, recv_sems):
        self.send_sems, self.recv_sems, self.slots, self.started = send_sems, recv_sems, {}, []

    def copy(self, key, src, dst, device):
        slot = self.slots.setdefault(key, len(self.slots))
        return pltpu.make_async_remote_copy(
            src_ref=src,
            dst_ref=dst,
            send_sem=self.send_sems.at[slot],
            recv_sem=self.recv_sems.at[slot],
            device_id=device,
            device_id_type=MESH,
        )

    def start(self, key, src, dst, device):
        made = self.copy(key, src, dst, device)
        made.start()
        self.started.append(made)

    def arrive(self, key, dst, device):
        self.copy(key, dst, dst, device).wait_recv()

    def drain(self):
        for made in self.started:
            made.wait_send()
        self.started = []


class Fetch:
    def __init__(self, wires, name, src, dst, lanes, first_lane=0):
        self.wires, self.name, self.src, self.dst, self.lanes, self.first_lane = wires, name, src, dst, lanes, first_lane
        self.size = src.shape[1 if lanes else 0] // (YS * CORES)

    def cut(self, ref, number, part, offset):
        size = self.size if part is None else self.size // 2
        start = pl.multiple_of(number * self.size, self.size) + (0 if part in (None, 0) else size)
        start = pl.multiple_of(start, size)
        if self.lanes:
            return ref.at[:, pl.ds(start, size)]
        return ref.at[pl.ds(start, size), pl.ds(offset, self.src.shape[1])]

    def slot(self, dy, dc, part=None):
        _, _, y, core = place()
        number = ((y + dy + YS) % YS) * CORES + (core if dc == 0 else 1 - core)
        return self.cut(self.dst, number, part, self.first_lane)

    def start(self, key, ref, device):
        self.wires.start((self.name, key), ref, ref, device)

    def arrive(self, key, ref):
        self.wires.arrive((self.name, key), ref, holder())

    def ask(self):
        _, _, y, core = place()
        self.wires.start((self.name, "x"), self.cut(self.src, y * CORES + core, None, 0), self.slot(0, 0), holder())

    def relay(self):
        self.arrive("x", self.slot(0, 0))
        self.start("y3", self.slot(0, 0), along_y(1))
        self.start("y1", self.slot(0, 0), along_y(-1))
        self.start("c0", self.slot(0, 0), twin())

    def pass_on(self):
        self.arrive("y3", self.slot(3, 0))
        self.start("h0", self.slot(3, 0, 0), along_y(1))
        self.start("c3", self.slot(3, 0), twin())
        self.arrive("y1", self.slot(1, 0))
        self.start("h1", self.slot(1, 0, 1), along_y(-1))
        self.start("c1", self.slot(1, 0), twin())

    def settle(self):
        self.arrive("h0", self.slot(2, 0, 0))
        self.arrive("h1", self.slot(2, 0, 1))
        self.start("c2", self.slot(2, 0), twin())

    def finish(self):
        for dy in (0, 3, 1, 2):
            self.arrive("c%d" % dy, self.slot(dy, 1))


def gather(wires, blocks, hook):
    rows = blocks[0].shape[2]
    low, high = pl.ds(0, rows // 2), pl.ds(rows // 2, rows // 2)
    up, down = 1, -1

    def full(h, dz, m):
        return blocks[h].at[dz, m]

    def spread(h, m):
        wires.start(("s", h, 3, m), full(h, 0, m), full(h, 3, m), along_z(up))
        wires.start(("s", h, 1, m), full(h, 0, m), full(h, 1, m), along_z(down))

    def to_mate(h, dz):
        wires.start(("m", h, dz), full(h, dz, 0), full(h, dz, 1), mate())

    def relay(h, m, onward):
        wires.arrive(("s", h, 3, m), full(h, 3, m), along_z(down))
        wires.start(("t", h, 0, m), blocks[h].at[3, m, low], blocks[h].at[2, m, low], along_z(up))
        if onward:
            to_mate(h, 3)
        wires.arrive(("s", h, 1, m), full(h, 1, m), along_z(up))
        wires.start(("t", h, 1, m), blocks[h].at[1, m, high], blocks[h].at[2, m, high], along_z(down))
        if onward:
            to_mate(h, 1)

    def last(h, m):
        wires.arrive(("t", h, 0, m), blocks[h].at[2, m, low], along_z(down))
        wires.arrive(("t", h, 1, m), blocks[h].at[2, m, high], along_z(up))

    to_mate(0, 0)
    spread(1, 0)
    spread(0, 0)
    to_mate(1, 0)
    hook("sent")
    wires.arrive(("m", 0, 0), full(0, 0, 1), mate())
    spread(0, 1)
    relay(1, 0, True)
    hook("one")
    relay(0, 0, False)
    wires.arrive(("m", 1, 0), full(1, 0, 1), mate())
    hook("own pair")
    last(1, 0)
    to_mate(1, 2)
    hook("two")
    relay(0, 1, False)
    hook("three")
    wires.arrive(("m", 1, 3), full(1, 3, 1), mate())
    wires.arrive(("m", 1, 1), full(1, 1, 1), mate())
    hook("sides")
    last(0, 0)
    last(0, 1)
    wires.arrive(("m", 1, 2), full(1, 2, 1), mate())
    hook("far")


def scatter(wires, out, bufs, produce, hook):
    z_half, z_full, mate0, mate1, e_half, e_full = bufs
    rows = out[0].shape[2]
    low, high = pl.ds(0, rows // 2), pl.ds(rows // 2, rows // 2)
    ways = ((0, 1, low, 1), (1, 3, high, -1))
    f32 = jnp.float32

    def wide(ref):
        return ref[...].astype(f32)

    def add_to(ref, *others):
        total = wide(ref)
        for other in others:
            total = total + wide(other)
        ref[...] = total.astype(ref.dtype)

    def mate_send(dz):
        wires.start(("m1", dz), out[1].at[dz, 1], mate1.at[dz], mate())

    def mate_join(dz):
        wires.arrive(("m1", dz), mate1.at[dz], mate())
        add_to(out[1].at[dz, 0], mate1.at[dz])

    produce(1, (2,))
    mate_send(2)
    produce(0, (2,))
    for m in (1, 0):
        for way, dz, part, step in ways:
            wires.start(("a", way, m), out[0].at[2, m, part], z_half.at[way, m], along_z(step))
    produce(0, (1, 3))
    produce(1, (1, 3))
    mate_send(1)
    mate_send(3)
    mate_join(2)
    for way, dz, part, step in ways:
        wires.start(("e", way), out[1].at[2, 0, part], e_half.at[way], along_z(step))
    for m in (1, 0):
        for way, dz, part, step in ways:
            wires.arrive(("a", way, m), z_half.at[way, m], along_z(-step))
            add_to(out[0].at[dz, m, part], z_half.at[way, m])
            wires.start(("b", way, m), out[0].at[dz, m], z_full.at[way, m], along_z(step))
    produce(1, (0,))
    mate_send(0)
    produce(0, (0,))
    hook("early")
    for way, dz, part, step in ways:
        mate_join(dz)
        wires.arrive(("e", way), e_half.at[way], along_z(-step))
        add_to(out[1].at[dz, 0, part], e_half.at[way])
        wires.start(("f", way), out[1].at[dz, 0], e_full.at[way], along_z(step))
    hook("middle")
    for way, dz, part, step in ways:
        wires.arrive(("b", way, 1), z_full.at[way, 1], along_z(-step))
    add_to(out[0].at[0, 1], z_full.at[0, 1], z_full.at[1, 1])
    wires.start(("m0",), out[0].at[0, 1], mate0, mate())
    hook("late")
    for way, dz, part, step in ways:
        wires.arrive(("b", way, 0), z_full.at[way, 0], along_z(-step))
    first = wide(out[0].at[0, 0]) + wide(z_full.at[0, 0]) + wide(z_full.at[1, 0])
    wires.arrive(("m1", 0), mate1.at[0], mate())
    second = wide(out[1].at[0, 0]) + wide(mate1.at[0])
    for way, dz, part, step in ways:
        wires.arrive(("f", way), e_full.at[way], along_z(-step))
        second = second + wide(e_full.at[way])
    wires.arrive(("m0",), mate0, mate())
    first = first + wide(mate0)
    return first, second


def norm_halves(rows, gain):
    mean_square = jnp.mean(rows * rows, axis=-1, keepdims=True)
    normed = (rows * lax.rsqrt(mean_square + EPSILON) * gain).astype(jnp.bfloat16)
    width, _ = column_halves(rows.shape[1])
    return normed[:, :width], normed[:, width:]


def stacked(blocks, h, dzs):
    _, _, rows, width = blocks[h].shape
    parts = [blocks[h][dz].reshape(2 * rows, width) for dz in dzs]
    return parts[0] if len(parts) == 1 else jnp.concatenate(parts, axis=0)


def project_kernel(
    tokens_ref, gain_ref, cos_ref, sin_ref, wq_hbm, wkv_hbm, wo_hbm, q_ref, kv_ref, wo_other,
    weights, others, blocks0, blocks1, load_sems, send_sems, recv_sems,
):
    blocks, rows = (blocks0, blocks1), blocks0.shape[2]
    split, width = blocks0.shape[3], weights.shape[0]
    neighbours = greet()
    qcols = wq_hbm.shape[1]
    cols = qcols + wkv_hbm.shape[1]
    z, x, _, _ = place()
    loads = [
        pltpu.make_async_copy(wq_hbm, weights.at[:, pl.ds(0, qcols)], load_sems.at[0]),
        pltpu.make_async_copy(wkv_hbm, weights.at[:, pl.ds(qcols, cols - qcols)], load_sems.at[1]),
    ]
    for load in loads:
        load.start()
    blocks0[0, 0], blocks1[0, 0] = norm_halves(tokens_ref[...].astype(jnp.float32), gain_ref[...])
    meet(neighbours)
    wires = Wires(send_sems, recv_sems)
    fetch_q = Fetch(wires, "q", wq_hbm, others, False, 0)
    fetch_kv = Fetch(wires, "kv", wkv_hbm, others, False, qcols)
    fetch_o = Fetch(wires, "o", wo_hbm, wo_other, True)

    def emit(dzs, mine):
        shard = weights if mine else others
        part = sum(
            jnp.dot(
                stacked(blocks, h, dzs),
                shard[slice(0, split) if h == 0 else slice(split, width), :],
                preferred_element_type=jnp.float32,
            )
            for h in range(2)
        )
        is_key = (x % 2 == 0) if mine else (x % 2 == 1)
        which = x % 2 if mine else 1 - x % 2
        first_col = 0 if mine else qcols
        for i, dz in enumerate(dzs):
            for m in range(2):
                whole = part[(2 * i + m) * rows : (2 * i + m + 1) * rows]
                zz = (z + dz) % SIDE
                mm = x // 2 if m == 0 else 1 - x // 2
                cosine, sine = cos_ref[zz, mm], sin_ref[zz, mm]
                for head in range(qcols // HEAD_DIM):
                    piece = whole[:, head * HEAD_DIM : (head + 1) * HEAD_DIM]
                    turned = piece * cosine + pltpu.roll(piece, HEAD_DIM // 2, 1) * sine
                    at = first_col + head * HEAD_DIM
                    q_ref[zz, mm, :, at : at + HEAD_DIM] = turned.astype(jnp.bfloat16)
                piece = whole[:, qcols:]
                turned = piece * cosine + pltpu.roll(piece, HEAD_DIM // 2, 1) * sine
                kv_ref[which, zz, mm] = jnp.where(is_key, turned, piece).astype(jnp.bfloat16)

    def hook(name):
        if name == "sent":
            for fetch in (fetch_q, fetch_kv, fetch_o):
                fetch.ask()
        elif name == "one":
            fetch_q.relay()
            fetch_kv.relay()
            for load in loads:
                load.wait()
        elif name == "own pair":
            emit((0,), True)
        elif name == "two":
            fetch_q.pass_on()
        elif name == "three":
            fetch_kv.pass_on()
            fetch_o.relay()
            fetch_q.settle()
        elif name == "sides":
            emit((3, 1), True)
            fetch_kv.settle()
            fetch_q.finish()
            fetch_kv.finish()
            emit((0,), False)
            emit((3, 1), False)
            fetch_o.pass_on()
        else:
            emit((2,), True)
            emit((2,), False)
            fetch_o.settle()
            fetch_o.finish()

    gather(wires, blocks, hook)
    wires.drain()


def project(tokens, gain, cosine, sine, w_query, w_keyval, w_out):
    rows, width = tokens.shape
    cols = w_query.shape[1] + w_keyval.shape[1]
    vmem = pl.BlockSpec(memory_space=pltpu.VMEM)
    hbm = pl.BlockSpec(memory_space=pl.ANY)
    bf16 = jnp.bfloat16
    return pl.pallas_call(
        project_kernel,
        out_shape=(
            jax.ShapeDtypeStruct((SIDE, 2, rows, 2 * w_query.shape[1]), bf16),
            jax.ShapeDtypeStruct((2, SIDE, 2, rows, w_keyval.shape[1]), bf16),
            jax.ShapeDtypeStruct(w_out.shape, bf16),
        ),
        in_specs=[vmem] * 4 + [hbm] * 3,
        out_specs=(vmem, vmem, hbm),
        scratch_shapes=[
            pltpu.VMEM((width, cols), bf16),
            pltpu.VMEM((width, cols), bf16),
            *[pltpu.VMEM((SIDE, 2, rows, part), bf16) for part in column_halves(width)],
            pltpu.SemaphoreType.DMA((2,)),
            pltpu.SemaphoreType.DMA((64,)),
            pltpu.SemaphoreType.DMA((64,)),
        ],
        compiler_params=pltpu.CompilerParams(
            collective_id=0, has_side_effects=True, vmem_limit_bytes=48 << 20
        ),
        name="project",
    )(tokens, gain, cosine, sine, w_query, w_keyval, w_out)


def finish_kernel(
    tokens_ref, attn_ref, gain_ref, wo_hbm, wo2_hbm, wg_hbm, wu_hbm, wd_hbm, out_ref,
    wo, wg, wu, wd, wg2, wu2, wd2, blocks0, blocks1, hidden, hidden2, sending0, sending1,
    z_half, z_full, mate0, mate1, e_half, e_full, state, load_sems, send_sems, recv_sems,
):
    blocks, sending = (blocks0, blocks1), (sending0, sending1)
    _, _, rows, split = blocks0.shape
    width = wo.shape[1]
    neighbours = greet()
    own = wo_hbm.shape[0]
    z, x, _, _ = place()
    loads = [
        pltpu.make_async_copy(src, dst, load_sems.at[i])
        for i, (src, dst) in enumerate(
            ((wo_hbm, wo.at[pl.ds(0, own)]), (wo2_hbm, wo.at[pl.ds(own, own)]), (wg_hbm, wg), (wu_hbm, wu), (wd_hbm, wd))
        )
    ]
    for load in loads:
        load.start()
    meet(neighbours)
    bufs = (z_half, z_full, mate0, mate1, e_half, e_full)
    weight_wires = Wires(send_sems.at[3], recv_sems.at[3])
    fetch_g = Fetch(weight_wires, "g", wg_hbm, wg2, True)
    fetch_u = Fetch(weight_wires, "u", wu_hbm, wu2, True)
    fetch_d = Fetch(weight_wires, "d", wd_hbm, wd2, True)
    fetch_g.ask()
    fetch_u.ask()
    loads[0].wait()
    loads[1].wait()

    def columns(h):
        return pl.ds(0, split) if h == 0 else pl.ds(split, width - split)

    def keep(h, dzs, part):
        for i, dz in enumerate(dzs):
            piece = part[2 * i * rows : 2 * (i + 1) * rows].astype(jnp.bfloat16)
            sending[h][dz] = piece.reshape(2, rows, piece.shape[1])

    def project_out(h, dzs):
        mine, other = x // 2, 1 - x // 2
        left = [attn_ref[(z + dz) % SIDE, m] for dz in dzs for m in (mine, other)]
        left = jnp.concatenate(left, axis=0)
        keep(h, dzs, jnp.dot(left, wo[:, columns(h)], preferred_element_type=jnp.float32))

    def hook_out(name):
        if name == "early":
            fetch_g.relay()
        elif name == "late":
            fetch_u.relay()
            fetch_g.pass_on()

    out_wires = Wires(send_sems.at[0], recv_sems.at[0])
    first, second = scatter(out_wires, sending, bufs, project_out, hook_out)
    for h, proj in enumerate((first, second)):
        state[:, columns(h)] = (tokens_ref[:, columns(h)].astype(jnp.float32) + proj).astype(jnp.bfloat16)
    blocks0[0, 0], blocks1[0, 0] = norm_halves(state[...].astype(jnp.float32), gain_ref[...])

    def gated(dzs, mine):
        gates, ups, result = (wg, wu, hidden) if mine else (wg2, wu2, hidden2)
        gate = upward = 0.0
        for h in range(2):
            left = stacked(blocks, h, dzs)
            across = (((1,), (1,)), ((), ()))
            gate = gate + lax.dot_general(left, gates[:, columns(h)], across, preferred_element_type=jnp.float32)
            upward = upward + lax.dot_general(left, ups[:, columns(h)], across, preferred_element_type=jnp.float32)
        value = (gate / (1.0 + jnp.exp(-gate)) * upward).astype(jnp.bfloat16)
        for i, dz in enumerate(dzs):
            result[dz] = value[2 * i * rows : 2 * (i + 1) * rows].reshape(2, rows, value.shape[1])

    def hook_gated(name):
        if name == "sent":
            fetch_d.ask()
            loads[2].wait()
            loads[3].wait()
        elif name == "one":
            fetch_g.settle()
            fetch_u.pass_on()
        elif name == "own pair":
            gated((0,), True)
            fetch_d.relay()
        elif name == "two":
            fetch_g.finish()
            fetch_u.settle()
        elif name == "sides":
            gated((3, 1), True)
            fetch_d.pass_on()
            fetch_u.finish()
            gated((0,), False)
            gated((3, 1), False)
        elif name == "far":
            gated((2,), True)
            gated((2,), False)
            fetch_d.settle()
            fetch_d.finish()
            loads[4].wait()

    gather_wires = Wires(send_sems.at[1], recv_sems.at[1])
    gather(gather_wires, blocks, hook_gated)
    out_wires.drain()

    def project_down(h, dzs):
        part = 0.0
        for values, weights in ((hidden, wd), (hidden2, wd2)):
            left = [values[dz].reshape(2 * rows, values.shape[3]) for dz in dzs]
            left = left[0] if len(left) == 1 else jnp.concatenate(left, axis=0)
            part = part + jnp.dot(left, weights[:, columns(h)], preferred_element_type=jnp.float32)
        keep(h, dzs, part)

    down_wires = Wires(send_sems.at[2], recv_sems.at[2])
    down = scatter(down_wires, sending, bufs, project_down, lambda name: None)
    for h in range(2):
        out_ref[:, columns(h)] = (state[:, columns(h)].astype(jnp.float32) + down[h]).astype(jnp.bfloat16)
    for wires in (gather_wires, down_wires, weight_wires):
        wires.drain()


def finish(tokens, attn, gain, w_out, w_out_other, w_gate, w_up, w_down):
    rows, width = tokens.shape
    hidden = w_gate.shape[0]
    vmem = pl.BlockSpec(memory_space=pltpu.VMEM)
    hbm = pl.BlockSpec(memory_space=pl.ANY)
    wide, narrow = column_halves(width)
    bf16 = jnp.bfloat16
    return pl.pallas_call(
        finish_kernel,
        out_shape=jax.ShapeDtypeStruct((rows, width), bf16),
        in_specs=[vmem] * 3 + [hbm] * 5,
        out_specs=vmem,
        scratch_shapes=[
            pltpu.VMEM((2 * w_out.shape[0], width), bf16),
            *[pltpu.VMEM((hidden, width), bf16)] * 6,
            pltpu.VMEM((SIDE, 2, rows, wide), bf16),
            pltpu.VMEM((SIDE, 2, rows, narrow), bf16),
            pltpu.VMEM((SIDE, 2, rows, hidden), bf16),
            pltpu.VMEM((SIDE, 2, rows, hidden), bf16),
            pltpu.VMEM((SIDE, 2, rows, wide), bf16),
            pltpu.VMEM((SIDE, 2, rows, narrow), bf16),
            pltpu.VMEM((2, 2, rows // 2, wide), bf16),
            pltpu.VMEM((2, 2, rows, wide), bf16),
            pltpu.VMEM((rows, wide), bf16),
            pltpu.VMEM((SIDE, rows, narrow), bf16),
            pltpu.VMEM((2, rows // 2, narrow), bf16),
            pltpu.VMEM((2, rows, narrow), bf16),
            pltpu.VMEM((rows, width), bf16),
            pltpu.SemaphoreType.DMA((5,)),
            pltpu.SemaphoreType.DMA((4, 48)),
            pltpu.SemaphoreType.DMA((4, 48)),
        ],
        compiler_params=pltpu.CompilerParams(
            collective_id=1, has_side_effects=True, vmem_limit_bytes=60 << 20
        ),
        name="finish",
    )(tokens, attn, gain, w_out, w_out_other, w_gate, w_up, w_down)


def serve_kernel(q_ref, own_ref, first_ref, spot_ref, o_ref, held, peak, total, summed, send_sems, recv_sems):
    z, x, y, core = place()
    mine = lax.rem(lax.div(x + 1, 2), 2)
    theirs = 1 - mine
    base = 1 - core
    rows = q_ref.shape[2]
    width = own_ref.shape[4]
    heads = q_ref.shape[3] // width
    factor = math.log2(math.e) / math.sqrt(width)
    across, ahead, other_core = holder(), along_y(1), twin()
    neighbours = greet()
    held[base, mine] = own_ref[...]
    meet(neighbours)
    started = []

    def send(g, c, target, device):
        made = pltpu.make_async_remote_copy(
            src_ref=held.at[g, c],
            dst_ref=held.at[target, c],
            send_sem=send_sems.at[len(started)],
            recv_sem=recv_sems.at[target, c],
            device_id=device,
            device_id_type=MESH,
        )
        made.start()
        started.append(True)

    def arrive(g, c):
        pltpu.make_async_remote_copy(
            src_ref=held.at[g, c],
            dst_ref=held.at[g, c],
            send_sem=send_sems.at[0],
            recv_sem=recv_sems.at[g, c],
            device_id=across,
            device_id_type=MESH,
        ).wait_recv()

    send(base, mine, base, across)
    send(base, mine, base + 2, ahead)
    send(base, mine, base, other_core)
    peak[...] = jnp.full(peak.shape, NEGATIVE, jnp.float32)
    total[...] = jnp.zeros(total.shape, jnp.float32)
    summed[...] = jnp.zeros(summed.shape, jnp.float32)

    in_run = lax.broadcasted_iota(jnp.int32, (1, 2 * rows), 1)
    later = (in_run >= rows).astype(jnp.int32)

    def column(ref, zz):
        return jnp.concatenate([ref[zz]] * heads, axis=0)

    def step(tiles, g, c, back, causal):
        run = 2 * rows
        shift = (back - 2 * y - core) * (SIDE * SIDE * rows)
        held_before = [(peak[zz], total[zz], summed[zz]) for zz, _, _ in tiles]
        scored = []
        for zz, begin, size in tiles:
            tile = [q_ref[zz, :, :, h * width : (h + 1) * width].reshape(run, width) for h in range(heads)]
            query = jnp.concatenate(tile, axis=0)
            keys = held[g, c, 0, begin : begin + size].reshape(size * run, width)
            scored.append(
                lax.dot_general(query, keys, (((1,), (1,)), ((), ())), preferred_element_type=jnp.float32)
            )
        after = []
        for (zz, begin, size), scores, (old, sums, outs) in zip(tiles, scored, held_before):
            low, high = column(first_ref, zz) + shift, column(spot_ref, zz) + shift
            parts = []
            for run_at in range(size):
                spots = in_run + c * (rows - 2 * rows * later) + later * (SIDE - 2) * rows
                spots = spots + (begin + run_at) * (SIDE * rows)
                seen = spots >= low
                if causal:
                    seen = seen & (spots <= high)
                parts.append(jnp.where(seen, scores[:, run_at * run : (run_at + 1) * run], NEGATIVE))
            top = functools.reduce(jnp.maximum, parts)
            new = jnp.maximum(old, jnp.broadcast_to(jnp.max(top, axis=1, keepdims=True) * factor, old.shape))
            decay = jnp.exp2(old - new)
            parts = [jnp.exp2(part * factor - new) for part in parts]
            weights = jnp.concatenate([part.astype(jnp.bfloat16) for part in parts], axis=1)
            values = held[g, c, 1, begin : begin + size].reshape(size * run, width)
            outs = outs * decay + jnp.dot(weights, values, preferred_element_type=jnp.float32)
            after.append((new, sums * decay + functools.reduce(jnp.add, parts), outs))
        for (zz, _, _), state in zip(tiles, after):
            peak[zz], total[zz], summed[zz] = state

    def own_block(c):
        for pair in ((0, 3), (1, 2)):
            step([(zz, 0, zz + 1) for zz in pair], base, c, 0, True)

    def far_block(c):
        for pair in ((0, 3), (1, 2)):
            step([(zz, zz, SIDE - zz) for zz in pair], base + 4, c, 4, False)

    def per_class(work):
        def one(i, carry):
            work(mine + i * (theirs - mine))
            return carry

        return one

    def first_class(i, carry):
        @pl.when(i == 1)
        def _():
            arrive(base, theirs)
            send(base, theirs, base, other_core)
            arrive(base + 2, mine)
            send(base + 2, mine, base + 4, ahead)
            send(base + 2, mine, base + 2, across)
            send(base + 2, mine, base + 2, other_core)

        own_block(mine + i * (theirs - mine))
        return carry

    lax.fori_loop(0, 2, first_class, 0)

    def middle(stage, carry):
        final = lax.div(stage, 4)
        back = (1 - final) * (1 + lax.rem(stage, 2)) + 3 * final
        c = mine + ((1 - final) * lax.div(stage, 2) + final * (stage - 4)) * (theirs - mine)

        @pl.when(stage == 2)
        def _():
            arrive(base + 2, theirs)
            send(base + 2, theirs, base + 2, other_core)
            arrive(base + 4, mine)
            send(base + 4, mine, base + 4, across)
            send(base + 4, mine, base + 4, other_core)

        @pl.when(stage == 4)
        def _():
            arrive(base + 4, theirs)
            send(base + 4, theirs, base + 4, other_core)

        @pl.when(back != 2)
        def _():
            arrive(base + back, c)

        def over_runs(pair, inner):
            step([(2 * pair + i, 0, SIDE) for i in range(2)], base + back, c, back, False)
            return inner

        return lax.fori_loop(0, SIDE // 2, over_runs, carry)

    lax.fori_loop(0, 6, middle, 0)
    lax.fori_loop(0, 2, per_class(far_block), 0)
    spare = core * 5
    arrive(spare, 0)
    arrive(spare, 1)
    for zz in range(SIDE):
        answer = (summed[zz] / jnp.sum(total[zz], axis=1, keepdims=True)).astype(jnp.bfloat16)
        for h in range(heads):
            piece = answer[h * 2 * rows : (h + 1) * 2 * rows]
            o_ref[zz, :, :, h * width : (h + 1) * width] = piece.reshape(2, rows, width)
    for number in range(len(started)):
        pltpu.make_async_remote_copy(
            src_ref=held.at[0, 0],
            dst_ref=held.at[0, 0],
            send_sem=send_sems.at[number],
            recv_sem=recv_sems.at[0, 0],
            device_id=across,
            device_id_type=MESH,
        ).wait_send()


def serve(queries, own, first, spots):
    rows = queries.shape[2]
    width = own.shape[4]
    heads = queries.shape[3] // width
    tall = heads * 2 * rows
    vmem = pl.BlockSpec(memory_space=pltpu.VMEM)
    return pl.pallas_call(
        serve_kernel,
        out_shape=jax.ShapeDtypeStruct(queries.shape, jnp.bfloat16),
        in_specs=[vmem] * 4,
        out_specs=vmem,
        scratch_shapes=[
            pltpu.VMEM((6, 2, *own.shape), jnp.bfloat16),
            pltpu.VMEM((SIDE, tall, 2 * rows), jnp.float32),
            pltpu.VMEM((SIDE, tall, 2 * rows), jnp.float32),
            pltpu.VMEM((SIDE, tall, width), jnp.float32),
            pltpu.SemaphoreType.DMA((11,)),
            pltpu.SemaphoreType.DMA((6, 2)),
        ],
        compiler_params=pltpu.CompilerParams(
            collective_id=2, has_side_effects=True, vmem_limit_bytes=40 << 20
        ),
        name="serve",
    )(queries, own, first, spots)


def body(tokens, doc_lengths, attn_gain, mlp_gain, w_query, w_keyval, w_out, w_gate, w_up, w_down):
    token_index = lax.axis_index("token")
    x = lax.axis_index("tensor") % SIDE
    rows = tokens.shape[0]
    qblk = 2 * rows
    block_rows = rows * SIDE * SIDE
    outer = (x == 0) | (x == SIDE - 1)
    lows, highs = jnp.where(outer, 0, 1), jnp.where(outer, SIDE - 1, SIDE - 2)
    runs = token_index * block_rows + jnp.arange(SIDE, dtype=jnp.int32) * (SIDE * rows)
    blocks = runs[:, None] + jnp.stack([lows, highs])[None, :] * rows
    spots = (blocks[:, :, None] + jnp.arange(rows, dtype=jnp.int32)).reshape(-1).astype(jnp.int32)
    ends = jnp.cumsum(doc_lengths)
    passed = spots[:, None] >= ends[None, :-1]
    first = jnp.max(jnp.where(passed, ends[None, :-1], 0), axis=1).astype(jnp.int32)
    position = (spots - first).astype(jnp.float32)
    half = HEAD_DIM // 2
    freq = jnp.exp(-math.log(ROPE_BASE) * jnp.arange(half, dtype=jnp.float32) * (2.0 / HEAD_DIM))
    angle = position[:, None] * freq[None, :]
    cosine, sine = jnp.cos(angle), jnp.sin(angle)
    cosine = jnp.concatenate([cosine, cosine], axis=1).reshape(SIDE, 2, rows, HEAD_DIM)
    sine = jnp.concatenate([-sine, sine], axis=1).reshape(SIDE, 2, rows, HEAD_DIM)
    queries, own, w_out_other = project(tokens, attn_gain[None, :], cosine, sine, w_query, w_keyval, w_out)
    attn = serve(queries, own, first.reshape(SIDE, qblk, 1), spots.reshape(SIDE, qblk, 1))
    return finish(tokens, attn, mlp_gain[None, :], w_out, w_out_other, w_gate.T, w_up.T, w_down)


def solution(mesh):
    return jax.shard_map(
        body,
        mesh=mesh,
        in_specs=(
            P(("token", "tensor"), None),
            P(),
            P(),
            P(),
            P(None, "tensor"),
            P(None, "tensor"),
            P("tensor", None),
            P(None, "tensor"),
            P(None, "tensor"),
            P("tensor", None),
        ),
        out_specs=P(("token", "tensor"), None),
        check_vma=False,
    )
```

```python
import functools
import math

import jax
import jax.numpy as jnp
from jax import lax
from jax.experimental import pallas as pl
from jax.experimental.pallas import tpu as pltpu
from jax.sharding import PartitionSpec as P

HEAD_DIM = 128
SIDE = 4
CORES = 2
YS = 4

EPSILON = 1e-05
ROPE_BASE = 500000.0
NEGATIVE = -1e30
MESH = pl.DeviceIdType.MESH


def place():
    me, token = lax.axis_index("tensor"), lax.axis_index("token")
    return me // SIDE, me % SIDE, token // CORES, token % CORES


def along_z(step):
    z, x, _, _ = place()
    return {"tensor": ((z + step + SIDE) % SIDE) * SIDE + x}


def mate():
    z, x, _, _ = place()
    return {"tensor": z * SIDE + SIDE - 1 - x}


def holder():
    z, x, _, _ = place()
    return {"tensor": z * SIDE + x + 1 - 2 * (x % 2)}


def along_y(step):
    _, _, y, core = place()
    return {"token": ((y + step + YS) % YS) * CORES + core}


def twin():
    _, _, y, core = place()
    return {"token": y * CORES + 1 - core}


def greet():
    others = [along_z(1), along_z(-1), mate(), holder(), along_y(1), along_y(-1), twin()]
    for other in others:
        pl.semaphore_signal(pltpu.get_barrier_semaphore(), inc=1, device_id=other, device_id_type=MESH)
    return len(others)


def meet(others):
    pl.semaphore_wait(pltpu.get_barrier_semaphore(), others)


def column_halves(width):
    first = width * 9 // 16
    return first, width - first


class Wires:
    def __init__(self, send_sems, recv_sems):
        self.send_sems, self.recv_sems, self.slots, self.started = send_sems, recv_sems, {}, []

    def copy(self, key, src, dst, device):
        slot = self.slots.setdefault(key, len(self.slots))
        return pltpu.make_async_remote_copy(
            src_ref=src,
            dst_ref=dst,
            send_sem=self.send_sems.at[slot],
            recv_sem=self.recv_sems.at[slot],
            device_id=device,
            device_id_type=MESH,
        )

    def start(self, key, src, dst, device):
        made = self.copy(key, src, dst, device)
        made.start()
        self.started.append(made)

    def arrive(self, key, dst, device):
        self.copy(key, dst, dst, device).wait_recv()

    def drain(self):
        for made in self.started:
            made.wait_send()
        self.started = []


class Fetch:
    def __init__(self, wires, name, src, dst, lanes, first_lane=0, landed=None, landed_sem=None):
        self.wires, self.name, self.src, self.dst, self.lanes, self.first_lane = wires, name, src, dst, lanes, first_lane
        self.landed, self.kept = landed, None
        if landed is not None:
            self.kept = pltpu.make_async_copy(landed, self.dst_slot(dst), landed_sem)

    @property
    def size(self):
        return self.src.shape[1 if self.lanes else 0] // (YS * CORES)

    def dst_slot(self, ref):
        _, _, y, core = place()
        return self.cut(ref, y * CORES + core, None, self.first_lane)

    def cut(self, ref, number, part, offset):
        size = self.size if part is None else self.size // 2
        start = pl.multiple_of(number * self.size, self.size) + (0 if part in (None, 0) else size)
        start = pl.multiple_of(start, size)
        if self.lanes:
            return ref.at[:, pl.ds(start, size)]
        return ref.at[pl.ds(start, size), pl.ds(offset, self.src.shape[1])]

    def slot(self, dy, dc, part=None):
        _, _, y, core = place()
        number = ((y + dy + YS) % YS) * CORES + (core if dc == 0 else 1 - core)
        return self.cut(self.dst, number, part, self.first_lane)

    def start(self, key, ref, device):
        self.wires.start((self.name, key), ref, ref, device)

    def arrive(self, key, ref):
        self.wires.arrive((self.name, key), ref, holder())

    def ask(self):
        _, _, y, core = place()
        self.wires.start((self.name, "x"), self.cut(self.src, y * CORES + core, None, 0), self.slot(0, 0), holder())

    def land(self, landed):
        self.wires.start((self.name, "x"), self.dst_slot(self.src), landed, holder())

    def relay(self):
        source = self.landed
        if source is None:
            source = self.slot(0, 0)
            self.arrive("x", source)
        else:
            self.kept.start()
        for key, device in (("y3", along_y(1)), ("y1", along_y(-1)), ("c0", twin())):
            self.wires.start((self.name, key), source, self.slot(0, 0), device)

    def pass_on(self):
        self.arrive("y3", self.slot(3, 0))
        self.start("h0", self.slot(3, 0, 0), along_y(1))
        self.start("c3", self.slot(3, 0), twin())
        self.arrive("y1", self.slot(1, 0))
        self.start("h1", self.slot(1, 0, 1), along_y(-1))
        self.start("c1", self.slot(1, 0), twin())

    def settle(self):
        self.arrive("h0", self.slot(2, 0, 0))
        self.arrive("h1", self.slot(2, 0, 1))
        self.start("c2", self.slot(2, 0), twin())

    def finish(self):
        for dy in (0, 3, 1, 2):
            self.arrive("c%d" % dy, self.slot(dy, 1))
        if self.kept is not None:
            self.kept.wait()


def gather(wires, blocks, hook):
    rows = blocks[0].shape[2]
    low, high = pl.ds(0, rows // 2), pl.ds(rows // 2, rows // 2)
    up, down = 1, -1

    def full(h, dz, m):
        return blocks[h].at[dz, m]

    def spread(h, m):
        wires.start(("s", h, 3, m), full(h, 0, m), full(h, 3, m), along_z(up))
        wires.start(("s", h, 1, m), full(h, 0, m), full(h, 1, m), along_z(down))

    def to_mate(h, dz):
        wires.start(("m", h, dz), full(h, dz, 0), full(h, dz, 1), mate())

    def relay(h, m, onward):
        wires.arrive(("s", h, 3, m), full(h, 3, m), along_z(down))
        wires.start(("t", h, 0, m), blocks[h].at[3, m, low], blocks[h].at[2, m, low], along_z(up))
        if onward:
            to_mate(h, 3)
        wires.arrive(("s", h, 1, m), full(h, 1, m), along_z(up))
        wires.start(("t", h, 1, m), blocks[h].at[1, m, high], blocks[h].at[2, m, high], along_z(down))
        if onward:
            to_mate(h, 1)

    def last(h, m):
        wires.arrive(("t", h, 0, m), blocks[h].at[2, m, low], along_z(down))
        wires.arrive(("t", h, 1, m), blocks[h].at[2, m, high], along_z(up))

    to_mate(0, 0)
    spread(1, 0)
    spread(0, 0)
    to_mate(1, 0)
    hook("sent")
    wires.arrive(("m", 0, 0), full(0, 0, 1), mate())
    spread(0, 1)
    relay(1, 0, True)
    hook("one")
    relay(0, 0, False)
    wires.arrive(("m", 1, 0), full(1, 0, 1), mate())
    hook("own pair")
    last(1, 0)
    to_mate(1, 2)
    hook("two")
    relay(0, 1, False)
    hook("three")
    wires.arrive(("m", 1, 3), full(1, 3, 1), mate())
    wires.arrive(("m", 1, 1), full(1, 1, 1), mate())
    hook("sides")
    last(0, 0)
    last(0, 1)
    wires.arrive(("m", 1, 2), full(1, 2, 1), mate())
    hook("far")


def scatter(wires, out, bufs, produce, hook):
    z_half, z_full, mate0, mate1, e_half, e_full = bufs
    rows = out[0].shape[2]
    low, high = pl.ds(0, rows // 2), pl.ds(rows // 2, rows // 2)
    ways = ((0, 1, low, 1), (1, 3, high, -1))
    f32 = jnp.float32

    def wide(ref):
        return ref[...].astype(f32)

    def add_to(ref, *others):
        total = wide(ref)
        for other in others:
            total = total + wide(other)
        ref[...] = total.astype(ref.dtype)

    def mate_send(dz):
        wires.start(("m1", dz), out[1].at[dz, 1], mate1.at[dz], mate())

    def mate_join(dz):
        wires.arrive(("m1", dz), mate1.at[dz], mate())
        add_to(out[1].at[dz, 0], mate1.at[dz])

    produce(1, (2,))
    mate_send(2)
    produce(0, (2,))
    for m in (1, 0):
        for way, dz, part, step in ways:
            wires.start(("a", way, m), out[0].at[2, m, part], z_half.at[way, m], along_z(step))
    hook("begun")
    produce(0, (1, 3))
    produce(1, (1, 3))
    mate_send(1)
    mate_send(3)
    mate_join(2)
    for way, dz, part, step in ways:
        wires.start(("e", way), out[1].at[2, 0, part], e_half.at[way], along_z(step))
    for m in (1, 0):
        for way, dz, part, step in ways:
            wires.arrive(("a", way, m), z_half.at[way, m], along_z(-step))
            add_to(out[0].at[dz, m, part], z_half.at[way, m])
            wires.start(("b", way, m), out[0].at[dz, m], z_full.at[way, m], along_z(step))
    produce(1, (0,))
    mate_send(0)
    produce(0, (0,))
    hook("early")
    for way, dz, part, step in ways:
        mate_join(dz)
        wires.arrive(("e", way), e_half.at[way], along_z(-step))
        add_to(out[1].at[dz, 0, part], e_half.at[way])
        wires.start(("f", way), out[1].at[dz, 0], e_full.at[way], along_z(step))
    hook("middle")
    for way, dz, part, step in ways:
        wires.arrive(("b", way, 1), z_full.at[way, 1], along_z(-step))
    add_to(out[0].at[0, 1], z_full.at[0, 1], z_full.at[1, 1])
    wires.start(("m0",), out[0].at[0, 1], mate0, mate())
    hook("late")
    for way, dz, part, step in ways:
        wires.arrive(("b", way, 0), z_full.at[way, 0], along_z(-step))
    first = wide(out[0].at[0, 0]) + wide(z_full.at[0, 0]) + wide(z_full.at[1, 0])
    wires.arrive(("m1", 0), mate1.at[0], mate())
    second = wide(out[1].at[0, 0]) + wide(mate1.at[0])
    for way, dz, part, step in ways:
        wires.arrive(("f", way), e_full.at[way], along_z(-step))
        second = second + wide(e_full.at[way])
    wires.arrive(("m0",), mate0, mate())
    first = first + wide(mate0)
    return first, second


def norm_halves(rows, gain):
    mean_square = jnp.mean(rows * rows, axis=-1, keepdims=True)
    normed = (rows * lax.rsqrt(mean_square + EPSILON) * gain).astype(jnp.bfloat16)
    width, _ = column_halves(rows.shape[1])
    return normed[:, :width], normed[:, width:]


def stacked(blocks, h, dzs):
    _, _, rows, width = blocks[h].shape
    parts = [blocks[h][dz].reshape(2 * rows, width) for dz in dzs]
    return parts[0] if len(parts) == 1 else jnp.concatenate(parts, axis=0)


def project_kernel(
    tokens_ref, gain_ref, cos_ref, sin_ref, wq_hbm, wkv_hbm, wo_hbm, wg_hbm, q_ref, kv_ref, landed_o, landed_g,
    weights, others, blocks0, blocks1, load_sems, send_sems, recv_sems,
):
    blocks, rows = (blocks0, blocks1), blocks0.shape[2]
    split, width = blocks0.shape[3], weights.shape[0]
    neighbours = greet()
    qcols = wq_hbm.shape[1]
    cols = qcols + wkv_hbm.shape[1]
    z, x, _, _ = place()
    loads = [
        pltpu.make_async_copy(wq_hbm, weights.at[:, pl.ds(0, qcols)], load_sems.at[0]),
        pltpu.make_async_copy(wkv_hbm, weights.at[:, pl.ds(qcols, cols - qcols)], load_sems.at[1]),
    ]
    for load in loads:
        load.start()
    blocks0[0, 0], blocks1[0, 0] = norm_halves(tokens_ref[...].astype(jnp.float32), gain_ref[...])
    meet(neighbours)
    wires = Wires(send_sems, recv_sems)
    fetch_q = Fetch(wires, "q", wq_hbm, others, False, 0)
    fetch_kv = Fetch(wires, "kv", wkv_hbm, others, False, qcols)
    fetch_o = Fetch(wires, "o", wo_hbm, None, True)
    fetch_g = Fetch(wires, "g", wg_hbm, None, True)

    def emit(dzs, mine):
        shard = weights if mine else others
        part = sum(
            jnp.dot(
                stacked(blocks, h, dzs),
                shard[slice(0, split) if h == 0 else slice(split, width), :],
                preferred_element_type=jnp.float32,
            )
            for h in range(2)
        )
        is_key = (x % 2 == 0) if mine else (x % 2 == 1)
        which = x % 2 if mine else 1 - x % 2
        first_col = 0 if mine else qcols
        for i, dz in enumerate(dzs):
            for m in range(2):
                whole = part[(2 * i + m) * rows : (2 * i + m + 1) * rows]
                zz = (z + dz) % SIDE
                mm = x // 2 if m == 0 else 1 - x // 2
                cosine, sine = cos_ref[zz, mm], sin_ref[zz, mm]
                for head in range(qcols // HEAD_DIM):
                    piece = whole[:, head * HEAD_DIM : (head + 1) * HEAD_DIM]
                    turned = piece * cosine + pltpu.roll(piece, HEAD_DIM // 2, 1) * sine
                    at = first_col + head * HEAD_DIM
                    q_ref[zz, mm, :, at : at + HEAD_DIM] = turned.astype(jnp.bfloat16)
                piece = whole[:, qcols:]
                turned = piece * cosine + pltpu.roll(piece, HEAD_DIM // 2, 1) * sine
                kv_ref[which, zz, mm] = jnp.where(is_key, turned, piece).astype(jnp.bfloat16)

    def hook(name):
        if name == "sent":
            fetch_q.ask()
            fetch_kv.ask()
            fetch_o.land(landed_o)
            fetch_g.land(landed_g)
        elif name == "one":
            fetch_q.relay()
            fetch_kv.relay()
            for load in loads:
                load.wait()
        elif name == "own pair":
            emit((0,), True)
        elif name == "two":
            fetch_q.pass_on()
        elif name == "three":
            fetch_kv.pass_on()
            fetch_q.settle()
        elif name == "sides":
            emit((3, 1), True)
            fetch_kv.settle()
            fetch_q.finish()
            fetch_kv.finish()
            emit((0,), False)
            emit((3, 1), False)
        else:
            emit((2,), True)
            emit((2,), False)

    gather(wires, blocks, hook)
    wires.arrive(("o", "x"), landed_o, holder())
    wires.arrive(("g", "x"), landed_g, holder())
    wires.drain()


def project(tokens, gain, cosine, sine, w_query, w_keyval, w_out, w_gate):
    rows, width = tokens.shape
    cols = w_query.shape[1] + w_keyval.shape[1]
    vmem = pl.BlockSpec(memory_space=pltpu.VMEM)
    hbm = pl.BlockSpec(memory_space=pl.ANY)
    bf16 = jnp.bfloat16
    return pl.pallas_call(
        project_kernel,
        out_shape=(
            jax.ShapeDtypeStruct((SIDE, 2, rows, 2 * w_query.shape[1]), bf16),
            jax.ShapeDtypeStruct((2, SIDE, 2, rows, w_keyval.shape[1]), bf16),
            jax.ShapeDtypeStruct((w_out.shape[0], w_out.shape[1] // (YS * CORES)), bf16),
            jax.ShapeDtypeStruct((w_gate.shape[0], w_gate.shape[1] // (YS * CORES)), bf16),
        ),
        in_specs=[vmem] * 4 + [hbm] * 4,
        out_specs=(vmem, vmem, hbm, hbm),
        scratch_shapes=[
            pltpu.VMEM((width, cols), bf16),
            pltpu.VMEM((width, cols), bf16),
            *[pltpu.VMEM((SIDE, 2, rows, part), bf16) for part in column_halves(width)],
            pltpu.SemaphoreType.DMA((2,)),
            pltpu.SemaphoreType.DMA((64,)),
            pltpu.SemaphoreType.DMA((64,)),
        ],
        compiler_params=pltpu.CompilerParams(
            collective_id=0, has_side_effects=True, vmem_limit_bytes=48 << 20
        ),
        name="project",
    )(tokens, gain, cosine, sine, w_query, w_keyval, w_out, w_gate)


def finish_kernel(
    tokens_ref, attn_ref, gain_ref, wo_hbm, wo2_hbm, wg_hbm, wu_hbm, wd_hbm, landed_g, out_ref,
    wo, wg, wu, wd, wg2, wu2, wd2, blocks0, blocks1, hidden, hidden2, sending0, sending1,
    z_half, z_full, mate0, mate1, e_half, e_full, state, load_sems, send_sems, recv_sems,
):
    blocks, sending = (blocks0, blocks1), (sending0, sending1)
    _, _, rows, split = blocks0.shape
    width = wo.shape[1]
    neighbours = greet()
    own = wo_hbm.shape[0]
    z, x, _, _ = place()
    loads = [
        pltpu.make_async_copy(src, dst, load_sems.at[i])
        for i, (src, dst) in enumerate(
            ((wo_hbm, wo.at[pl.ds(0, own)]), (wo2_hbm, wo.at[pl.ds(own, own)]), (wg_hbm, wg), (wu_hbm, wu), (wd_hbm, wd))
        )
    ]
    for load in loads[:2]:
        load.start()
    meet(neighbours)
    bufs = (z_half, z_full, mate0, mate1, e_half, e_full)
    weight_wires = Wires(send_sems.at[3], recv_sems.at[3])
    fetch_g = Fetch(weight_wires, "g", wg_hbm, wg2, True, 0, landed_g, load_sems.at[5])
    fetch_u = Fetch(weight_wires, "u", wu_hbm, wu2, True)
    fetch_d = Fetch(weight_wires, "d", wd_hbm, wd2, True)
    loads[0].wait()
    loads[1].wait()

    def columns(h):
        return pl.ds(0, split) if h == 0 else pl.ds(split, width - split)

    def keep(h, dzs, part):
        for i, dz in enumerate(dzs):
            piece = part[2 * i * rows : 2 * (i + 1) * rows].astype(jnp.bfloat16)
            sending[h][dz] = piece.reshape(2, rows, piece.shape[1])

    def project_out(h, dzs):
        mine, other = x // 2, 1 - x // 2
        left = [attn_ref[(z + dz) % SIDE, m] for dz in dzs for m in (mine, other)]
        left = jnp.concatenate(left, axis=0)
        keep(h, dzs, jnp.dot(left, wo[:, columns(h)], preferred_element_type=jnp.float32))

    def hook_out(name):
        if name == "begun":
            for load in loads[2:]:
                load.start()
            fetch_g.relay()
            fetch_u.ask()
            fetch_d.ask()
        elif name == "early":
            fetch_g.pass_on()
            fetch_u.relay()
        elif name == "late":
            fetch_g.settle()
            fetch_d.relay()

    out_wires = Wires(send_sems.at[0], recv_sems.at[0])
    first, second = scatter(out_wires, sending, bufs, project_out, hook_out)
    for h, proj in enumerate((first, second)):
        state[:, columns(h)] = (tokens_ref[:, columns(h)].astype(jnp.float32) + proj).astype(jnp.bfloat16)
    blocks0[0, 0], blocks1[0, 0] = norm_halves(state[...].astype(jnp.float32), gain_ref[...])

    def gated(dzs, mine):
        gates, ups, result = (wg, wu, hidden) if mine else (wg2, wu2, hidden2)
        gate = upward = 0.0
        for h in range(2):
            left = stacked(blocks, h, dzs)
            across = (((1,), (1,)), ((), ()))
            gate = gate + lax.dot_general(left, gates[:, columns(h)], across, preferred_element_type=jnp.float32)
            upward = upward + lax.dot_general(left, ups[:, columns(h)], across, preferred_element_type=jnp.float32)
        value = (gate / (1.0 + jnp.exp(-gate)) * upward).astype(jnp.bfloat16)
        for i, dz in enumerate(dzs):
            result[dz] = value[2 * i * rows : 2 * (i + 1) * rows].reshape(2, rows, value.shape[1])

    def hook_gated(name):
        if name == "sent":
            loads[2].wait()
            loads[3].wait()
            fetch_u.pass_on()
        elif name == "one":
            fetch_g.finish()
            fetch_d.pass_on()
        elif name == "own pair":
            gated((0,), True)
            fetch_u.settle()
        elif name == "three":
            fetch_d.settle()
        elif name == "sides":
            gated((3, 1), True)
            fetch_u.finish()
            gated((0,), False)
            gated((3, 1), False)
        elif name == "far":
            gated((2,), True)
            gated((2,), False)
            fetch_d.finish()
            loads[4].wait()

    gather_wires = Wires(send_sems.at[1], recv_sems.at[1])
    gather(gather_wires, blocks, hook_gated)
    out_wires.drain()

    def project_down(h, dzs):
        part = 0.0
        for values, weights in ((hidden, wd), (hidden2, wd2)):
            left = [values[dz].reshape(2 * rows, values.shape[3]) for dz in dzs]
            left = left[0] if len(left) == 1 else jnp.concatenate(left, axis=0)
            part = part + jnp.dot(left, weights[:, columns(h)], preferred_element_type=jnp.float32)
        keep(h, dzs, part)

    down_wires = Wires(send_sems.at[2], recv_sems.at[2])
    down = scatter(down_wires, sending, bufs, project_down, lambda name: None)
    for h in range(2):
        out_ref[:, columns(h)] = (state[:, columns(h)].astype(jnp.float32) + down[h]).astype(jnp.bfloat16)
    for wires in (gather_wires, down_wires, weight_wires):
        wires.drain()


def finish(tokens, attn, gain, w_out, w_out_other, w_gate, w_up, w_down, landed_g):
    rows, width = tokens.shape
    hidden = w_gate.shape[0]
    vmem = pl.BlockSpec(memory_space=pltpu.VMEM)
    hbm = pl.BlockSpec(memory_space=pl.ANY)
    wide, narrow = column_halves(width)
    bf16 = jnp.bfloat16
    return pl.pallas_call(
        finish_kernel,
        out_shape=jax.ShapeDtypeStruct((rows, width), bf16),
        in_specs=[vmem] * 3 + [hbm] * 6,
        out_specs=vmem,
        scratch_shapes=[
            pltpu.VMEM((2 * w_out.shape[0], width), bf16),
            *[pltpu.VMEM((hidden, width), bf16)] * 6,
            pltpu.VMEM((SIDE, 2, rows, wide), bf16),
            pltpu.VMEM((SIDE, 2, rows, narrow), bf16),
            pltpu.VMEM((SIDE, 2, rows, hidden), bf16),
            pltpu.VMEM((SIDE, 2, rows, hidden), bf16),
            pltpu.VMEM((SIDE, 2, rows, wide), bf16),
            pltpu.VMEM((SIDE, 2, rows, narrow), bf16),
            pltpu.VMEM((2, 2, rows // 2, wide), bf16),
            pltpu.VMEM((2, 2, rows, wide), bf16),
            pltpu.VMEM((rows, wide), bf16),
            pltpu.VMEM((SIDE, rows, narrow), bf16),
            pltpu.VMEM((2, rows // 2, narrow), bf16),
            pltpu.VMEM((2, rows, narrow), bf16),
            pltpu.VMEM((rows, width), bf16),
            pltpu.SemaphoreType.DMA((6,)),
            pltpu.SemaphoreType.DMA((4, 48)),
            pltpu.SemaphoreType.DMA((4, 48)),
        ],
        compiler_params=pltpu.CompilerParams(
            collective_id=1, has_side_effects=True, vmem_limit_bytes=60 << 20
        ),
        name="finish",
    )(tokens, attn, gain, w_out, w_out_other, w_gate, w_up, w_down, landed_g)


def serve_kernel(
    q_ref, own_ref, first_ref, spot_ref, wo_hbm, landed_o, o_ref, wo_other,
    held, peak, total, summed, send_sems, recv_sems, weight_send, weight_recv, landed_sem,
):
    z, x, y, core = place()
    mine = lax.rem(lax.div(x + 1, 2), 2)
    theirs = 1 - mine
    base = 1 - core
    rows = q_ref.shape[2]
    width = own_ref.shape[4]
    heads = q_ref.shape[3] // width
    factor = math.log2(math.e) / math.sqrt(width)
    across, ahead, other_core = holder(), along_y(1), twin()
    neighbours = greet()
    held[base, mine] = own_ref[...]
    meet(neighbours)
    started = []
    weight_wires = Wires(weight_send, weight_recv)
    fetch_o = Fetch(weight_wires, "o", wo_hbm, wo_other, True, 0, landed_o, landed_sem.at[0])

    def send(g, c, target, device):
        made = pltpu.make_async_remote_copy(
            src_ref=held.at[g, c],
            dst_ref=held.at[target, c],
            send_sem=send_sems.at[len(started)],
            recv_sem=recv_sems.at[target, c],
            device_id=device,
            device_id_type=MESH,
        )
        made.start()
        started.append(True)

    def arrive(g, c):
        pltpu.make_async_remote_copy(
            src_ref=held.at[g, c],
            dst_ref=held.at[g, c],
            send_sem=send_sems.at[0],
            recv_sem=recv_sems.at[g, c],
            device_id=across,
            device_id_type=MESH,
        ).wait_recv()

    send(base, mine, base, across)
    send(base, mine, base + 2, ahead)
    send(base, mine, base, other_core)
    peak[...] = jnp.full(peak.shape, NEGATIVE, jnp.float32)
    total[...] = jnp.zeros(total.shape, jnp.float32)
    summed[...] = jnp.zeros(summed.shape, jnp.float32)

    in_run = lax.broadcasted_iota(jnp.int32, (1, 2 * rows), 1)
    later = (in_run >= rows).astype(jnp.int32)

    def column(ref, zz):
        return jnp.concatenate([ref[zz]] * heads, axis=0)

    def step(tiles, g, c, back, causal):
        run = 2 * rows
        shift = (back - 2 * y - core) * (SIDE * SIDE * rows)
        held_before = [(peak[zz], total[zz], summed[zz]) for zz, _, _ in tiles]
        scored = []
        for zz, begin, size in tiles:
            tile = [q_ref[zz, :, :, h * width : (h + 1) * width].reshape(run, width) for h in range(heads)]
            query = jnp.concatenate(tile, axis=0)
            keys = held[g, c, 0, begin : begin + size].reshape(size * run, width)
            scored.append(
                lax.dot_general(query, keys, (((1,), (1,)), ((), ())), preferred_element_type=jnp.float32)
            )
        after = []
        for (zz, begin, size), scores, (old, sums, outs) in zip(tiles, scored, held_before):
            low, high = column(first_ref, zz) + shift, column(spot_ref, zz) + shift
            parts = []
            for run_at in range(size):
                spots = in_run + c * (rows - 2 * rows * later) + later * (SIDE - 2) * rows
                spots = spots + (begin + run_at) * (SIDE * rows)
                seen = spots >= low
                if causal:
                    seen = seen & (spots <= high)
                parts.append(jnp.where(seen, scores[:, run_at * run : (run_at + 1) * run], NEGATIVE))
            top = functools.reduce(jnp.maximum, parts)
            new = jnp.maximum(old, jnp.broadcast_to(jnp.max(top, axis=1, keepdims=True) * factor, old.shape))
            decay = jnp.exp2(old - new)
            parts = [jnp.exp2(part * factor - new) for part in parts]
            weights = jnp.concatenate([part.astype(jnp.bfloat16) for part in parts], axis=1)
            values = held[g, c, 1, begin : begin + size].reshape(size * run, width)
            outs = outs * decay + jnp.dot(weights, values, preferred_element_type=jnp.float32)
            after.append((new, sums * decay + functools.reduce(jnp.add, parts), outs))
        for (zz, _, _), state in zip(tiles, after):
            peak[zz], total[zz], summed[zz] = state

    def own_block(c):
        for pair in ((0, 3), (1, 2)):
            step([(zz, 0, zz + 1) for zz in pair], base, c, 0, True)

    def far_block(c):
        for pair in ((0, 3), (1, 2)):
            step([(zz, zz, SIDE - zz) for zz in pair], base + 4, c, 4, False)

    def per_class(work):
        def one(i, carry):
            work(mine + i * (theirs - mine))
            return carry

        return one

    def first_class(i, carry):
        @pl.when(i == 1)
        def _():
            arrive(base, theirs)
            send(base, theirs, base, other_core)
            arrive(base + 2, mine)
            send(base + 2, mine, base + 4, ahead)
            send(base + 2, mine, base + 2, across)
            send(base + 2, mine, base + 2, other_core)

        own_block(mine + i * (theirs - mine))
        return carry

    lax.fori_loop(0, 2, first_class, 0)
    fetch_o.relay()

    def middle(stage, carry):
        final = lax.div(stage, 4)
        back = (1 - final) * (1 + lax.rem(stage, 2)) + 3 * final
        c = mine + ((1 - final) * lax.div(stage, 2) + final * (stage - 4)) * (theirs - mine)

        @pl.when(stage == 2)
        def _():
            arrive(base + 2, theirs)
            send(base + 2, theirs, base + 2, other_core)
            arrive(base + 4, mine)
            send(base + 4, mine, base + 4, across)
            send(base + 4, mine, base + 4, other_core)

        @pl.when(stage == 4)
        def _():
            arrive(base + 4, theirs)
            send(base + 4, theirs, base + 4, other_core)

        @pl.when(back != 2)
        def _():
            arrive(base + back, c)

        def over_runs(pair, inner):
            step([(2 * pair + i, 0, SIDE) for i in range(2)], base + back, c, back, False)
            return inner

        return lax.fori_loop(0, SIDE // 2, over_runs, carry)

    lax.fori_loop(0, 4, middle, 0)
    fetch_o.pass_on()
    lax.fori_loop(4, 6, middle, 0)
    fetch_o.settle()
    lax.fori_loop(0, 2, per_class(far_block), 0)
    spare = core * 5
    arrive(spare, 0)
    arrive(spare, 1)
    fetch_o.finish()
    weight_wires.drain()
    for zz in range(SIDE):
        answer = (summed[zz] / jnp.sum(total[zz], axis=1, keepdims=True)).astype(jnp.bfloat16)
        for h in range(heads):
            piece = answer[h * 2 * rows : (h + 1) * 2 * rows]
            o_ref[zz, :, :, h * width : (h + 1) * width] = piece.reshape(2, rows, width)
    for number in range(len(started)):
        pltpu.make_async_remote_copy(
            src_ref=held.at[0, 0],
            dst_ref=held.at[0, 0],
            send_sem=send_sems.at[number],
            recv_sem=recv_sems.at[0, 0],
            device_id=across,
            device_id_type=MESH,
        ).wait_send()


def serve(queries, own, first, spots, w_out, landed_o):
    rows = queries.shape[2]
    width = own.shape[4]
    heads = queries.shape[3] // width
    tall = heads * 2 * rows
    vmem = pl.BlockSpec(memory_space=pltpu.VMEM)
    hbm = pl.BlockSpec(memory_space=pl.ANY)
    return pl.pallas_call(
        serve_kernel,
        out_shape=(
            jax.ShapeDtypeStruct(queries.shape, jnp.bfloat16),
            jax.ShapeDtypeStruct(w_out.shape, jnp.bfloat16),
        ),
        in_specs=[vmem] * 4 + [hbm] * 2,
        out_specs=(vmem, hbm),
        scratch_shapes=[
            pltpu.VMEM((6, 2, *own.shape), jnp.bfloat16),
            pltpu.VMEM((SIDE, tall, 2 * rows), jnp.float32),
            pltpu.VMEM((SIDE, tall, 2 * rows), jnp.float32),
            pltpu.VMEM((SIDE, tall, width), jnp.float32),
            pltpu.SemaphoreType.DMA((11,)),
            pltpu.SemaphoreType.DMA((6, 2)),
            pltpu.SemaphoreType.DMA((12,)),
            pltpu.SemaphoreType.DMA((12,)),
            pltpu.SemaphoreType.DMA((1,)),
        ],
        compiler_params=pltpu.CompilerParams(
            collective_id=2, has_side_effects=True, vmem_limit_bytes=40 << 20
        ),
        name="serve",
    )(queries, own, first, spots, w_out, landed_o)


def body(tokens, doc_lengths, attn_gain, mlp_gain, w_query, w_keyval, w_out, w_gate, w_up, w_down):
    token_index = lax.axis_index("token")
    x = lax.axis_index("tensor") % SIDE
    rows = tokens.shape[0]
    qblk = 2 * rows
    block_rows = rows * SIDE * SIDE
    outer = (x == 0) | (x == SIDE - 1)
    lows, highs = jnp.where(outer, 0, 1), jnp.where(outer, SIDE - 1, SIDE - 2)
    runs = token_index * block_rows + jnp.arange(SIDE, dtype=jnp.int32) * (SIDE * rows)
    blocks = runs[:, None] + jnp.stack([lows, highs])[None, :] * rows
    spots = (blocks[:, :, None] + jnp.arange(rows, dtype=jnp.int32)).reshape(-1).astype(jnp.int32)
    first = jnp.zeros_like(spots)
    end = jnp.int32(0)
    for document in range(doc_lengths.shape[0] - 1):
        end = end + doc_lengths[document]
        first = jnp.where(spots >= end, end, first)
    position = (spots - first).astype(jnp.float32)
    half = HEAD_DIM // 2
    freq = jnp.exp(-math.log(ROPE_BASE) * jnp.arange(half, dtype=jnp.float32) * (2.0 / HEAD_DIM))
    angle = position[:, None] * freq[None, :]
    cosine, sine = jnp.cos(angle), jnp.sin(angle)
    cosine = jnp.concatenate([cosine, cosine], axis=1).reshape(SIDE, 2, rows, HEAD_DIM)
    sine = jnp.concatenate([-sine, sine], axis=1).reshape(SIDE, 2, rows, HEAD_DIM)
    gates = w_gate.T
    queries, own, landed_o, landed_g = project(
        tokens, attn_gain[None, :], cosine, sine, w_query, w_keyval, w_out, gates
    )
    first, spots = first.reshape(SIDE, qblk, 1), spots.reshape(SIDE, qblk, 1)
    attn, w_out_other = serve(queries, own, first, spots, w_out, landed_o)
    return finish(tokens, attn, mlp_gain[None, :], w_out, w_out_other, gates, w_up.T, w_down, landed_g)


def solution(mesh):
    return jax.shard_map(
        body,
        mesh=mesh,
        in_specs=(
            P(("token", "tensor"), None),
            P(),
            P(),
            P(),
            P(None, "tensor"),
            P(None, "tensor"),
            P("tensor", None),
            P(None, "tensor"),
            P(None, "tensor"),
            P("tensor", None),
        ),
        out_specs=P(("token", "tensor"), None),
        check_vma=False,
    )
```

```python
import functools
import math

import jax
import jax.numpy as jnp
from jax import lax
from jax.experimental import pallas as pl
from jax.experimental.pallas import tpu as pltpu
from jax.sharding import PartitionSpec as P

HEAD_DIM = 128
SIDE = 4
CORES = 2
YS = 4

EPSILON = 1e-05
ROPE_BASE = 500000.0
NEGATIVE = -1e30
MESH = pl.DeviceIdType.MESH


def place():
    me, token = lax.axis_index("tensor"), lax.axis_index("token")
    return me // SIDE, me % SIDE, token // CORES, token % CORES


def along_z(step):
    z, x, _, _ = place()
    return {"tensor": ((z + step + SIDE) % SIDE) * SIDE + x}


def mate():
    z, x, _, _ = place()
    return {"tensor": z * SIDE + SIDE - 1 - x}


def holder():
    z, x, _, _ = place()
    return {"tensor": z * SIDE + x + 1 - 2 * (x % 2)}


def along_y(step):
    _, _, y, core = place()
    return {"token": ((y + step + YS) % YS) * CORES + core}


def twin():
    _, _, y, core = place()
    return {"token": y * CORES + 1 - core}


def greet():
    others = [along_z(1), along_z(-1), mate(), holder(), along_y(1), along_y(-1), twin()]
    for other in others:
        pl.semaphore_signal(pltpu.get_barrier_semaphore(), inc=1, device_id=other, device_id_type=MESH)
    return len(others)


def meet(others):
    pl.semaphore_wait(pltpu.get_barrier_semaphore(), others)


def row_class(x):
    return lax.rem(lax.div(x + 1, 2), 2)


def document_start(doc_ref, spots):
    first, end = jnp.zeros_like(spots), 0
    for document in range(doc_ref.shape[0] - 1):
        end = end + doc_ref[document]
        first = jnp.where(spots >= end, end, first)
    return first


def column_halves(width):
    first = width * 9 // 16
    return first, width - first


class Wires:
    def __init__(self, send_sems, recv_sems):
        self.send_sems, self.recv_sems, self.slots, self.started = send_sems, recv_sems, {}, []

    def copy(self, key, src, dst, device):
        slot = self.slots.setdefault(key, len(self.slots))
        return pltpu.make_async_remote_copy(
            src_ref=src,
            dst_ref=dst,
            send_sem=self.send_sems.at[slot],
            recv_sem=self.recv_sems.at[slot],
            device_id=device,
            device_id_type=MESH,
        )

    def start(self, key, src, dst, device):
        made = self.copy(key, src, dst, device)
        made.start()
        self.started.append(made)

    def arrive(self, key, dst, device):
        self.copy(key, dst, dst, device).wait_recv()

    def drain(self):
        for made in self.started:
            made.wait_send()
        self.started = []


class Fetch:
    def __init__(self, wires, name, src, dst, lanes, first_lane=0, landed=None, landed_sem=None):
        self.wires, self.name, self.src, self.dst, self.lanes, self.first_lane = wires, name, src, dst, lanes, first_lane
        self.landed, self.kept = landed, None
        if landed is not None:
            self.kept = pltpu.make_async_copy(landed, self.dst_slot(dst), landed_sem)

    @property
    def size(self):
        return self.src.shape[1 if self.lanes else 0] // (YS * CORES)

    def dst_slot(self, ref):
        _, _, y, core = place()
        return self.cut(ref, y * CORES + core, None, self.first_lane)

    def cut(self, ref, number, part, offset):
        size = self.size if part is None else self.size // 2
        start = pl.multiple_of(number * self.size, self.size) + (0 if part in (None, 0) else size)
        start = pl.multiple_of(start, size)
        if self.lanes:
            return ref.at[:, pl.ds(start, size)]
        return ref.at[pl.ds(start, size), pl.ds(offset, self.src.shape[1])]

    def slot(self, dy, dc, part=None):
        _, _, y, core = place()
        number = ((y + dy + YS) % YS) * CORES + (core if dc == 0 else 1 - core)
        return self.cut(self.dst, number, part, self.first_lane)

    def start(self, key, ref, device):
        self.wires.start((self.name, key), ref, ref, device)

    def arrive(self, key, ref):
        self.wires.arrive((self.name, key), ref, holder())

    def ask(self):
        _, _, y, core = place()
        self.wires.start((self.name, "x"), self.cut(self.src, y * CORES + core, None, 0), self.slot(0, 0), holder())

    def land(self, landed):
        self.wires.start((self.name, "x"), self.dst_slot(self.src), landed, holder())

    def relay(self):
        source = self.landed
        if source is None:
            source = self.slot(0, 0)
            self.arrive("x", source)
        else:
            self.kept.start()
        for key, device in (("y3", along_y(1)), ("y1", along_y(-1)), ("c0", twin())):
            self.wires.start((self.name, key), source, self.slot(0, 0), device)

    def pass_on(self):
        self.arrive("y3", self.slot(3, 0))
        self.start("h0", self.slot(3, 0, 0), along_y(1))
        self.start("c3", self.slot(3, 0), twin())
        self.arrive("y1", self.slot(1, 0))
        self.start("h1", self.slot(1, 0, 1), along_y(-1))
        self.start("c1", self.slot(1, 0), twin())

    def settle(self):
        self.arrive("h0", self.slot(2, 0, 0))
        self.arrive("h1", self.slot(2, 0, 1))
        self.start("c2", self.slot(2, 0), twin())

    def finish(self):
        for dy in (0, 3, 1, 2):
            self.arrive("c%d" % dy, self.slot(dy, 1))
        if self.kept is not None:
            self.kept.wait()


def gather(wires, blocks, hook):
    rows = blocks[0].shape[2]
    low, high = pl.ds(0, rows // 2), pl.ds(rows // 2, rows // 2)
    up, down = 1, -1

    def full(h, dz, m):
        return blocks[h].at[dz, m]

    def spread(h, m):
        wires.start(("s", h, 3, m), full(h, 0, m), full(h, 3, m), along_z(up))
        wires.start(("s", h, 1, m), full(h, 0, m), full(h, 1, m), along_z(down))

    def to_mate(h, dz):
        wires.start(("m", h, dz), full(h, dz, 0), full(h, dz, 1), mate())

    def relay(h, m, onward):
        wires.arrive(("s", h, 3, m), full(h, 3, m), along_z(down))
        wires.start(("t", h, 0, m), blocks[h].at[3, m, low], blocks[h].at[2, m, low], along_z(up))
        if onward:
            to_mate(h, 3)
        wires.arrive(("s", h, 1, m), full(h, 1, m), along_z(up))
        wires.start(("t", h, 1, m), blocks[h].at[1, m, high], blocks[h].at[2, m, high], along_z(down))
        if onward:
            to_mate(h, 1)

    def last(h, m):
        wires.arrive(("t", h, 0, m), blocks[h].at[2, m, low], along_z(down))
        wires.arrive(("t", h, 1, m), blocks[h].at[2, m, high], along_z(up))

    to_mate(0, 0)
    spread(1, 0)
    spread(0, 0)
    to_mate(1, 0)
    hook("sent")
    wires.arrive(("m", 0, 0), full(0, 0, 1), mate())
    spread(0, 1)
    relay(1, 0, True)
    hook("one")
    relay(0, 0, False)
    wires.arrive(("m", 1, 0), full(1, 0, 1), mate())
    hook("own pair")
    last(1, 0)
    to_mate(1, 2)
    hook("two")
    relay(0, 1, False)
    hook("three")
    wires.arrive(("m", 1, 3), full(1, 3, 1), mate())
    wires.arrive(("m", 1, 1), full(1, 1, 1), mate())
    hook("sides")
    last(0, 0)
    last(0, 1)
    wires.arrive(("m", 1, 2), full(1, 2, 1), mate())
    hook("far")


def scatter(wires, out, bufs, produce, hook):
    z_half, z_full, mate0, mate1, e_half, e_full = bufs
    rows = out[0].shape[2]
    low, high = pl.ds(0, rows // 2), pl.ds(rows // 2, rows // 2)
    ways = ((0, 1, low, 1), (1, 3, high, -1))
    f32 = jnp.float32

    def wide(ref):
        return ref[...].astype(f32)

    def add_to(ref, *others):
        total = wide(ref)
        for other in others:
            total = total + wide(other)
        ref[...] = total.astype(ref.dtype)

    def mate_send(dz):
        wires.start(("m1", dz), out[1].at[dz, 1], mate1.at[dz], mate())

    def mate_join(dz):
        wires.arrive(("m1", dz), mate1.at[dz], mate())
        add_to(out[1].at[dz, 0], mate1.at[dz])

    produce(1, (2,))
    mate_send(2)
    produce(0, (2,))
    for m in (1, 0):
        for way, dz, part, step in ways:
            wires.start(("a", way, m), out[0].at[2, m, part], z_half.at[way, m], along_z(step))
    hook("begun")
    produce(0, (1, 3))
    produce(1, (1, 3))
    mate_send(1)
    mate_send(3)
    mate_join(2)
    for way, dz, part, step in ways:
        wires.start(("e", way), out[1].at[2, 0, part], e_half.at[way], along_z(step))
    for m in (1, 0):
        for way, dz, part, step in ways:
            wires.arrive(("a", way, m), z_half.at[way, m], along_z(-step))
            add_to(out[0].at[dz, m, part], z_half.at[way, m])
            wires.start(("b", way, m), out[0].at[dz, m], z_full.at[way, m], along_z(step))
    produce(1, (0,))
    mate_send(0)
    produce(0, (0,))
    hook("early")
    for way, dz, part, step in ways:
        mate_join(dz)
        wires.arrive(("e", way), e_half.at[way], along_z(-step))
        add_to(out[1].at[dz, 0, part], e_half.at[way])
        wires.start(("f", way), out[1].at[dz, 0], e_full.at[way], along_z(step))
    hook("middle")
    for way, dz, part, step in ways:
        wires.arrive(("b", way, 1), z_full.at[way, 1], along_z(-step))
    add_to(out[0].at[0, 1], z_full.at[0, 1], z_full.at[1, 1])
    wires.start(("m0",), out[0].at[0, 1], mate0, mate())
    hook("late")
    for way, dz, part, step in ways:
        wires.arrive(("b", way, 0), z_full.at[way, 0], along_z(-step))
    first = wide(out[0].at[0, 0]) + wide(z_full.at[0, 0]) + wide(z_full.at[1, 0])
    wires.arrive(("m1", 0), mate1.at[0], mate())
    second = wide(out[1].at[0, 0]) + wide(mate1.at[0])
    for way, dz, part, step in ways:
        wires.arrive(("f", way), e_full.at[way], along_z(-step))
        second = second + wide(e_full.at[way])
    wires.arrive(("m0",), mate0, mate())
    first = first + wide(mate0)
    return first, second


def norm_halves(rows, gain):
    mean_square = jnp.mean(rows * rows, axis=-1, keepdims=True)
    normed = (rows * lax.rsqrt(mean_square + EPSILON) * gain).astype(jnp.bfloat16)
    width, _ = column_halves(rows.shape[1])
    return normed[:, :width], normed[:, width:]


def stacked(blocks, h, dzs):
    _, _, rows, width = blocks[h].shape
    parts = [blocks[h][dz].reshape(2 * rows, width) for dz in dzs]
    return parts[0] if len(parts) == 1 else jnp.concatenate(parts, axis=0)


def project_kernel(
    tokens_hbm, gain_ref, doc_ref, wq_hbm, wkv_hbm, wo_hbm, wg_hbm, q_ref, kv_ref, landed_o, landed_g,
    tokens_ref, cos_ref, sin_ref, weights, others, blocks0, blocks1, load_sems, send_sems, recv_sems,
):
    blocks, rows = (blocks0, blocks1), blocks0.shape[2]
    split, width = blocks0.shape[3], weights.shape[0]
    arriving = pltpu.make_async_copy(tokens_hbm, tokens_ref, load_sems.at[2])
    arriving.start()
    neighbours = greet()
    qcols = wq_hbm.shape[1]
    cols = qcols + wkv_hbm.shape[1]
    z, x, y, core = place()
    mine, token = row_class(x), y * CORES + core
    loads = [
        pltpu.make_async_copy(wq_hbm, weights.at[:, pl.ds(0, qcols)], load_sems.at[0]),
        pltpu.make_async_copy(wkv_hbm, weights.at[:, pl.ds(qcols, cols - qcols)], load_sems.at[1]),
    ]
    for load in loads:
        load.start()
    arriving.wait()
    blocks0[0, 0], blocks1[0, 0] = norm_halves(tokens_ref[...].astype(jnp.float32), gain_ref[...])
    meet(neighbours)
    wires = Wires(send_sems, recv_sems)

    def angles(number, carry):
        run, m = lax.div(number, 2), lax.rem(number, 2)
        at_x = mine + m * (SIDE - 1 - 2 * mine)
        shape = (rows, HEAD_DIM)
        spots = lax.broadcasted_iota(jnp.int32, shape, 0) + ((token * SIDE + run) * SIDE + at_x) * rows
        position = (spots - document_start(doc_ref, spots)).astype(jnp.float32)
        lane = lax.broadcasted_iota(jnp.int32, shape, 1)
        upper = lane >= HEAD_DIM // 2
        pair = jnp.where(upper, lane - HEAD_DIM // 2, lane).astype(jnp.float32)
        angle = position * jnp.exp(-math.log(ROPE_BASE) * pair * (2.0 / HEAD_DIM))
        sine = jnp.sin(angle)
        cos_ref[number] = jnp.cos(angle)
        sin_ref[number] = jnp.where(upper, sine, -sine)
        return carry
    fetch_q = Fetch(wires, "q", wq_hbm, others, False, 0)
    fetch_kv = Fetch(wires, "kv", wkv_hbm, others, False, qcols)
    fetch_o = Fetch(wires, "o", wo_hbm, None, True)
    fetch_g = Fetch(wires, "g", wg_hbm, None, True)

    def emit(dzs, mine):
        shard = weights if mine else others
        part = sum(
            jnp.dot(
                stacked(blocks, h, dzs),
                shard[slice(0, split) if h == 0 else slice(split, width), :],
                preferred_element_type=jnp.float32,
            )
            for h in range(2)
        )
        is_key = (x % 2 == 0) if mine else (x % 2 == 1)
        which = x % 2 if mine else 1 - x % 2
        first_col = 0 if mine else qcols
        for i, dz in enumerate(dzs):
            for m in range(2):
                whole = part[(2 * i + m) * rows : (2 * i + m + 1) * rows]
                zz = (z + dz) % SIDE
                mm = x // 2 if m == 0 else 1 - x // 2
                cosine, sine = cos_ref[2 * zz + mm], sin_ref[2 * zz + mm]
                for head in range(qcols // HEAD_DIM):
                    piece = whole[:, head * HEAD_DIM : (head + 1) * HEAD_DIM]
                    turned = piece * cosine + pltpu.roll(piece, HEAD_DIM // 2, 1) * sine
                    at = first_col + head * HEAD_DIM
                    q_ref[zz, mm, :, at : at + HEAD_DIM] = turned.astype(jnp.bfloat16)
                piece = whole[:, qcols:]
                turned = piece * cosine + pltpu.roll(piece, HEAD_DIM // 2, 1) * sine
                kv_ref[which, zz, mm] = jnp.where(is_key, turned, piece).astype(jnp.bfloat16)

    def hook(name):
        if name == "sent":
            fetch_q.ask()
            fetch_kv.ask()
            fetch_o.land(landed_o)
            fetch_g.land(landed_g)
            lax.fori_loop(0, 2 * SIDE, angles, 0)
        elif name == "one":
            fetch_q.relay()
            fetch_kv.relay()
            for load in loads:
                load.wait()
        elif name == "own pair":
            emit((0,), True)
        elif name == "two":
            fetch_q.pass_on()
        elif name == "three":
            fetch_kv.pass_on()
            fetch_q.settle()
        elif name == "sides":
            emit((3, 1), True)
            fetch_kv.settle()
            fetch_q.finish()
            fetch_kv.finish()
            emit((0,), False)
            emit((3, 1), False)
        else:
            emit((2,), True)
            emit((2,), False)

    gather(wires, blocks, hook)
    wires.arrive(("o", "x"), landed_o, holder())
    wires.arrive(("g", "x"), landed_g, holder())
    wires.drain()


def project(tokens, gain, doc_lengths, w_query, w_keyval, w_out, w_gate):
    rows, width = tokens.shape
    cols = w_query.shape[1] + w_keyval.shape[1]
    vmem = pl.BlockSpec(memory_space=pltpu.VMEM)
    hbm = pl.BlockSpec(memory_space=pl.ANY)
    bf16 = jnp.bfloat16
    return pl.pallas_call(
        project_kernel,
        out_shape=(
            jax.ShapeDtypeStruct((SIDE, 2, rows, 2 * w_query.shape[1]), bf16),
            jax.ShapeDtypeStruct((2, SIDE, 2, rows, w_keyval.shape[1]), bf16),
            jax.ShapeDtypeStruct((w_out.shape[0], w_out.shape[1] // (YS * CORES)), bf16),
            jax.ShapeDtypeStruct((w_gate.shape[0], w_gate.shape[1] // (YS * CORES)), bf16),
        ),
        in_specs=[hbm, vmem, pl.BlockSpec(memory_space=pltpu.SMEM)] + [hbm] * 4,
        out_specs=(vmem, vmem, hbm, hbm),
        scratch_shapes=[
            pltpu.VMEM((rows, width), bf16),
            pltpu.VMEM((2 * SIDE, rows, HEAD_DIM), jnp.float32),
            pltpu.VMEM((2 * SIDE, rows, HEAD_DIM), jnp.float32),
            pltpu.VMEM((width, cols), bf16),
            pltpu.VMEM((width, cols), bf16),
            *[pltpu.VMEM((SIDE, 2, rows, part), bf16) for part in column_halves(width)],
            pltpu.SemaphoreType.DMA((3,)),
            pltpu.SemaphoreType.DMA((64,)),
            pltpu.SemaphoreType.DMA((64,)),
        ],
        compiler_params=pltpu.CompilerParams(
            collective_id=0, has_side_effects=True, vmem_limit_bytes=60 << 20
        ),
        name="project",
    )(tokens, gain, doc_lengths, w_query, w_keyval, w_out, w_gate)


def finish_kernel(
    tokens_hbm, attn_hbm, gain_ref, wo_hbm, wo2_hbm, wg_hbm, wu_hbm, wd_hbm, landed_g, out_ref,
    tokens_ref, attn_ref, wo, wg, wu, wd, wg2, wu2, wd2, blocks0, blocks1, hidden, hidden2, sending0, sending1,
    z_half, z_full, mate0, mate1, e_half, e_full, state, load_sems, send_sems, recv_sems,
):
    blocks, sending = (blocks0, blocks1), (sending0, sending1)
    _, _, rows, split = blocks0.shape
    width = wo.shape[1]
    neighbours = greet()
    own = wo_hbm.shape[0]
    z, x, _, _ = place()
    loads = [
        pltpu.make_async_copy(src, dst, load_sems.at[i])
        for i, (src, dst) in enumerate(
            ((wo_hbm, wo.at[pl.ds(0, own)]), (wo2_hbm, wo.at[pl.ds(own, own)]), (wg_hbm, wg), (wu_hbm, wu), (wd_hbm, wd))
        )
    ]
    arriving = [
        pltpu.make_async_copy(attn_hbm, attn_ref, load_sems.at[6]),
        pltpu.make_async_copy(tokens_hbm, tokens_ref, load_sems.at[7]),
    ]
    for load in arriving[:1] + loads[:2] + arriving[1:]:
        load.start()
    meet(neighbours)
    for load in arriving:
        load.wait()
    bufs = (z_half, z_full, mate0, mate1, e_half, e_full)
    weight_wires = Wires(send_sems.at[3], recv_sems.at[3])
    fetch_g = Fetch(weight_wires, "g", wg_hbm, wg2, True, 0, landed_g, load_sems.at[5])
    fetch_u = Fetch(weight_wires, "u", wu_hbm, wu2, True)
    fetch_d = Fetch(weight_wires, "d", wd_hbm, wd2, True)
    loads[0].wait()
    loads[1].wait()

    def columns(h):
        return pl.ds(0, split) if h == 0 else pl.ds(split, width - split)

    def keep(h, dzs, part):
        for i, dz in enumerate(dzs):
            piece = part[2 * i * rows : 2 * (i + 1) * rows].astype(jnp.bfloat16)
            sending[h][dz] = piece.reshape(2, rows, piece.shape[1])

    def project_out(h, dzs):
        mine, other = x // 2, 1 - x // 2
        left = [attn_ref[(z + dz) % SIDE, m] for dz in dzs for m in (mine, other)]
        left = jnp.concatenate(left, axis=0)
        keep(h, dzs, jnp.dot(left, wo[:, columns(h)], preferred_element_type=jnp.float32))

    def hook_out(name):
        if name == "begun":
            for load in loads[2:]:
                load.start()
            fetch_g.relay()
            fetch_u.ask()
            fetch_d.ask()
        elif name == "early":
            fetch_g.pass_on()
            fetch_u.relay()
        elif name == "late":
            fetch_g.settle()
            fetch_d.relay()

    out_wires = Wires(send_sems.at[0], recv_sems.at[0])
    first, second = scatter(out_wires, sending, bufs, project_out, hook_out)
    for h, proj in enumerate((first, second)):
        state[:, columns(h)] = (tokens_ref[:, columns(h)].astype(jnp.float32) + proj).astype(jnp.bfloat16)
    blocks0[0, 0], blocks1[0, 0] = norm_halves(state[...].astype(jnp.float32), gain_ref[...])

    def gated(dzs, mine):
        gates, ups, result = (wg, wu, hidden) if mine else (wg2, wu2, hidden2)
        gate = upward = 0.0
        for h in range(2):
            left = stacked(blocks, h, dzs)
            across = (((1,), (1,)), ((), ()))
            gate = gate + lax.dot_general(left, gates[:, columns(h)], across, preferred_element_type=jnp.float32)
            upward = upward + lax.dot_general(left, ups[:, columns(h)], across, preferred_element_type=jnp.float32)
        value = (gate / (1.0 + jnp.exp(-gate)) * upward).astype(jnp.bfloat16)
        for i, dz in enumerate(dzs):
            result[dz] = value[2 * i * rows : 2 * (i + 1) * rows].reshape(2, rows, value.shape[1])

    def hook_gated(name):
        if name == "sent":
            loads[2].wait()
            loads[3].wait()
            fetch_u.pass_on()
        elif name == "one":
            fetch_g.finish()
            fetch_d.pass_on()
        elif name == "own pair":
            gated((0,), True)
            fetch_u.settle()
        elif name == "three":
            fetch_d.settle()
        elif name == "sides":
            gated((3, 1), True)
            fetch_u.finish()
            gated((0,), False)
            gated((3, 1), False)
        elif name == "far":
            gated((2,), True)
            gated((2,), False)
            fetch_d.finish()
            loads[4].wait()

    gather_wires = Wires(send_sems.at[1], recv_sems.at[1])
    gather(gather_wires, blocks, hook_gated)
    out_wires.drain()

    def project_down(h, dzs):
        part = 0.0
        for values, weights in ((hidden, wd), (hidden2, wd2)):
            left = [values[dz].reshape(2 * rows, values.shape[3]) for dz in dzs]
            left = left[0] if len(left) == 1 else jnp.concatenate(left, axis=0)
            part = part + jnp.dot(left, weights[:, columns(h)], preferred_element_type=jnp.float32)
        keep(h, dzs, part)

    down_wires = Wires(send_sems.at[2], recv_sems.at[2])
    down = scatter(down_wires, sending, bufs, project_down, lambda name: None)
    for h in range(2):
        out_ref[:, columns(h)] = (state[:, columns(h)].astype(jnp.float32) + down[h]).astype(jnp.bfloat16)
    for wires in (gather_wires, down_wires, weight_wires):
        wires.drain()


def finish(tokens, attn, gain, w_out, w_out_other, w_gate, w_up, w_down, landed_g):
    rows, width = tokens.shape
    hidden = w_gate.shape[0]
    vmem = pl.BlockSpec(memory_space=pltpu.VMEM)
    hbm = pl.BlockSpec(memory_space=pl.ANY)
    wide, narrow = column_halves(width)
    bf16 = jnp.bfloat16
    return pl.pallas_call(
        finish_kernel,
        out_shape=jax.ShapeDtypeStruct((rows, width), bf16),
        in_specs=[hbm] * 2 + [vmem] + [hbm] * 6,
        out_specs=vmem,
        scratch_shapes=[
            pltpu.VMEM((rows, width), bf16),
            pltpu.VMEM(attn.shape, bf16),
            pltpu.VMEM((2 * w_out.shape[0], width), bf16),
            *[pltpu.VMEM((hidden, width), bf16)] * 6,
            pltpu.VMEM((SIDE, 2, rows, wide), bf16),
            pltpu.VMEM((SIDE, 2, rows, narrow), bf16),
            pltpu.VMEM((SIDE, 2, rows, hidden), bf16),
            pltpu.VMEM((SIDE, 2, rows, hidden), bf16),
            pltpu.VMEM((SIDE, 2, rows, wide), bf16),
            pltpu.VMEM((SIDE, 2, rows, narrow), bf16),
            pltpu.VMEM((2, 2, rows // 2, wide), bf16),
            pltpu.VMEM((2, 2, rows, wide), bf16),
            pltpu.VMEM((rows, wide), bf16),
            pltpu.VMEM((SIDE, rows, narrow), bf16),
            pltpu.VMEM((2, rows // 2, narrow), bf16),
            pltpu.VMEM((2, rows, narrow), bf16),
            pltpu.VMEM((rows, width), bf16),
            pltpu.SemaphoreType.DMA((8,)),
            pltpu.SemaphoreType.DMA((4, 48)),
            pltpu.SemaphoreType.DMA((4, 48)),
        ],
        compiler_params=pltpu.CompilerParams(
            collective_id=1, has_side_effects=True, vmem_limit_bytes=60 << 20
        ),
        name="finish",
    )(tokens, attn, gain, w_out, w_out_other, w_gate, w_up, w_down, landed_g)


def serve_kernel(
    q_ref, own_ref, doc_ref, wo_hbm, landed_o, o_ref, wo_other,
    first_ref, spot_ref, held, peak, total, summed, send_sems, recv_sems, weight_send, weight_recv, landed_sem,
):
    z, x, y, core = place()
    mine = row_class(x)
    theirs = 1 - mine
    base = 1 - core
    rows = q_ref.shape[2]
    width = own_ref.shape[4]
    heads = q_ref.shape[3] // width
    factor = math.log2(math.e) / math.sqrt(width)
    across, ahead, other_core = holder(), along_y(1), twin()
    neighbours = greet()
    held[base, mine] = own_ref[...]
    meet(neighbours)
    started = []
    weight_wires = Wires(weight_send, weight_recv)
    fetch_o = Fetch(weight_wires, "o", wo_hbm, wo_other, True, 0, landed_o, landed_sem.at[0])

    def send(g, c, target, device):
        made = pltpu.make_async_remote_copy(
            src_ref=held.at[g, c],
            dst_ref=held.at[target, c],
            send_sem=send_sems.at[len(started)],
            recv_sem=recv_sems.at[target, c],
            device_id=device,
            device_id_type=MESH,
        )
        made.start()
        started.append(True)

    def arrive(g, c):
        pltpu.make_async_remote_copy(
            src_ref=held.at[g, c],
            dst_ref=held.at[g, c],
            send_sem=send_sems.at[0],
            recv_sem=recv_sems.at[g, c],
            device_id=across,
            device_id_type=MESH,
        ).wait_recv()

    send(base, mine, base, across)
    send(base, mine, base + 2, ahead)
    send(base, mine, base, other_core)
    peak[...] = jnp.full(peak.shape, NEGATIVE, jnp.float32)
    total[...] = jnp.zeros(total.shape, jnp.float32)
    summed[...] = jnp.zeros(summed.shape, jnp.float32)

    in_run = lax.broadcasted_iota(jnp.int32, (1, 2 * rows), 1)
    later = (in_run >= rows).astype(jnp.int32)

    def places(zz, carry):
        row = lax.broadcasted_iota(jnp.int32, first_ref.shape[1:], 0) & (2 * rows - 1)
        other = (row >= rows).astype(jnp.int32)
        spots = row + (mine - other + other * (SIDE - 1 - 2 * mine)) * rows
        spots = spots + ((2 * y + core) * SIDE + zz) * SIDE * rows
        spot_ref[zz] = spots
        first_ref[zz] = document_start(doc_ref, spots)
        return carry

    lax.fori_loop(0, SIDE, places, 0)

    def step(tiles, g, c, back, causal):
        run = 2 * rows
        shift = (back - 2 * y - core) * (SIDE * SIDE * rows)
        held_before = [(peak[zz], total[zz], summed[zz]) for zz, _, _ in tiles]
        scored = []
        for zz, begin, size in tiles:
            tile = [q_ref[zz, :, :, h * width : (h + 1) * width].reshape(run, width) for h in range(heads)]
            query = jnp.concatenate(tile, axis=0)
            keys = held[g, c, 0, begin : begin + size].reshape(size * run, width)
            scored.append(
                lax.dot_general(query, keys, (((1,), (1,)), ((), ())), preferred_element_type=jnp.float32)
            )
        after = []
        for (zz, begin, size), scores, (old, sums, outs) in zip(tiles, scored, held_before):
            low, high = first_ref[zz] + shift, spot_ref[zz] + shift
            parts = []
            for run_at in range(size):
                spots = in_run + c * (rows - 2 * rows * later) + later * (SIDE - 2) * rows
                spots = spots + (begin + run_at) * (SIDE * rows)
                seen = spots >= low
                if causal:
                    seen = seen & (spots <= high)
                parts.append(jnp.where(seen, scores[:, run_at * run : (run_at + 1) * run], NEGATIVE))
            top = functools.reduce(jnp.maximum, parts)
            new = jnp.maximum(old, jnp.broadcast_to(jnp.max(top, axis=1, keepdims=True) * factor, old.shape))
            decay = jnp.exp2(old - new)
            parts = [jnp.exp2(part * factor - new) for part in parts]
            weights = jnp.concatenate([part.astype(jnp.bfloat16) for part in parts], axis=1)
            values = held[g, c, 1, begin : begin + size].reshape(size * run, width)
            outs = outs * decay + jnp.dot(weights, values, preferred_element_type=jnp.float32)
            after.append((new, sums * decay + functools.reduce(jnp.add, parts), outs))
        for (zz, _, _), state in zip(tiles, after):
            peak[zz], total[zz], summed[zz] = state

    def own_block(c):
        for pair in ((0, 3), (1, 2)):
            step([(zz, 0, zz + 1) for zz in pair], base, c, 0, True)

    def far_block(c):
        for pair in ((0, 3), (1, 2)):
            step([(zz, zz, SIDE - zz) for zz in pair], base + 4, c, 4, False)

    def per_class(work):
        def one(i, carry):
            work(mine + i * (theirs - mine))
            return carry

        return one

    def first_class(i, carry):
        @pl.when(i == 1)
        def _():
            arrive(base, theirs)
            send(base, theirs, base, other_core)
            arrive(base + 2, mine)
            send(base + 2, mine, base + 4, ahead)
            send(base + 2, mine, base + 2, across)
            send(base + 2, mine, base + 2, other_core)

        own_block(mine + i * (theirs - mine))
        return carry

    lax.fori_loop(0, 2, first_class, 0)
    fetch_o.relay()

    def middle(stage, carry):
        final = lax.div(stage, 4)
        back = (1 - final) * (1 + lax.rem(stage, 2)) + 3 * final
        c = mine + ((1 - final) * lax.div(stage, 2) + final * (stage - 4)) * (theirs - mine)

        @pl.when(stage == 2)
        def _():
            arrive(base + 2, theirs)
            send(base + 2, theirs, base + 2, other_core)
            arrive(base + 4, mine)
            send(base + 4, mine, base + 4, across)
            send(base + 4, mine, base + 4, other_core)

        @pl.when(stage == 4)
        def _():
            arrive(base + 4, theirs)
            send(base + 4, theirs, base + 4, other_core)

        @pl.when(back != 2)
        def _():
            arrive(base + back, c)

        def over_runs(pair, inner):
            step([(2 * pair + i, 0, SIDE) for i in range(2)], base + back, c, back, False)
            return inner

        return lax.fori_loop(0, SIDE // 2, over_runs, carry)

    lax.fori_loop(0, 4, middle, 0)
    fetch_o.pass_on()
    lax.fori_loop(4, 6, middle, 0)
    fetch_o.settle()
    lax.fori_loop(0, 2, per_class(far_block), 0)
    spare = core * 5
    arrive(spare, 0)
    arrive(spare, 1)
    fetch_o.finish()
    weight_wires.drain()
    for zz in range(SIDE):
        answer = (summed[zz] / jnp.sum(total[zz], axis=1, keepdims=True)).astype(jnp.bfloat16)
        for h in range(heads):
            piece = answer[h * 2 * rows : (h + 1) * 2 * rows]
            o_ref[zz, :, :, h * width : (h + 1) * width] = piece.reshape(2, rows, width)
    for number in range(len(started)):
        pltpu.make_async_remote_copy(
            src_ref=held.at[0, 0],
            dst_ref=held.at[0, 0],
            send_sem=send_sems.at[number],
            recv_sem=recv_sems.at[0, 0],
            device_id=across,
            device_id_type=MESH,
        ).wait_send()


def serve(queries, own, doc_lengths, w_out, landed_o):
    rows = queries.shape[2]
    width = own.shape[4]
    heads = queries.shape[3] // width
    tall = heads * 2 * rows
    vmem = pl.BlockSpec(memory_space=pltpu.VMEM)
    hbm = pl.BlockSpec(memory_space=pl.ANY)
    return pl.pallas_call(
        serve_kernel,
        out_shape=(
            jax.ShapeDtypeStruct(queries.shape, jnp.bfloat16),
            jax.ShapeDtypeStruct(w_out.shape, jnp.bfloat16),
        ),
        in_specs=[vmem] * 2 + [pl.BlockSpec(memory_space=pltpu.SMEM)] + [hbm] * 2,
        out_specs=(vmem, hbm),
        scratch_shapes=[
            pltpu.VMEM((SIDE, tall, 2 * rows), jnp.int32),
            pltpu.VMEM((SIDE, tall, 2 * rows), jnp.int32),
            pltpu.VMEM((6, 2, *own.shape), jnp.bfloat16),
            pltpu.VMEM((SIDE, tall, 2 * rows), jnp.float32),
            pltpu.VMEM((SIDE, tall, 2 * rows), jnp.float32),
            pltpu.VMEM((SIDE, tall, width), jnp.float32),
            pltpu.SemaphoreType.DMA((11,)),
            pltpu.SemaphoreType.DMA((6, 2)),
            pltpu.SemaphoreType.DMA((12,)),
            pltpu.SemaphoreType.DMA((12,)),
            pltpu.SemaphoreType.DMA((1,)),
        ],
        compiler_params=pltpu.CompilerParams(
            collective_id=2, has_side_effects=True, vmem_limit_bytes=60 << 20
        ),
        name="serve",
    )(queries, own, doc_lengths, w_out, landed_o)


def body(tokens, doc_lengths, attn_gain, mlp_gain, w_query, w_keyval, w_out, w_gate, w_up, w_down):
    gates = w_gate.T
    queries, own, landed_o, landed_g = project(
        tokens, attn_gain[None, :], doc_lengths, w_query, w_keyval, w_out, gates
    )
    attn, w_out_other = serve(queries, own, doc_lengths, w_out, landed_o)
    return finish(tokens, attn, mlp_gain[None, :], w_out, w_out_other, gates, w_up.T, w_down, landed_g)


def solution(mesh):
    return jax.shard_map(
        body,
        mesh=mesh,
        in_specs=(
            P(("token", "tensor"), None),
            P(),
            P(),
            P(),
            P(None, "tensor"),
            P(None, "tensor"),
            P("tensor", None),
            P(None, "tensor"),
            P(None, "tensor"),
            P("tensor", None),
        ),
        out_specs=P(("token", "tensor"), None),
        check_vma=False,
    )
```

```python
import functools
import math

import jax
import jax.numpy as jnp
from jax import lax
from jax.experimental import pallas as pl
from jax.experimental.pallas import tpu as pltpu
from jax.sharding import PartitionSpec as P

HEAD_DIM = 128
SIDE = 4
CORES = 2
YS = 4

EPSILON = 1e-05
ROPE_BASE = 500000.0
NEGATIVE = -1e30
MESH = pl.DeviceIdType.MESH


def place():
    me, token = lax.axis_index("tensor"), lax.axis_index("token")
    return me // SIDE, me % SIDE, token // CORES, token % CORES


def along_z(step):
    z, x, _, _ = place()
    return {"tensor": ((z + step + SIDE) % SIDE) * SIDE + x}


def mate():
    z, x, _, _ = place()
    return {"tensor": z * SIDE + SIDE - 1 - x}


def holder():
    z, x, _, _ = place()
    return {"tensor": z * SIDE + x + 1 - 2 * (x % 2)}


def along_y(step):
    _, _, y, core = place()
    return {"token": ((y + step + YS) % YS) * CORES + core}


def twin():
    _, _, y, core = place()
    return {"token": y * CORES + 1 - core}


def greet():
    others = [along_z(1), along_z(-1), mate(), holder(), along_y(1), along_y(-1), twin()]
    for other in others:
        pl.semaphore_signal(pltpu.get_barrier_semaphore(), inc=1, device_id=other, device_id_type=MESH)
    return len(others)


def meet(others):
    pl.semaphore_wait(pltpu.get_barrier_semaphore(), others)


def row_class(x):
    return lax.rem(lax.div(x + 1, 2), 2)


def document_start(doc_ref, spots):
    first, end = jnp.zeros_like(spots), 0
    for document in range(doc_ref.shape[0] - 1):
        end = end + doc_ref[document]
        first = jnp.where(spots >= end, end, first)
    return first


def column_halves(width):
    first = width * 9 // 16
    return first, width - first


class Wires:
    def __init__(self, send_sems, recv_sems):
        self.send_sems, self.recv_sems, self.slots, self.started = send_sems, recv_sems, {}, []

    def copy(self, key, src, dst, device):
        slot = self.slots.setdefault(key, len(self.slots))
        return pltpu.make_async_remote_copy(
            src_ref=src,
            dst_ref=dst,
            send_sem=self.send_sems.at[slot],
            recv_sem=self.recv_sems.at[slot],
            device_id=device,
            device_id_type=MESH,
        )

    def start(self, key, src, dst, device):
        made = self.copy(key, src, dst, device)
        made.start()
        self.started.append(made)

    def arrive(self, key, dst, device):
        self.copy(key, dst, dst, device).wait_recv()

    def drain(self):
        for made in self.started:
            made.wait_send()
        self.started = []


class Fetch:
    def __init__(self, wires, name, src, dst, lanes, first_lane=0, landed=None, landed_sem=None):
        self.wires, self.name, self.src, self.dst, self.lanes, self.first_lane = wires, name, src, dst, lanes, first_lane
        self.landed, self.kept = landed, None
        if landed is not None:
            self.kept = pltpu.make_async_copy(landed, self.dst_slot(dst), landed_sem)

    @property
    def size(self):
        return self.src.shape[1 if self.lanes else 0] // (YS * CORES)

    def dst_slot(self, ref):
        _, _, y, core = place()
        return self.cut(ref, y * CORES + core, None, self.first_lane)

    def cut(self, ref, number, part, offset):
        size = self.size if part is None else self.size // 2
        start = pl.multiple_of(number * self.size, self.size) + (0 if part in (None, 0) else size)
        start = pl.multiple_of(start, size)
        if self.lanes:
            return ref.at[:, pl.ds(start, size)]
        return ref.at[pl.ds(start, size), pl.ds(offset, self.src.shape[1])]

    def slot(self, dy, dc, part=None):
        _, _, y, core = place()
        number = ((y + dy + YS) % YS) * CORES + (core if dc == 0 else 1 - core)
        return self.cut(self.dst, number, part, self.first_lane)

    def start(self, key, ref, device):
        self.wires.start((self.name, key), ref, ref, device)

    def arrive(self, key, ref):
        self.wires.arrive((self.name, key), ref, holder())

    def ask(self):
        _, _, y, core = place()
        self.wires.start((self.name, "x"), self.cut(self.src, y * CORES + core, None, 0), self.slot(0, 0), holder())

    def land(self, landed):
        self.wires.start((self.name, "x"), self.dst_slot(self.src), landed, holder())

    def relay(self):
        source = self.landed
        if source is None:
            source = self.slot(0, 0)
            self.arrive("x", source)
        else:
            self.kept.start()
        for key, device in (("y3", along_y(1)), ("y1", along_y(-1)), ("c0", twin())):
            self.wires.start((self.name, key), source, self.slot(0, 0), device)

    def pass_on(self):
        self.arrive("y3", self.slot(3, 0))
        self.start("h0", self.slot(3, 0, 0), along_y(1))
        self.start("c3", self.slot(3, 0), twin())
        self.arrive("y1", self.slot(1, 0))
        self.start("h1", self.slot(1, 0, 1), along_y(-1))
        self.start("c1", self.slot(1, 0), twin())

    def settle(self):
        self.arrive("h0", self.slot(2, 0, 0))
        self.arrive("h1", self.slot(2, 0, 1))
        self.start("c2", self.slot(2, 0), twin())

    def finish(self):
        for dy in (0, 3, 1, 2):
            self.arrive("c%d" % dy, self.slot(dy, 1))
        if self.kept is not None:
            self.kept.wait()


def gather(wires, blocks, hook):
    rows = blocks[0].shape[2]
    low, high = pl.ds(0, rows // 2), pl.ds(rows // 2, rows // 2)
    up, down = 1, -1

    def full(h, dz, m):
        return blocks[h].at[dz, m]

    def spread(h, m):
        wires.start(("s", h, 3, m), full(h, 0, m), full(h, 3, m), along_z(up))
        wires.start(("s", h, 1, m), full(h, 0, m), full(h, 1, m), along_z(down))

    def to_mate(h, dz):
        wires.start(("m", h, dz), full(h, dz, 0), full(h, dz, 1), mate())

    def relay(h, m, onward):
        wires.arrive(("s", h, 3, m), full(h, 3, m), along_z(down))
        wires.start(("t", h, 0, m), blocks[h].at[3, m, low], blocks[h].at[2, m, low], along_z(up))
        if onward:
            to_mate(h, 3)
        wires.arrive(("s", h, 1, m), full(h, 1, m), along_z(up))
        wires.start(("t", h, 1, m), blocks[h].at[1, m, high], blocks[h].at[2, m, high], along_z(down))
        if onward:
            to_mate(h, 1)

    def last(h, m):
        wires.arrive(("t", h, 0, m), blocks[h].at[2, m, low], along_z(down))
        wires.arrive(("t", h, 1, m), blocks[h].at[2, m, high], along_z(up))

    to_mate(0, 0)
    spread(1, 0)
    spread(0, 0)
    to_mate(1, 0)
    hook("sent")
    wires.arrive(("m", 0, 0), full(0, 0, 1), mate())
    spread(0, 1)
    relay(1, 0, True)
    hook("one")
    relay(0, 0, False)
    wires.arrive(("m", 1, 0), full(1, 0, 1), mate())
    hook("own pair")
    last(1, 0)
    to_mate(1, 2)
    hook("two")
    relay(0, 1, False)
    hook("three")
    wires.arrive(("m", 1, 3), full(1, 3, 1), mate())
    wires.arrive(("m", 1, 1), full(1, 1, 1), mate())
    hook("sides")
    last(0, 0)
    last(0, 1)
    wires.arrive(("m", 1, 2), full(1, 2, 1), mate())
    hook("far")


def scatter(wires, out, bufs, produce, hook):
    z_half, z_full, mate0, mate1, e_half, e_full = bufs
    rows = out[0].shape[2]
    low, high = pl.ds(0, rows // 2), pl.ds(rows // 2, rows // 2)
    ways = ((0, 1, low, 1), (1, 3, high, -1))
    f32 = jnp.float32

    def wide(ref):
        return ref[...].astype(f32)

    def add_to(ref, *others):
        total = wide(ref)
        for other in others:
            total = total + wide(other)
        ref[...] = total.astype(ref.dtype)

    def mate_send(dz):
        wires.start(("m1", dz), out[1].at[dz, 1], mate1.at[dz], mate())

    def mate_join(dz):
        wires.arrive(("m1", dz), mate1.at[dz], mate())
        add_to(out[1].at[dz, 0], mate1.at[dz])

    produce(1, (2,))
    mate_send(2)
    produce(0, (2,))
    for m in (1, 0):
        for way, dz, part, step in ways:
            wires.start(("a", way, m), out[0].at[2, m, part], z_half.at[way, m], along_z(step))
    hook("begun")
    produce(0, (1, 3))
    produce(1, (1, 3))
    mate_send(1)
    mate_send(3)
    mate_join(2)
    for way, dz, part, step in ways:
        wires.start(("e", way), out[1].at[2, 0, part], e_half.at[way], along_z(step))
    for m in (1, 0):
        for way, dz, part, step in ways:
            wires.arrive(("a", way, m), z_half.at[way, m], along_z(-step))
            add_to(out[0].at[dz, m, part], z_half.at[way, m])
            wires.start(("b", way, m), out[0].at[dz, m], z_full.at[way, m], along_z(step))
    produce(1, (0,))
    mate_send(0)
    produce(0, (0,))
    hook("early")
    for way, dz, part, step in ways:
        mate_join(dz)
        wires.arrive(("e", way), e_half.at[way], along_z(-step))
        add_to(out[1].at[dz, 0, part], e_half.at[way])
        wires.start(("f", way), out[1].at[dz, 0], e_full.at[way], along_z(step))
    hook("middle")
    for way, dz, part, step in ways:
        wires.arrive(("b", way, 1), z_full.at[way, 1], along_z(-step))
    add_to(out[0].at[0, 1], z_full.at[0, 1], z_full.at[1, 1])
    wires.start(("m0",), out[0].at[0, 1], mate0, mate())
    hook("late")
    for way, dz, part, step in ways:
        wires.arrive(("b", way, 0), z_full.at[way, 0], along_z(-step))
    first = wide(out[0].at[0, 0]) + wide(z_full.at[0, 0]) + wide(z_full.at[1, 0])
    wires.arrive(("m1", 0), mate1.at[0], mate())
    second = wide(out[1].at[0, 0]) + wide(mate1.at[0])
    for way, dz, part, step in ways:
        wires.arrive(("f", way), e_full.at[way], along_z(-step))
        second = second + wide(e_full.at[way])
    wires.arrive(("m0",), mate0, mate())
    first = first + wide(mate0)
    return first, second


def norm_halves(rows, gain):
    mean_square = jnp.mean(rows * rows, axis=-1, keepdims=True)
    normed = (rows * lax.rsqrt(mean_square + EPSILON) * gain).astype(jnp.bfloat16)
    width, _ = column_halves(rows.shape[1])
    return normed[:, :width], normed[:, width:]


def stacked(blocks, h, dzs):
    _, _, rows, width = blocks[h].shape
    parts = [blocks[h][dz].reshape(2 * rows, width) for dz in dzs]
    return parts[0] if len(parts) == 1 else jnp.concatenate(parts, axis=0)


def project_kernel(
    tokens_hbm, gain_ref, doc_ref, wq_hbm, wkv_hbm, wo_hbm, wg_hbm, q_ref, kv_ref, landed_o, landed_g,
    tokens_ref, cos_ref, sin_ref, weights, others, blocks0, blocks1, load_sems, send_sems, recv_sems,
):
    blocks, rows = (blocks0, blocks1), blocks0.shape[2]
    split, width = blocks0.shape[3], weights.shape[0]
    arriving = pltpu.make_async_copy(tokens_hbm, tokens_ref, load_sems.at[2])
    arriving.start()
    neighbours = greet()
    qcols = wq_hbm.shape[1]
    cols = qcols + wkv_hbm.shape[1]
    z, x, y, core = place()
    mine, token = row_class(x), y * CORES + core
    loads = [
        pltpu.make_async_copy(wq_hbm, weights.at[:, pl.ds(0, qcols)], load_sems.at[0]),
        pltpu.make_async_copy(wkv_hbm, weights.at[:, pl.ds(qcols, cols - qcols)], load_sems.at[1]),
    ]
    for load in loads:
        load.start()
    arriving.wait()
    blocks0[0, 0], blocks1[0, 0] = norm_halves(tokens_ref[...].astype(jnp.float32), gain_ref[...])
    meet(neighbours)
    wires = Wires(send_sems, recv_sems)

    def angles(number, carry):
        run, m = lax.div(number, 2), lax.rem(number, 2)
        at_x = mine + m * (SIDE - 1 - 2 * mine)
        shape = (rows, HEAD_DIM)
        spots = lax.broadcasted_iota(jnp.int32, shape, 0) + ((token * SIDE + run) * SIDE + at_x) * rows
        position = (spots - document_start(doc_ref, spots)).astype(jnp.float32)
        lane = lax.broadcasted_iota(jnp.int32, shape, 1)
        upper = lane >= HEAD_DIM // 2
        pair = jnp.where(upper, lane - HEAD_DIM // 2, lane).astype(jnp.float32)
        angle = position * jnp.exp(-math.log(ROPE_BASE) * pair * (2.0 / HEAD_DIM))
        sine = jnp.sin(angle)
        cos_ref[number] = jnp.cos(angle)
        sin_ref[number] = jnp.where(upper, sine, -sine)
        return carry
    fetch_q = Fetch(wires, "q", wq_hbm, others, False, 0)
    fetch_kv = Fetch(wires, "kv", wkv_hbm, others, False, qcols)
    fetch_o = Fetch(wires, "o", wo_hbm, None, True)
    fetch_g = Fetch(wires, "g", wg_hbm, None, True)

    def emit(dzs, mine):
        shard = weights if mine else others
        part = sum(
            jnp.dot(
                stacked(blocks, h, dzs),
                shard[slice(0, split) if h == 0 else slice(split, width), :],
                preferred_element_type=jnp.float32,
            )
            for h in range(2)
        )
        is_key = (x % 2 == 0) if mine else (x % 2 == 1)
        which = x % 2 if mine else 1 - x % 2
        first_col = 0 if mine else qcols
        for i, dz in enumerate(dzs):
            for m in range(2):
                whole = part[(2 * i + m) * rows : (2 * i + m + 1) * rows]
                zz = (z + dz) % SIDE
                mm = x // 2 if m == 0 else 1 - x // 2
                cosine, sine = cos_ref[2 * zz + mm], sin_ref[2 * zz + mm]
                for head in range(qcols // HEAD_DIM):
                    piece = whole[:, head * HEAD_DIM : (head + 1) * HEAD_DIM]
                    turned = piece * cosine + pltpu.roll(piece, HEAD_DIM // 2, 1) * sine
                    at = first_col + head * HEAD_DIM
                    q_ref[zz, mm, :, at : at + HEAD_DIM] = turned.astype(jnp.bfloat16)
                piece = whole[:, qcols:]
                turned = piece * cosine + pltpu.roll(piece, HEAD_DIM // 2, 1) * sine
                kv_ref[which, zz, mm] = jnp.where(is_key, turned, piece).astype(jnp.bfloat16)

    def hook(name):
        if name == "sent":
            fetch_q.ask()
            fetch_kv.ask()
            fetch_o.land(landed_o)
            fetch_g.land(landed_g)
            lax.fori_loop(0, 2 * SIDE, angles, 0)
        elif name == "one":
            fetch_q.relay()
            fetch_kv.relay()
            for load in loads:
                load.wait()
        elif name == "own pair":
            emit((0,), True)
        elif name == "two":
            fetch_q.pass_on()
        elif name == "three":
            fetch_kv.pass_on()
            fetch_q.settle()
        elif name == "sides":
            emit((3, 1), True)
            fetch_kv.settle()
            fetch_q.finish()
            fetch_kv.finish()
            emit((0,), False)
            emit((3, 1), False)
        else:
            emit((2,), True)
            emit((2,), False)

    gather(wires, blocks, hook)
    wires.arrive(("o", "x"), landed_o, holder())
    wires.arrive(("g", "x"), landed_g, holder())
    wires.drain()


def project(tokens, gain, doc_lengths, w_query, w_keyval, w_out, w_gate):
    rows, width = tokens.shape
    cols = w_query.shape[1] + w_keyval.shape[1]
    vmem = pl.BlockSpec(memory_space=pltpu.VMEM)
    hbm = pl.BlockSpec(memory_space=pl.ANY)
    bf16 = jnp.bfloat16
    return pl.pallas_call(
        project_kernel,
        out_shape=(
            jax.ShapeDtypeStruct((SIDE, 2, rows, 2 * w_query.shape[1]), bf16),
            jax.ShapeDtypeStruct((2, SIDE, 2, rows, w_keyval.shape[1]), bf16),
            jax.ShapeDtypeStruct((w_out.shape[0], w_out.shape[1] // (YS * CORES)), bf16),
            jax.ShapeDtypeStruct((w_gate.shape[0], w_gate.shape[1] // (YS * CORES)), bf16),
        ),
        in_specs=[hbm, vmem, pl.BlockSpec(memory_space=pltpu.SMEM)] + [hbm] * 4,
        out_specs=(vmem, vmem, hbm, hbm),
        scratch_shapes=[
            pltpu.VMEM((rows, width), bf16),
            pltpu.VMEM((2 * SIDE, rows, HEAD_DIM), jnp.float32),
            pltpu.VMEM((2 * SIDE, rows, HEAD_DIM), jnp.float32),
            pltpu.VMEM((width, cols), bf16),
            pltpu.VMEM((width, cols), bf16),
            *[pltpu.VMEM((SIDE, 2, rows, part), bf16) for part in column_halves(width)],
            pltpu.SemaphoreType.DMA((3,)),
            pltpu.SemaphoreType.DMA((64,)),
            pltpu.SemaphoreType.DMA((64,)),
        ],
        compiler_params=pltpu.CompilerParams(
            collective_id=0, has_side_effects=True, vmem_limit_bytes=60 << 20
        ),
        name="project",
    )(tokens, gain, doc_lengths, w_query, w_keyval, w_out, w_gate)


def finish_kernel(
    tokens_hbm, attn_hbm, gain_ref, wo_hbm, wo2_hbm, wg_hbm, wu_hbm, wd_hbm, landed_g, out_ref,
    tokens_ref, attn_ref, wo, wg, wu, wd, wg2, wu2, wd2, blocks0, blocks1, hidden, hidden2, sending0, sending1,
    z_half, z_full, mate0, mate1, e_half, e_full, state, load_sems, send_sems, recv_sems,
):
    blocks, sending = (blocks0, blocks1), (sending0, sending1)
    _, _, rows, split = blocks0.shape
    width = wo.shape[1]
    neighbours = greet()
    own = wo_hbm.shape[0]
    z, x, _, _ = place()
    loads = [
        pltpu.make_async_copy(src, dst, load_sems.at[i])
        for i, (src, dst) in enumerate(
            ((wo_hbm, wo.at[pl.ds(0, own)]), (wo2_hbm, wo.at[pl.ds(own, own)]), (wg_hbm, wg), (wu_hbm, wu), (wd_hbm, wd))
        )
    ]
    arriving = [
        pltpu.make_async_copy(attn_hbm, attn_ref, load_sems.at[6]),
        pltpu.make_async_copy(tokens_hbm, tokens_ref, load_sems.at[7]),
    ]
    for load in arriving[:1] + loads[:2] + arriving[1:]:
        load.start()
    meet(neighbours)
    arriving[0].wait()
    bufs = (z_half, z_full, mate0, mate1, e_half, e_full)
    weight_wires = Wires(send_sems.at[3], recv_sems.at[3])
    fetch_g = Fetch(weight_wires, "g", wg_hbm, wg2, True, 0, landed_g, load_sems.at[5])
    fetch_u = Fetch(weight_wires, "u", wu_hbm, wu2, True)
    fetch_d = Fetch(weight_wires, "d", wd_hbm, wd2, True)
    loads[0].wait()
    loads[1].wait()

    def columns(h):
        return pl.ds(0, split) if h == 0 else pl.ds(split, width - split)

    def keep(h, dzs, part):
        for i, dz in enumerate(dzs):
            piece = part[2 * i * rows : 2 * (i + 1) * rows].astype(jnp.bfloat16)
            sending[h][dz] = piece.reshape(2, rows, piece.shape[1])

    def project_out(h, dzs):
        mine, other = x // 2, 1 - x // 2
        left = [attn_ref[(z + dz) % SIDE, m] for dz in dzs for m in (mine, other)]
        left = jnp.concatenate(left, axis=0)
        keep(h, dzs, jnp.dot(left, wo[:, columns(h)], preferred_element_type=jnp.float32))

    def hook_out(name):
        if name == "begun":
            for load in loads[2:]:
                load.start()
            fetch_g.relay()
            fetch_u.ask()
            fetch_d.ask()
        elif name == "early":
            fetch_g.pass_on()
            fetch_u.relay()
        elif name == "late":
            fetch_g.settle()
            fetch_d.relay()

    out_wires = Wires(send_sems.at[0], recv_sems.at[0])
    first, second = scatter(out_wires, sending, bufs, project_out, hook_out)
    arriving[1].wait()
    for h, proj in enumerate((first, second)):
        state[:, columns(h)] = (tokens_ref[:, columns(h)].astype(jnp.float32) + proj).astype(jnp.bfloat16)
    blocks0[0, 0], blocks1[0, 0] = norm_halves(state[...].astype(jnp.float32), gain_ref[...])

    def gated(dzs, mine):
        gates, ups, result = (wg, wu, hidden) if mine else (wg2, wu2, hidden2)
        gate = upward = 0.0
        for h in range(2):
            left = stacked(blocks, h, dzs)
            across = (((1,), (1,)), ((), ()))
            gate = gate + lax.dot_general(left, gates[:, columns(h)], across, preferred_element_type=jnp.float32)
            upward = upward + lax.dot_general(left, ups[:, columns(h)], across, preferred_element_type=jnp.float32)
        value = (gate / (1.0 + jnp.exp(-gate)) * upward).astype(jnp.bfloat16)
        for i, dz in enumerate(dzs):
            result[dz] = value[2 * i * rows : 2 * (i + 1) * rows].reshape(2, rows, value.shape[1])

    def hook_gated(name):
        if name == "sent":
            loads[2].wait()
            loads[3].wait()
            fetch_u.pass_on()
        elif name == "one":
            fetch_g.finish()
            fetch_d.pass_on()
        elif name == "own pair":
            gated((0,), True)
            fetch_u.settle()
        elif name == "three":
            fetch_d.settle()
        elif name == "sides":
            gated((3, 1), True)
            fetch_u.finish()
            gated((0,), False)
            gated((3, 1), False)
        elif name == "far":
            gated((2,), True)
            gated((2,), False)
            fetch_d.finish()
            loads[4].wait()

    gather_wires = Wires(send_sems.at[1], recv_sems.at[1])
    gather(gather_wires, blocks, hook_gated)
    out_wires.drain()

    def project_down(h, dzs):
        part = 0.0
        for values, weights in ((hidden, wd), (hidden2, wd2)):
            left = [values[dz].reshape(2 * rows, values.shape[3]) for dz in dzs]
            left = left[0] if len(left) == 1 else jnp.concatenate(left, axis=0)
            part = part + jnp.dot(left, weights[:, columns(h)], preferred_element_type=jnp.float32)
        keep(h, dzs, part)

    down_wires = Wires(send_sems.at[2], recv_sems.at[2])
    down = scatter(down_wires, sending, bufs, project_down, lambda name: None)
    for h in range(2):
        out_ref[:, columns(h)] = (state[:, columns(h)].astype(jnp.float32) + down[h]).astype(jnp.bfloat16)
    for wires in (gather_wires, down_wires, weight_wires):
        wires.drain()


def finish(tokens, attn, gain, w_out, w_out_other, w_gate, w_up, w_down, landed_g):
    rows, width = tokens.shape
    hidden = w_gate.shape[0]
    vmem = pl.BlockSpec(memory_space=pltpu.VMEM)
    hbm = pl.BlockSpec(memory_space=pl.ANY)
    wide, narrow = column_halves(width)
    bf16 = jnp.bfloat16
    return pl.pallas_call(
        finish_kernel,
        out_shape=jax.ShapeDtypeStruct((rows, width), bf16),
        in_specs=[hbm] * 2 + [vmem] + [hbm] * 6,
        out_specs=vmem,
        scratch_shapes=[
            pltpu.VMEM((rows, width), bf16),
            pltpu.VMEM(attn.shape, bf16),
            pltpu.VMEM((2 * w_out.shape[0], width), bf16),
            *[pltpu.VMEM((hidden, width), bf16)] * 6,
            pltpu.VMEM((SIDE, 2, rows, wide), bf16),
            pltpu.VMEM((SIDE, 2, rows, narrow), bf16),
            pltpu.VMEM((SIDE, 2, rows, hidden), bf16),
            pltpu.VMEM((SIDE, 2, rows, hidden), bf16),
            pltpu.VMEM((SIDE, 2, rows, wide), bf16),
            pltpu.VMEM((SIDE, 2, rows, narrow), bf16),
            pltpu.VMEM((2, 2, rows // 2, wide), bf16),
            pltpu.VMEM((2, 2, rows, wide), bf16),
            pltpu.VMEM((rows, wide), bf16),
            pltpu.VMEM((SIDE, rows, narrow), bf16),
            pltpu.VMEM((2, rows // 2, narrow), bf16),
            pltpu.VMEM((2, rows, narrow), bf16),
            pltpu.VMEM((rows, width), bf16),
            pltpu.SemaphoreType.DMA((8,)),
            pltpu.SemaphoreType.DMA((4, 48)),
            pltpu.SemaphoreType.DMA((4, 48)),
        ],
        compiler_params=pltpu.CompilerParams(
            collective_id=1, has_side_effects=True, vmem_limit_bytes=60 << 20
        ),
        name="finish",
    )(tokens, attn, gain, w_out, w_out_other, w_gate, w_up, w_down, landed_g)


def serve_kernel(
    q_hbm, own_hbm, doc_ref, wo_hbm, landed_o, o_ref, wo_other,
    q_ref, first_ref, spot_ref, held, peak, total, summed, send_sems, recv_sems, weight_send, weight_recv, landed_sem,
):
    z, x, y, core = place()
    mine = row_class(x)
    theirs = 1 - mine
    base = 1 - core
    rows = q_ref.shape[2]
    width = own_hbm.shape[4]
    heads = q_ref.shape[3] // width
    factor = math.log2(math.e) / math.sqrt(width)
    across, ahead, other_core = holder(), along_y(1), twin()
    neighbours = greet()
    loads = [
        pltpu.make_async_copy(own_hbm, held.at[base, mine], landed_sem.at[1]),
        pltpu.make_async_copy(q_hbm, q_ref, landed_sem.at[2]),
    ]
    for load in loads:
        load.start()
    meet(neighbours)
    loads[0].wait()
    started = []
    weight_wires = Wires(weight_send, weight_recv)
    fetch_o = Fetch(weight_wires, "o", wo_hbm, wo_other, True, 0, landed_o, landed_sem.at[0])

    def send(g, c, target, device):
        made = pltpu.make_async_remote_copy(
            src_ref=held.at[g, c],
            dst_ref=held.at[target, c],
            send_sem=send_sems.at[len(started)],
            recv_sem=recv_sems.at[target, c],
            device_id=device,
            device_id_type=MESH,
        )
        made.start()
        started.append(True)

    def arrive(g, c):
        pltpu.make_async_remote_copy(
            src_ref=held.at[g, c],
            dst_ref=held.at[g, c],
            send_sem=send_sems.at[0],
            recv_sem=recv_sems.at[g, c],
            device_id=across,
            device_id_type=MESH,
        ).wait_recv()

    send(base, mine, base, across)
    send(base, mine, base + 2, ahead)
    send(base, mine, base, other_core)
    peak[...] = jnp.full(peak.shape, NEGATIVE, jnp.float32)
    total[...] = jnp.zeros(total.shape, jnp.float32)
    summed[...] = jnp.zeros(summed.shape, jnp.float32)

    in_run = lax.broadcasted_iota(jnp.int32, (1, 2 * rows), 1)
    later = (in_run >= rows).astype(jnp.int32)

    def places(zz, carry):
        row = lax.broadcasted_iota(jnp.int32, first_ref.shape[1:], 0) & (2 * rows - 1)
        other = (row >= rows).astype(jnp.int32)
        spots = row + (mine - other + other * (SIDE - 1 - 2 * mine)) * rows
        spots = spots + ((2 * y + core) * SIDE + zz) * SIDE * rows
        spot_ref[zz] = spots
        first_ref[zz] = document_start(doc_ref, spots)
        return carry

    lax.fori_loop(0, SIDE, places, 0)
    loads[1].wait()

    def step(tiles, g, c, back, causal):
        run = 2 * rows
        shift = (back - 2 * y - core) * (SIDE * SIDE * rows)
        held_before = [(peak[zz], total[zz], summed[zz]) for zz, _, _ in tiles]
        scored = []
        for zz, begin, size in tiles:
            tile = [q_ref[zz, :, :, h * width : (h + 1) * width].reshape(run, width) for h in range(heads)]
            query = jnp.concatenate(tile, axis=0)
            keys = held[g, c, 0, begin : begin + size].reshape(size * run, width)
            scored.append(
                lax.dot_general(query, keys, (((1,), (1,)), ((), ())), preferred_element_type=jnp.float32)
            )
        after = []
        for (zz, begin, size), scores, (old, sums, outs) in zip(tiles, scored, held_before):
            low, high = first_ref[zz] + shift, spot_ref[zz] + shift
            parts = []
            for run_at in range(size):
                spots = in_run + c * (rows - 2 * rows * later) + later * (SIDE - 2) * rows
                spots = spots + (begin + run_at) * (SIDE * rows)
                seen = spots >= low
                if causal:
                    seen = seen & (spots <= high)
                parts.append(jnp.where(seen, scores[:, run_at * run : (run_at + 1) * run], NEGATIVE))
            top = functools.reduce(jnp.maximum, parts)
            new = jnp.maximum(old, jnp.broadcast_to(jnp.max(top, axis=1, keepdims=True) * factor, old.shape))
            decay = jnp.exp2(old - new)
            parts = [jnp.exp2(part * factor - new) for part in parts]
            weights = jnp.concatenate([part.astype(jnp.bfloat16) for part in parts], axis=1)
            values = held[g, c, 1, begin : begin + size].reshape(size * run, width)
            outs = outs * decay + jnp.dot(weights, values, preferred_element_type=jnp.float32)
            after.append((new, sums * decay + functools.reduce(jnp.add, parts), outs))
        for (zz, _, _), state in zip(tiles, after):
            peak[zz], total[zz], summed[zz] = state

    def own_block(c):
        for pair in ((0, 3), (1, 2)):
            step([(zz, 0, zz + 1) for zz in pair], base, c, 0, True)

    def far_block(c):
        for pair in ((0, 3), (1, 2)):
            step([(zz, zz, SIDE - zz) for zz in pair], base + 4, c, 4, False)

    def per_class(work):
        def one(i, carry):
            work(mine + i * (theirs - mine))
            return carry

        return one

    def first_class(i, carry):
        @pl.when(i == 1)
        def _():
            arrive(base, theirs)
            send(base, theirs, base, other_core)
            arrive(base + 2, mine)
            send(base + 2, mine, base + 4, ahead)
            send(base + 2, mine, base + 2, across)
            send(base + 2, mine, base + 2, other_core)

        own_block(mine + i * (theirs - mine))
        return carry

    lax.fori_loop(0, 2, first_class, 0)
    fetch_o.relay()

    def middle(stage, carry):
        final = lax.div(stage, 4)
        back = (1 - final) * (1 + lax.rem(stage, 2)) + 3 * final
        c = mine + ((1 - final) * lax.div(stage, 2) + final * (stage - 4)) * (theirs - mine)

        @pl.when(stage == 2)
        def _():
            arrive(base + 2, theirs)
            send(base + 2, theirs, base + 2, other_core)
            arrive(base + 4, mine)
            send(base + 4, mine, base + 4, across)
            send(base + 4, mine, base + 4, other_core)

        @pl.when(stage == 4)
        def _():
            arrive(base + 4, theirs)
            send(base + 4, theirs, base + 4, other_core)

        @pl.when(back != 2)
        def _():
            arrive(base + back, c)

        def over_runs(pair, inner):
            step([(2 * pair + i, 0, SIDE) for i in range(2)], base + back, c, back, False)
            return inner

        return lax.fori_loop(0, SIDE // 2, over_runs, carry)

    lax.fori_loop(0, 4, middle, 0)
    fetch_o.pass_on()
    lax.fori_loop(4, 6, middle, 0)
    fetch_o.settle()
    lax.fori_loop(0, 2, per_class(far_block), 0)
    spare = core * 5
    arrive(spare, 0)
    arrive(spare, 1)
    fetch_o.finish()
    weight_wires.drain()
    for zz in range(SIDE):
        answer = (summed[zz] / jnp.sum(total[zz], axis=1, keepdims=True)).astype(jnp.bfloat16)
        for h in range(heads):
            piece = answer[h * 2 * rows : (h + 1) * 2 * rows]
            o_ref[zz, :, :, h * width : (h + 1) * width] = piece.reshape(2, rows, width)
    for number in range(len(started)):
        pltpu.make_async_remote_copy(
            src_ref=held.at[0, 0],
            dst_ref=held.at[0, 0],
            send_sem=send_sems.at[number],
            recv_sem=recv_sems.at[0, 0],
            device_id=across,
            device_id_type=MESH,
        ).wait_send()


def serve(queries, own, doc_lengths, w_out, landed_o):
    rows = queries.shape[2]
    width = own.shape[4]
    heads = queries.shape[3] // width
    tall = heads * 2 * rows
    vmem = pl.BlockSpec(memory_space=pltpu.VMEM)
    hbm = pl.BlockSpec(memory_space=pl.ANY)
    return pl.pallas_call(
        serve_kernel,
        out_shape=(
            jax.ShapeDtypeStruct(queries.shape, jnp.bfloat16),
            jax.ShapeDtypeStruct(w_out.shape, jnp.bfloat16),
        ),
        in_specs=[hbm] * 2 + [pl.BlockSpec(memory_space=pltpu.SMEM)] + [hbm] * 2,
        out_specs=(vmem, hbm),
        scratch_shapes=[
            pltpu.VMEM(queries.shape, jnp.bfloat16),
            pltpu.VMEM((SIDE, tall, 2 * rows), jnp.int32),
            pltpu.VMEM((SIDE, tall, 2 * rows), jnp.int32),
            pltpu.VMEM((6, 2, *own.shape), jnp.bfloat16),
            pltpu.VMEM((SIDE, tall, 2 * rows), jnp.float32),
            pltpu.VMEM((SIDE, tall, 2 * rows), jnp.float32),
            pltpu.VMEM((SIDE, tall, width), jnp.float32),
            pltpu.SemaphoreType.DMA((11,)),
            pltpu.SemaphoreType.DMA((6, 2)),
            pltpu.SemaphoreType.DMA((12,)),
            pltpu.SemaphoreType.DMA((12,)),
            pltpu.SemaphoreType.DMA((3,)),
        ],
        compiler_params=pltpu.CompilerParams(
            collective_id=2, has_side_effects=True, vmem_limit_bytes=60 << 20
        ),
        name="serve",
    )(queries, own, doc_lengths, w_out, landed_o)


def body(tokens, doc_lengths, attn_gain, mlp_gain, w_query, w_keyval, w_out, w_gate, w_up, w_down):
    gates = w_gate.T
    queries, own, landed_o, landed_g = project(
        tokens, attn_gain[None, :], doc_lengths, w_query, w_keyval, w_out, gates
    )
    attn, w_out_other = serve(queries, own, doc_lengths, w_out, landed_o)
    return finish(tokens, attn, mlp_gain[None, :], w_out, w_out_other, gates, w_up.T, w_down, landed_g)


def solution(mesh):
    return jax.shard_map(
        body,
        mesh=mesh,
        in_specs=(
            P(("token", "tensor"), None),
            P(),
            P(),
            P(),
            P(None, "tensor"),
            P(None, "tensor"),
            P("tensor", None),
            P(None, "tensor"),
            P(None, "tensor"),
            P("tensor", None),
        ),
        out_specs=P(("token", "tensor"), None),
        check_vma=False,
    )
```
